32 devices in a mesh: dp: 8 (over y, x, core), tensor: 4 (over z).
Axes of the slice: x: 2, y: 2, z: 4, core: 2. Of those that a mesh axis runs over, the one named last changes fastest.
Arguments:
- text_in: bfloat16 [32, 1004, 768], P(('dp', 'tensor')), may hold values from -6 to 6
- start_memory: bfloat16 [10, 768], replicated, may hold values from -6 to 6
- w_qkv: bfloat16 [3, 768, 768], P(None, None, 'tensor'), may hold values from -0.21875 to 0.21875
- b_qv: bfloat16 [2, 768], P(None, 'tensor'), may hold values from -1.796875 to 1.796875
- w_o: bfloat16 [768, 768], P('tensor'), may hold values from -0.875 to 0.875
- w_up: bfloat16 [768, 3072], P(None, 'tensor'), may hold values from -0.21875 to 0.21875
- b_up: bfloat16 [3072], P('tensor'), may hold values from -1.796875 to 1.796875
- w_down: bfloat16 [3072, 768], P('tensor'), may hold values from -0.109375 to 0.109375
- norm_gains: float32 [2, 768], replicated, may hold values from 0.25 to 1.75
- biases: float32 [4, 768], replicated, may hold values from -1.8 to 1.8
- cot_text: bfloat16 [32, 1004, 768], P(('dp', 'tensor')), may hold values from -6 to 6
- cot_memory: bfloat16 [32, 10, 768], P(('dp', 'tensor')), may hold values from -6 to 6
Outputs:
- text_out: bfloat16 [32, 1004, 768], P(('dp', 'tensor'))
- memory_out: bfloat16 [32, 10, 768], P(('dp', 'tensor'))
- grad_text: float32 [32, 1004, 768], P(('dp', 'tensor'))
- grad_memory: float32 [10, 768], replicated
- grad_w_qkv: float32 [3, 768, 768], P(None, None, 'tensor')
- grad_b_qv: float32 [2, 768], P(None, 'tensor')
- grad_w_o: float32 [768, 768], P('tensor')
- grad_w_up: float32 [768, 3072], P(None, 'tensor')
- grad_b_up: float32 [3072], P('tensor')
- grad_w_down: float32 [3072, 768], P('tensor')
- grad_gains: float32 [2, 768], replicated
- grad_biases: float32 [4, 768], replicated
The draws below stay inside these ranges and needn't reach their ends.
All inputs are finite; a program needn't handle non-finite values.
Results may differ from the reference program's by a relative error of at most 0.015.
The reference program's roundings to bfloat16 on the way count: a program that leaves them out, or rounds other values in their place, can miss the bound.
Values may be sent and summed in bfloat16 or wider, within the bound.
No kernel may reach another device: no remote copies, remote signals or barrier semaphores. Data moves between devices by JAX's collectives and lax.ppermute only.
A program may use at most 256 MiB of HBM per device.

```python
import math
import jax
import jax.numpy as jnp
from jax import lax

D = 768
FF = 3072
HEAD_DIM = 64
MEMORY = 10
SEGMENTS = 2
SEQ_OWN = 1
SEQUENCES = 32
TEXT_LEN = 1004
N_TENSOR = 4


def levels(rng, shape, split, low, high):
    loudness, own = 1.0, jax.random.fold_in(rng, 6)
    for axis_at, blocks in split:
        draws = jnp.exp(jax.random.uniform(jax.random.fold_in(own, axis_at), (blocks,), jnp.float32, low / len(split), high / len(split)))
        loudness = loudness * jnp.repeat(draws, shape[axis_at] // blocks).reshape([-1 if axis == axis_at else 1 for axis in range(len(shape))])
    return loudness


def noise(stream_key, extent, width, bound, split=(), held_as=jnp.bfloat16):
    values = width * jax.random.normal(stream_key, extent, jnp.float32)
    if split:
        values = values * levels(stream_key, extent, split, -0.22, 0.18)
    return jnp.clip(values, -bound, bound).astype(held_as)


def setup_inputs(seed: int = 0) -> dict:
    key_of = jax.random.split(jax.random.key(seed), 13)
    text_in = noise(key_of[0], (SEQUENCES, TEXT_LEN, D), 1.0, 6.0, ((0, 32),))
    start_memory = noise(key_of[1], (MEMORY, D), 1.0, 6.0)
    w_qkv = noise(key_of[2], (3, D, D), D ** -0.5, 0.21875, ((2, 4),))
    b_qv = noise(key_of[3], (2, D), 0.3, 1.796875, ((1, 4),))
    w_o = noise(key_of[4], (D, D), (D // 16) ** -0.5, 0.875, ((0, 4),))
    w_up = noise(key_of[5], (D, FF), D ** -0.5, 0.21875, ((1, 4),))
    b_up = noise(key_of[6], (FF,), 0.3, 1.796875, ((0, 4),))
    w_down = noise(key_of[7], (FF, D), FF ** -0.5, 0.109375, ((0, 4),))
    norm_gains = jnp.clip(1.0 + 0.15 * jax.random.normal(key_of[8], (2, D), jnp.float32), 0.25, 1.75)
    biases = noise(key_of[9], (4, D), 0.3, 1.8, (), jnp.float32)
    cot_text = noise(key_of[10], (SEQUENCES, TEXT_LEN, D), 1.0, 6.0, ((0, 32),))
    cot_memory = noise(key_of[11], (SEQUENCES, MEMORY, D), 1.0, 6.0, ((0, 32),))
    return dict(text_in=text_in, start_memory=start_memory, w_qkv=w_qkv, b_qv=b_qv, w_o=w_o, w_up=w_up, b_up=b_up, w_down=w_down, norm_gains=norm_gains, biases=biases, cot_text=cot_text, cot_memory=cot_memory)


@jax.custom_vjp
def low(v):
    return lax.optimization_barrier(v.astype(jnp.bfloat16)).astype(jnp.float32)

@jax.custom_vjp
def low_back(v):
    return v

def low_keep(v):
    return (low(v), None)

def low_pass(kept, grad):
    return (grad,)

def back_keep(v):
    return (v, None)

def back_low(kept, grad):
    return (low(grad),)
low.defvjp(low_keep, low_pass)
low_back.defvjp(back_keep, back_low)
HIGH = lax.Precision.HIGHEST
EPSILON = 1e-06

def norm_apply(value, gain, shift):
    row_mean = lax.optimization_barrier(jnp.mean(value, -1, keepdims=True))
    centred = value - row_mean
    return centred * lax.rsqrt(lax.optimization_barrier(jnp.mean(centred * centred, -1, keepdims=True)) + EPSILON) * gain + shift

def block_layer(layer_in, w_qkv, b_qv, w_o, w_up, b_up, w_down, norm_gains, biases):
    groups, row_total, model_width = layer_in.shape
    head_count = model_width // HEAD_DIM
    queries = low(low_back(jnp.einsum('grd,de->gre', layer_in, w_qkv[0], precision=HIGH) + b_qv[0]))
    key_rows = low(low_back(jnp.einsum('grd,de->gre', layer_in, w_qkv[1], precision=HIGH)))
    values = low(low_back(jnp.einsum('grd,de->gre', layer_in, w_qkv[2], precision=HIGH) + b_qv[1]))
    queries = queries.reshape(groups, row_total, head_count, HEAD_DIM)
    key_rows = key_rows.reshape(groups, row_total, head_count, HEAD_DIM)
    values = values.reshape(groups, row_total, head_count, HEAD_DIM)
    scores = low_back(jnp.einsum('gqhe,gkhe->ghqk', queries, key_rows, precision=HIGH) * (1.0 / math.sqrt(HEAD_DIM)))
    attn_probs = low(jax.nn.softmax(scores, -1))
    attended = jnp.einsum('ghqk,gkhe->gqhe', attn_probs, values, precision=HIGH)
    attended = low(low_back(attended.reshape(groups, row_total, model_width)))
    attn_out = low_back(jnp.einsum('grc,cd->grd', attended, w_o, precision=HIGH))
    middle = norm_apply(layer_in + attn_out + biases[0], norm_gains[0], biases[1])
    hidden = low_back(jnp.einsum('grd,df->grf', low(middle), w_up, precision=HIGH) + b_up)
    active = low(jax.nn.gelu(hidden, approximate=False))
    ffn_out = low_back(jnp.einsum('grf,fd->grd', active, w_down, precision=HIGH))
    return norm_apply(middle + ffn_out + biases[2], norm_gains[1], biases[3])

def rmt_forward(text_rows, start_mem, *weights):
    groups = text_rows.shape[0]
    seg_size = text_rows.shape[1] // SEGMENTS
    write_init = jnp.broadcast_to(start_mem[None], (groups,) + start_mem.shape)
    read_mem = write_init
    pieces = []
    for segment in range(SEGMENTS):
        layer_in = jnp.concatenate([read_mem, text_rows[:, segment * seg_size:(segment + 1) * seg_size], write_init], 1)
        result = block_layer(layer_in, *weights)
        pieces.append(result[:, MEMORY:MEMORY + seg_size])
        read_mem = low(result[:, MEMORY + seg_size:])
    return (jnp.concatenate(pieces, 1), read_mem)

def reference(text_in, start_memory, w_qkv, b_qv, w_o, w_up, b_up, w_down, norm_gains, biases, cot_text, cot_memory):
    weights = tuple((a.astype(jnp.float32) for a in (w_qkv, b_qv, w_o, w_up, b_up, w_down, norm_gains, biases)))
    start_mem = start_memory.astype(jnp.float32)
    group_size = SEQ_OWN * N_TENSOR
    group_count = SEQUENCES // group_size
    text_all = text_in.astype(jnp.float32).reshape((group_count, group_size) + text_in.shape[1:])
    cot_all = cot_text.astype(jnp.float32).reshape((group_count, group_size) + cot_text.shape[1:])
    cot_mems = cot_memory.astype(jnp.float32).reshape((group_count, group_size) + cot_memory.shape[1:])

    def scan_step(totals, scan_item):
        text_rows, grad_rows, grad_mems = scan_item
        results, pullback = jax.vjp(rmt_forward, text_rows, start_mem, *weights)
        gradients = pullback((grad_rows, grad_mems))
        totals = tuple((a + b for a, b in zip(totals, gradients[1:])))
        return (totals, (results[0].astype(jnp.bfloat16), results[1].astype(jnp.bfloat16), gradients[0]))
    zero_grads = tuple((jnp.zeros_like(a) for a in (start_mem,) + weights))
    totals, (text_outs, memory_outs, grad_texts) = lax.scan(scan_step, zero_grads, (text_all, cot_all, cot_mems))
    return (text_outs.reshape(text_in.shape), memory_outs.reshape(cot_memory.shape), grad_texts.reshape(text_in.shape), totals[0], totals[1], totals[2], totals[3], totals[4], totals[5], totals[6], totals[7], totals[8])
```

```python
import math

import jax
import jax.numpy as jnp
from jax import lax
from jax.sharding import PartitionSpec as P

HEAD_DIM = 64
SEGMENTS = 2
EPSILON = 1e-06
F32 = jnp.float32
BF16 = jnp.bfloat16


def dot(a, b, ca, cb):
    return lax.dot_general(a, b, (((ca,), (cb,)), ((), ())), preferred_element_type=F32)


def norm_stats(value):
    centred = value - jnp.mean(value, -1, keepdims=True)
    rstd = lax.rsqrt(jnp.mean(centred * centred, -1, keepdims=True) + EPSILON)
    return centred * rstd, rstd


def norm_backward(grad_out, normed, rstd, gain):
    scaled = grad_out * gain
    first = jnp.mean(scaled, -1, keepdims=True)
    second = jnp.mean(scaled * normed, -1, keepdims=True)
    return rstd * (scaled - first - normed * second)


def gelu_exact(values):
    return jax.nn.gelu(values, approximate=False)


def bit_pairs(axis, bit):
    return [(i, i ^ bit) for i in range(lax.axis_size(axis))]


def bit_of(axis, bit):
    return (lax.axis_index(axis) // bit) % 2


def bit_orders():
    bits = [1 << i for i in range(1, lax.axis_size("dp").bit_length() - 1)]
    return bits[::-1], bits


def chunk_index(order):
    index = 0
    for place, bit in enumerate(order + [1]):
        index = index + bit_of("dp", bit) * (1 << place)
    return index


def join(own, bit):
    other = lax.ppermute(own, "dp", bit_pairs("dp", bit))
    rows, at = own.shape[-2], bit_of("dp", bit) * own.shape[-2]
    both = jnp.zeros(own.shape[:-2] + (2 * rows, own.shape[-1]), own.dtype)
    both = lax.dynamic_update_slice_in_dim(both, own, at, own.ndim - 2)
    return lax.dynamic_update_slice_in_dim(both, other, rows - at, own.ndim - 2)


def join_all(part):
    half = part.shape[-1] // 2
    sides = []
    for side, order in enumerate(bit_orders()):
        piece = part[..., side * half : (side + 1) * half]
        for bit in order:
            piece = join(piece, bit)
        sides.append(piece)
    return join(jnp.concatenate(sides, -1), 1)


def line_gather(part):
    n = lax.axis_size("tensor")
    t = lax.axis_index("tensor")
    up, down = [part], [part]
    for k in range(1, n):
        up.append(lax.ppermute(up[-1], "tensor", [(z, z + 1) for z in range(k - 1, n - 1)]))
        down.append(lax.ppermute(down[-1], "tensor", [(z, z - 1) for z in range(1, n - k + 1)]))
    return jnp.stack([jnp.where(t >= s, up[s], down[n - s]) for s in range(1, n)])


def gather_rows(shard, extra=None):
    width = shard.shape[-1]
    rows = shard.shape[0] // lax.axis_size("dp")
    half = width // 2
    part = jnp.concatenate(
        [
            lax.dynamic_slice_in_dim(shard[:, side * half : (side + 1) * half], chunk_index(order) * rows, rows, 0)
            for side, order in enumerate(bit_orders())
        ],
        1,
    )
    if extra is not None:
        part = jnp.concatenate([part, extra])
    slots = line_gather(part)
    full = jnp.concatenate([shard[None], join_all(slots[:, :rows])])
    return full if extra is None else (full, jnp.concatenate([extra[None], slots[:, rows:]]))


def halve(total, bit):
    rows = total.shape[1] // 2
    at = bit_of("dp", bit) * rows
    send = lax.dynamic_slice_in_dim(total, rows - at, rows, 1).astype(BF16)
    keep = lax.dynamic_slice_in_dim(total, at, rows, 1)
    return keep + lax.ppermute(send, "dp", bit_pairs("dp", bit)).astype(F32)


def reduce_rows(partial):
    n = lax.axis_size("tensor")
    half = partial.shape[-1] // 2
    total = halve(partial, 1)
    sides = []
    for side, order in enumerate(bit_orders()):
        piece = total[..., side * half : (side + 1) * half]
        for bit in order[::-1]:
            piece = halve(piece, bit)
        sides.append(piece)
    total = jnp.concatenate(sides, -1)
    up = down = jnp.zeros(total.shape[1:], F32)
    for k in range(1, n):
        up = lax.ppermute((total[k] + up).astype(BF16), "tensor", [(z, z + 1) for z in range(min(k, n - 1))]).astype(F32)
        down = lax.ppermute(
            (total[n - k] + down).astype(BF16), "tensor", [(z, z - 1) for z in range(n - k, n)]
        ).astype(F32)
    return join_all((total[0] + up + down).astype(BF16)).astype(F32)


def sum_small(value):
    for axis in ("dp", "tensor"):
        bit = 1
        while bit < lax.axis_size(axis):
            value = value + lax.ppermute(value, axis, bit_pairs(axis, bit))
            bit *= 2
    return value


def local(text_in, start_memory, w_qkv, b_qv, w_o, w_up, b_up, w_down, norm_gains, biases, cot_text, cot_memory):
    text, cot_rows, cot_mem = text_in[0], cot_text[0], cot_memory[0]
    text_total, width = text.shape
    mem = start_memory.shape[0]
    seg = text_total // SEGMENTS
    n_t = lax.axis_size("tensor")
    head_part = w_qkv.shape[2]
    heads = width // HEAD_DIM
    scale = 1.0 / math.sqrt(HEAD_DIM)

    first = jnp.concatenate([w_qkv.transpose(0, 2, 1).reshape(3 * head_part, width), w_o])
    small = jnp.concatenate([b_qv.reshape(-1), b_up.reshape(-1)])
    small = jnp.pad(small, (0, 16 * width - small.shape[0])).reshape(16, width)
    first, small = gather_rows(first, small)
    qkv_t = [first[:, i * head_part : (i + 1) * head_part].reshape(width, width) for i in range(3)]
    out_full = first[:, 3 * head_part :].reshape(width, width)
    up_full = gather_rows(w_up)
    down_full = gather_rows(w_down)
    small = small.reshape(n_t, -1).astype(F32)
    q_bias = small[:, :head_part].reshape(1, -1)
    v_bias = small[:, head_part : 2 * head_part].reshape(1, -1)
    up_bias = small[:, 2 * head_part : 2 * head_part + b_up.shape[0]]

    read = start_memory
    kept, pieces = [], []
    for s in range(SEGMENTS):
        x = jnp.concatenate([text[s * seg : (s + 1) * seg], start_memory, read])
        rows = seg + mem
        q = (dot(x[:rows], qkv_t[0], 1, 1) + q_bias).astype(BF16).reshape(rows, heads, HEAD_DIM)
        k = dot(x, qkv_t[1], 1, 1).astype(BF16).reshape(-1, heads, HEAD_DIM)
        v = (dot(x, qkv_t[2], 1, 1) + v_bias).astype(BF16).reshape(-1, heads, HEAD_DIM)
        scores = jnp.einsum("qhe,khe->hqk", q, k, preferred_element_type=F32) * scale
        lse = jax.nn.logsumexp(scores, -1, keepdims=True)
        probs = jnp.exp(scores - lse).astype(BF16)
        att = jnp.einsum("hqk,khe->qhe", probs, v, preferred_element_type=F32).astype(BF16).reshape(rows, width)
        pre1 = x[:rows].astype(F32) + dot(att, out_full, 1, 0) + biases[0]
        n1, r1 = norm_stats(pre1)
        middle = n1 * norm_gains[0] + biases[1]
        low = middle.astype(BF16)
        hidden = jnp.einsum("rd,tdf->trf", low, up_full, preferred_element_type=F32) + up_bias[:, None]
        act = gelu_exact(hidden).astype(BF16)
        ffn = jnp.einsum("trf,tfd->rd", act, down_full, preferred_element_type=F32)
        n2, r2 = norm_stats(middle + ffn + biases[2])
        result = (n2 * norm_gains[1] + biases[3]).astype(BF16)
        pieces.append(result[:seg])
        read = result[seg:]
        kept.append((x, q, k, v, lse, att, n1, r1, low, hidden, n2, r2))

    d_qkv, d_out, d_up, d_down = [], [], [], []
    d_gain, d_bias, d_bqv, d_bup = [], [], [], []
    d_mem = jnp.zeros((mem, width), F32)
    carry = cot_mem.astype(F32)
    d_text = [None] * SEGMENTS
    for s in reversed(range(SEGMENTS)):
        x, q, k, v, lse, att, n1, r1, low, hidden, n2, r2 = kept[s]
        rows = seg + mem
        g_res = jnp.concatenate([cot_rows[s * seg : (s + 1) * seg].astype(F32), carry])
        g_pre2 = norm_backward(g_res, n2, r2, norm_gains[1])
        g_ffn = g_pre2.astype(BF16)
        act, pull = jax.vjp(gelu_exact, hidden)
        act = act.astype(BF16)
        d_down.append(jnp.einsum("trf,rd->tfd", act, g_ffn, preferred_element_type=F32))
        g_act = jnp.einsum("rd,tfd->trf", g_ffn, down_full, preferred_element_type=F32)
        g_hid = pull(g_act)[0].astype(BF16)
        d_up.append(jnp.einsum("rd,trf->tdf", low, g_hid, preferred_element_type=F32))
        d_bup.append(jnp.sum(g_hid.astype(F32), 1))
        g_mid = g_pre2 + jnp.einsum("trf,tdf->rd", g_hid, up_full, preferred_element_type=F32)
        g_pre1 = norm_backward(g_mid, n1, r1, norm_gains[0])
        g_attn = g_pre1.astype(BF16)
        d_out.append(dot(att, g_attn, 0, 0))
        g_att = dot(g_attn, out_full, 1, 1).astype(BF16).reshape(rows, heads, HEAD_DIM)
        scores = jnp.einsum("qhe,khe->hqk", q, k, preferred_element_type=F32) * scale
        full = jnp.exp(scores - lse)
        g_probs = jnp.einsum("qhe,khe->hqk", g_att, v, preferred_element_type=F32)
        g_sc = (full * (g_probs - jnp.sum(g_probs * full, -1, keepdims=True))).astype(BF16)
        g_q = (jnp.einsum("hqk,khe->qhe", g_sc, k, preferred_element_type=F32) * scale).astype(BF16)
        g_k = (jnp.einsum("hqk,qhe->khe", g_sc, q, preferred_element_type=F32) * scale).astype(BF16)
        g_v = jnp.einsum("hqk,qhe->khe", full.astype(BF16), g_att, preferred_element_type=F32).astype(BF16)
        g_q, g_k, g_v = (g.reshape(-1, width) for g in (g_q, g_k, g_v))
        d_qkv.append(jnp.stack([dot(g_q, x[:rows], 0, 0), dot(g_k, x, 0, 0), dot(g_v, x, 0, 0)]))
        d_bqv.append(jnp.stack([jnp.sum(g_q.astype(F32), 0), jnp.sum(g_v.astype(F32), 0)]))
        g_x = dot(g_k, qkv_t[1], 1, 0) + dot(g_v, qkv_t[2], 1, 0)
        top = g_x[:rows] + dot(g_q, qkv_t[0], 1, 0) + g_pre1
        d_text[s] = top[:seg]
        d_mem = d_mem + top[seg:]
        if s > 0:
            carry = g_x[rows:]
        else:
            d_mem = d_mem + g_x[rows:]
        d_gain.append(jnp.stack([jnp.sum(g_mid * n1, 0), jnp.sum(g_res * n2, 0)]))
        d_bias.append(jnp.stack([jnp.sum(g, 0) for g in (g_pre1, g_mid, g_pre2, g_res)]))

    total = lambda parts: parts[0] + parts[1]
    g_down = reduce_rows(total(d_down))
    g_up = reduce_rows(total(d_up))
    g_first = total(d_qkv).reshape(3, n_t, head_part, width).transpose(1, 0, 2, 3).reshape(n_t, -1, width)
    g_first = reduce_rows(jnp.concatenate([g_first, total(d_out).reshape(n_t, head_part, width)], 1))
    g_qkv = g_first[: 3 * head_part].reshape(3, head_part, width).transpose(0, 2, 1)
    g_out = g_first[3 * head_part :]
    t = lax.axis_index("tensor")
    order = (t - jnp.arange(n_t)) % n_t
    by_slot = jnp.concatenate(
        [total(d_bqv).reshape(2, n_t, head_part).transpose(1, 0, 2).reshape(n_t, -1), total(d_bup)], 1
    )
    by_index = jnp.zeros((n_t,) + by_slot.shape[1:], F32).at[order].set(by_slot)
    vectors = jnp.concatenate([total(d_gain), total(d_bias), d_mem])
    count = vectors.size
    vectors = sum_small(jnp.concatenate([vectors.reshape(-1), by_index.reshape(-1)]).reshape(-1, 128)).reshape(-1)
    own = lax.dynamic_slice_in_dim(vectors[count:].reshape(n_t, -1), t, 1, 0)[0]
    g_bqv = own[: 2 * head_part].reshape(2, head_part)
    g_bup = own[2 * head_part :]
    vectors = vectors[:count].reshape(-1, width)

    return (
        jnp.concatenate(pieces)[None],
        read[None],
        jnp.concatenate(d_text)[None],
        vectors[6 : 6 + mem],
        g_qkv,
        g_bqv,
        g_out,
        g_up,
        g_bup,
        g_down,
        vectors[:2],
        vectors[2:6],
    )


def solution(mesh):
    own = P(("dp", "tensor"), None, None)
    return jax.shard_map(
        local,
        mesh=mesh,
        in_specs=(
            own, P(), P(None, None, "tensor"), P(None, "tensor"), P("tensor", None), P(None, "tensor"),
            P("tensor"), P("tensor", None), P(), P(), own, own,
        ),
        out_specs=(
            own, own, own, P(), P(None, None, "tensor"), P(None, "tensor"), P("tensor", None),
            P(None, "tensor"), P("tensor"), P("tensor", None), P(), P(),
        ),
        check_vma=False,
    )
```

```python
import math

import jax
import jax.numpy as jnp
from jax import lax
from jax.experimental import pallas as pl
from jax.experimental.pallas import tpu as pltpu
from jax.sharding import PartitionSpec as P

HEAD_DIM = 64
SEGMENTS = 2
EPSILON = 1e-06
F32 = jnp.float32
BF16 = jnp.bfloat16


def dot(a, b, ca, cb):
    return lax.dot_general(a, b, (((ca,), (cb,)), ((), ())), preferred_element_type=F32)


def norm_stats(value):
    centred = value - jnp.mean(value, -1, keepdims=True)
    rstd = lax.rsqrt(jnp.mean(centred * centred, -1, keepdims=True) + EPSILON)
    return centred * rstd, rstd


def norm_backward(grad_out, normed, rstd, gain):
    scaled = grad_out * gain
    first = jnp.mean(scaled, -1, keepdims=True)
    second = jnp.mean(scaled * normed, -1, keepdims=True)
    return rstd * (scaled - first - normed * second)


def gelu_exact(values):
    return jax.nn.gelu(values, approximate=False)


def log2(n):
    return n.bit_length() - 1


def outer_mask(core, step):
    outer = log2(lax.axis_size("dp")) - 1
    return 2 << (step if core == 0 else outer - 1 - step)


def outer_exchange(value, step):
    pairs = [(i, i ^ outer_mask(i & 1, step)) for i in range(lax.axis_size("dp"))]
    return lax.ppermute(value, "dp", pairs)


def core_exchange(value):
    return lax.ppermute(value, "dp", [(i, i ^ 1) for i in range(lax.axis_size("dp"))])


def line_exchange(value, step):
    n = lax.axis_size("tensor")
    pairs = []
    for i in range(lax.axis_size("dp")):
        mask = 1 << (step if i & 1 == 0 else log2(n) - 1 - step)
        pairs += [(i * n + t, i * n + (t ^ mask)) for t in range(n)]
    return lax.ppermute(value, ("dp", "tensor"), pairs)


def outer_steps():
    return range(log2(lax.axis_size("dp")) - 1)


def line_steps():
    return range(log2(lax.axis_size("tensor")))


def arrival_sources():
    half = lax.axis_size("dp") // 2
    tables = [
        jnp.array([sum(outer_mask(core, i) for i in outer_steps() if j >> i & 1) for j in range(half)], jnp.int32)
        for core in (0, 1)
    ]
    d = lax.axis_index("dp")
    core = d % 2
    mine = jnp.where(core == 0, tables[0], tables[1])
    theirs = jnp.where(core == 0, tables[1], tables[0])
    return jnp.concatenate([d ^ mine, d ^ 1 ^ theirs])


def slot_masks():
    n = lax.axis_size("tensor")
    orders = []
    for flip in (False, True):
        places = [log2(n) - 1 - i if flip else i for i in line_steps()]
        orders.append(jnp.array([sum(1 << places[i] for i in line_steps() if s >> i & 1) for s in range(n)], jnp.int32))
    core = lax.axis_index("dp") % 2
    return jnp.where(core == 0, orders[0], orders[1]), jnp.where(core == 0, orders[1], orders[0])


def other_half_slots():
    n = lax.axis_size("tensor")
    return [sum(1 << (log2(n) - 1 - i) for i in line_steps() if s >> i & 1) for s in range(n)]


def reorder(chunks, source, scatter, dtype):
    n, rows, width = chunks.shape

    def body(source_ref, in_ref, out_ref):
        out_ref[...] = in_ref[...].astype(dtype)

    straight = lambda i, source: (i, 0, 0)
    moved = lambda i, source: (source[i], 0, 0)
    block = (1, rows, width)
    return pl.pallas_call(
        body,
        grid_spec=pltpu.PrefetchScalarGridSpec(
            num_scalar_prefetch=1,
            grid=(n,),
            in_specs=[pl.BlockSpec(block, straight if scatter else moved)],
            out_specs=pl.BlockSpec(block, moved if scatter else straight),
        ),
        out_shape=jax.ShapeDtypeStruct(chunks.shape, dtype),
        name="reorder",
    )(source, chunks)


def gather_chunks(chunks):
    slots = lax.dynamic_index_in_dim(chunks, lax.axis_index("dp"), 0)
    for step in line_steps():
        slots = jnp.concatenate([slots, line_exchange(slots, step)])
    rest = slots[None, 1:]
    for step in outer_steps():
        rest = jnp.concatenate([rest, outer_exchange(rest, step)])
    return reorder(chunks, arrival_sources(), False, BF16), rest, core_exchange(rest)


def reduce_begin(first, own, received):
    half = first.shape[0] // 2
    keep = jnp.concatenate([first[:half, None], own], 1)
    send = jnp.concatenate([first[half:, None], received], 1)
    return keep, send.astype(BF16)


def reduce_end(keep, send):
    total = (keep + core_exchange(send).astype(F32)).astype(BF16)
    plus = lambda a, b: (a.astype(F32) + b.astype(F32)).astype(BF16)
    for step in reversed(outer_steps()):
        half = total.shape[0] // 2
        total = plus(total[:half], outer_exchange(total[half:], step))
    total = total[0]
    for step in reversed(line_steps()):
        half = total.shape[0] // 2
        total = plus(total[:half], line_exchange(total[half:], step))
    for step in outer_steps():
        total = jnp.concatenate([total, outer_exchange(total, step)])
    total = jnp.concatenate([total, core_exchange(total)])
    return reorder(total, arrival_sources(), True, F32)


def sum_small(value):
    for axis in ("dp", "tensor"):
        bit = 1
        while bit < lax.axis_size(axis):
            value = value + lax.ppermute(value, axis, [(i, i ^ bit) for i in range(lax.axis_size(axis))])
            bit *= 2
    return value


def local(text_in, start_memory, w_qkv, b_qv, w_o, w_up, b_up, w_down, norm_gains, biases, cot_text, cot_memory):
    text, cot_rows, cot_mem = text_in[0], cot_text[0], cot_memory[0]
    text_total, width = text.shape
    mem = start_memory.shape[0]
    seg = text_total // SEGMENTS
    n_t, n_dp = lax.axis_size("tensor"), lax.axis_size("dp")
    heads = width // HEAD_DIM
    own_heads = heads // n_t
    feats = HEAD_DIM // n_dp
    group = 4 * own_heads * feats
    ff = b_up.shape[0]
    chunk = ff // n_dp
    half = n_dp // 2
    scale = 1.0 / math.sqrt(HEAD_DIM)
    swap = other_half_slots()
    source = arrival_sources()

    def by_head(first, own, received):
        received = jnp.stack([received[:, swap[s] - 1] for s in range(1, n_t)], 1)
        rows = jnp.concatenate([first[:, None], jnp.concatenate([own, received])], 1)
        rows = rows.reshape(n_dp, n_t, 4, own_heads, feats, -1)
        return rows.transpose(2, 1, 3, 0, 4, 5).reshape(4, width, -1)

    def by_arrival(kinds):
        rows = kinds.reshape(kinds.shape[0], n_t, own_heads, n_dp, feats, -1).transpose(3, 1, 0, 2, 4, 5)
        rows = rows.reshape(n_dp, n_t, -1, kinds.shape[-1])
        received = jnp.stack([rows[half:, swap[s]] for s in range(1, n_t)], 1)
        return rows[:, 0], rows[:half, 1:], received

    kinds = jnp.concatenate([w_qkv.transpose(0, 2, 1), w_o[None]]).reshape(4, own_heads, n_dp, feats, width)
    kinds = kinds.transpose(2, 0, 1, 3, 4).reshape(n_dp, group, width)
    small = b_qv.reshape(2, own_heads, n_dp, feats).transpose(2, 0, 1, 3).reshape(n_dp, -1)
    small = jnp.concatenate([small, b_up.reshape(n_dp, chunk)], 1)
    n_small = small.shape[1]
    small = jnp.pad(small, ((0, 0), (0, 8 * width - n_small))).reshape(n_dp, 8, width)
    got = gather_chunks(jnp.concatenate([kinds, small], 1))
    q_w, k_w, v_w, o_w = by_head(*(g[..., :group, :] for g in got))
    small = [g[..., group:, :].reshape(g.shape[:-2] + (-1,))[..., :n_small].astype(F32) for g in got]
    qv = [s[..., : 2 * own_heads * feats].reshape(s.shape[:-1] + (2 * own_heads * feats, 1)) for s in small]
    qv = [jnp.concatenate([s, s], -2) for s in qv]
    qv = by_head(*qv)
    q_bias, v_bias = qv[0].reshape(1, -1), qv[1].reshape(1, -1)
    up_bias = jnp.concatenate([s[..., 2 * own_heads * feats :].reshape(-1) for s in small])
    flat = lambda got: jnp.concatenate([g.reshape(-1, width) for g in got])
    up_full = flat(gather_chunks(w_up.T.reshape(n_dp, chunk, width)))
    down_full = flat(gather_chunks(w_down.reshape(n_dp, chunk, width)))

    def by_chunk(rows):
        own, received = (rows[ff + i * half * (n_t - 1) * chunk :][: half * (n_t - 1) * chunk] for i in (0, 1))
        shape = (half, n_t - 1, chunk, -1)
        return rows[:ff].reshape(n_dp, chunk, -1), own.reshape(shape), received.reshape(shape)

    read = start_memory
    kept, pieces = [], []
    for s in range(SEGMENTS):
        x = jnp.concatenate([text[s * seg : (s + 1) * seg], start_memory, read])
        rows = seg + mem
        q = (dot(x[:rows], q_w, 1, 1) + q_bias).astype(BF16).reshape(rows, heads, HEAD_DIM)
        k = dot(x, k_w, 1, 1).astype(BF16).reshape(-1, heads, HEAD_DIM)
        v = (dot(x, v_w, 1, 1) + v_bias).astype(BF16).reshape(-1, heads, HEAD_DIM)
        scores = jnp.einsum("qhe,khe->hqk", q, k, preferred_element_type=F32) * scale
        lse = jax.nn.logsumexp(scores, -1, keepdims=True)
        probs = jnp.exp(scores - lse).astype(BF16)
        att = jnp.einsum("hqk,khe->qhe", probs, v, preferred_element_type=F32).astype(BF16).reshape(rows, width)
        pre1 = x[:rows].astype(F32) + dot(att, o_w, 1, 0) + biases[0]
        n1, r1 = norm_stats(pre1)
        middle = n1 * norm_gains[0] + biases[1]
        low = middle.astype(BF16)
        hidden = dot(low, up_full, 1, 1) + up_bias
        act = gelu_exact(hidden).astype(BF16)
        ffn = dot(act, down_full, 1, 0)
        n2, r2 = norm_stats(middle + ffn + biases[2])
        result = (n2 * norm_gains[1] + biases[3]).astype(BF16)
        pieces.append(result[:seg])
        read = result[seg:]
        kept.append((x, q, k, v, lse, att, n1, r1, low, hidden, n2, r2))

    d_qkv, d_out, d_up, d_down = [], [], [], []
    d_gain, d_bias, d_bqv, d_bup = [], [], [], []
    d_mem = jnp.zeros((mem, width), F32)
    carry = cot_mem.astype(F32)
    d_text = [None] * SEGMENTS
    for s in reversed(range(SEGMENTS)):
        x, q, k, v, lse, att, n1, r1, low, hidden, n2, r2 = kept[s]
        rows = seg + mem
        g_res = jnp.concatenate([cot_rows[s * seg : (s + 1) * seg].astype(F32), carry])
        g_pre2 = norm_backward(g_res, n2, r2, norm_gains[1])
        g_ffn = g_pre2.astype(BF16)
        act, pull = jax.vjp(gelu_exact, hidden)
        act = act.astype(BF16)
        d_down.append(dot(act, g_ffn, 0, 0))
        g_act = dot(g_ffn, down_full, 1, 1)
        g_hid = pull(g_act)[0].astype(BF16)
        d_up.append(dot(g_hid, low, 0, 0))
        d_bup.append(jnp.sum(g_hid.astype(F32), 0))
        g_mid = g_pre2 + dot(g_hid, up_full, 1, 0)
        g_pre1 = norm_backward(g_mid, n1, r1, norm_gains[0])
        if s == 0:
            begun = [reduce_begin(*by_chunk(d[0] + d[1])) for d in (d_down, d_up)]
            g_pre1, begun = lax.optimization_barrier((g_pre1, begun))
            reduced = [reduce_end(*b) for b in begun]
        g_attn = g_pre1.astype(BF16)
        d_out.append(dot(att, g_attn, 0, 0))
        g_att = dot(g_attn, o_w, 1, 1).astype(BF16).reshape(rows, heads, HEAD_DIM)
        scores = jnp.einsum("qhe,khe->hqk", q, k, preferred_element_type=F32) * scale
        full = jnp.exp(scores - lse)
        g_probs = jnp.einsum("qhe,khe->hqk", g_att, v, preferred_element_type=F32)
        g_sc = (full * (g_probs - jnp.sum(g_probs * full, -1, keepdims=True))).astype(BF16)
        g_q = (jnp.einsum("hqk,khe->qhe", g_sc, k, preferred_element_type=F32) * scale).astype(BF16)
        g_k = (jnp.einsum("hqk,qhe->khe", g_sc, q, preferred_element_type=F32) * scale).astype(BF16)
        g_v = jnp.einsum("hqk,qhe->khe", full.astype(BF16), g_att, preferred_element_type=F32).astype(BF16)
        g_q, g_k, g_v = (g.reshape(-1, width) for g in (g_q, g_k, g_v))
        d_qkv.append(jnp.stack([dot(g_q, x[:rows], 0, 0), dot(g_k, x, 0, 0), dot(g_v, x, 0, 0)]))
        d_bqv.append(jnp.stack([jnp.sum(g_q.astype(F32), 0), jnp.sum(g_v.astype(F32), 0)]))
        g_x = dot(g_k, k_w, 1, 0) + dot(g_v, v_w, 1, 0)
        top = g_x[:rows] + dot(g_q, q_w, 1, 0) + g_pre1
        d_text[s] = top[:seg]
        d_mem = d_mem + top[seg:]
        if s > 0:
            carry = g_x[rows:]
        else:
            d_mem = d_mem + g_x[rows:]
        d_gain.append(jnp.stack([jnp.sum(g_mid * n1, 0), jnp.sum(g_res * n2, 0)]))
        d_bias.append(jnp.stack([jnp.sum(g, 0) for g in (g_pre1, g_mid, g_pre2, g_res)]))

    total = lambda parts: parts[0] + parts[1]
    g_down = reduced[0].reshape(ff, width)
    g_up = reduced[1].reshape(ff, width).T
    g_kinds = jnp.concatenate([total(d_qkv), total(d_out)[None]])
    g_kinds = reduce_end(*reduce_begin(*by_arrival(g_kinds)))
    g_kinds = g_kinds.reshape(n_dp, 4, own_heads, feats, width).transpose(1, 2, 0, 3, 4).reshape(4, -1, width)
    g_qkv, g_out = g_kinds[:3].transpose(0, 2, 1), g_kinds[3]
    t = lax.axis_index("tensor")
    small = [
        jnp.concatenate([a.reshape(a.shape[:-2] + (-1,)), b.reshape(b.shape[:-2] + (-1,))], -1)
        for a, b in zip(by_arrival(total(d_bqv)[..., None]), by_chunk(total(d_bup)[:, None]))
    ]
    masks, other_masks = slot_masks()
    at = jnp.concatenate([
        (t * n_dp + source),
        ((t ^ masks[1:]) * n_dp + source[:half, None]).reshape(-1),
        ((t ^ other_masks[1:]) * n_dp + source[half:, None]).reshape(-1),
    ])
    small = jnp.concatenate([s.reshape(-1, n_small) for s in small])
    pick = (jnp.arange(n_t * n_dp)[:, None] == at).astype(F32)
    small = jnp.dot(pick, small, precision=lax.Precision.HIGHEST)
    vectors = jnp.concatenate([total(d_gain), total(d_bias), d_mem])
    count = vectors.size
    vectors = sum_small(jnp.concatenate([vectors.reshape(-1), small.reshape(-1)]).reshape(-1, 128)).reshape(-1)
    own = lax.dynamic_slice_in_dim(vectors[count:].reshape(n_t, -1), t, 1, 0)[0].reshape(n_dp, n_small)
    n_qv = n_small - chunk
    g_bqv = own[:, :n_qv].reshape(n_dp, 2, own_heads, feats).transpose(1, 2, 0, 3).reshape(2, -1)
    g_bup = own[:, n_qv:].reshape(-1)
    vectors = vectors[:count].reshape(-1, width)

    return (
        jnp.concatenate(pieces)[None],
        read[None],
        jnp.concatenate(d_text)[None],
        vectors[6 : 6 + mem],
        g_qkv,
        g_bqv,
        g_out,
        g_up,
        g_bup,
        g_down,
        vectors[:2],
        vectors[2:6],
    )


def solution(mesh):
    own = P(("dp", "tensor"), None, None)
    return jax.shard_map(
        local,
        mesh=mesh,
        in_specs=(
            own, P(), P(None, None, "tensor"), P(None, "tensor"), P("tensor", None), P(None, "tensor"),
            P("tensor"), P("tensor", None), P(), P(), own, own,
        ),
        out_specs=(
            own, own, own, P(), P(None, None, "tensor"), P(None, "tensor"), P("tensor", None),
            P(None, "tensor"), P("tensor"), P("tensor", None), P(), P(),
        ),
        check_vma=False,
    )
```

```python
import math

import jax
import jax.numpy as jnp
from jax import lax
from jax.experimental import pallas as pl
from jax.experimental.pallas import tpu as pltpu
from jax.sharding import PartitionSpec as P

HEAD_DIM = 64
SEGMENTS = 2
EPSILON = 1e-06
LANES = 128
F32 = jnp.float32
BF16 = jnp.bfloat16


def dot(a, b, ca, cb):
    return lax.dot_general(a, b, (((ca,), (cb,)), ((), ())), preferred_element_type=F32)


def norm_stats(value):
    centred = value - jnp.mean(value, -1, keepdims=True)
    rstd = lax.rsqrt(jnp.mean(centred * centred, -1, keepdims=True) + EPSILON)
    return centred * rstd, rstd


def norm_backward(grad_out, normed, rstd, gain):
    scaled = grad_out * gain
    first = jnp.mean(scaled, -1, keepdims=True)
    second = jnp.mean(scaled * normed, -1, keepdims=True)
    return rstd * (scaled - first - normed * second)


def log2(n):
    return n.bit_length() - 1


def outer_mask(core, step):
    outer = log2(lax.axis_size("dp")) - 1
    return 2 << (step if core == 0 else outer - 1 - step)


def outer_exchange(value, step):
    pairs = [(i, i ^ outer_mask(i & 1, step)) for i in range(lax.axis_size("dp"))]
    return lax.ppermute(value, "dp", pairs)


def core_exchange(value):
    return lax.ppermute(value, "dp", [(i, i ^ 1) for i in range(lax.axis_size("dp"))])


def line_exchange(value, step):
    n = lax.axis_size("tensor")
    pairs = []
    for i in range(lax.axis_size("dp")):
        mask = 1 << (step if i & 1 == 0 else log2(n) - 1 - step)
        pairs += [(i * n + t, i * n + (t ^ mask)) for t in range(n)]
    return lax.ppermute(value, ("dp", "tensor"), pairs)


def outer_steps():
    return range(log2(lax.axis_size("dp")) - 1)


def line_steps():
    return range(log2(lax.axis_size("tensor")))


def arrival_sources():
    half = lax.axis_size("dp") // 2
    tables = [
        jnp.array([sum(outer_mask(core, i) for i in outer_steps() if j >> i & 1) for j in range(half)], jnp.int32)
        for core in (0, 1)
    ]
    d = lax.axis_index("dp")
    core = d % 2
    mine = jnp.where(core == 0, tables[0], tables[1])
    theirs = jnp.where(core == 0, tables[1], tables[0])
    return jnp.concatenate([d ^ mine, d ^ 1 ^ theirs])


def slot_masks():
    n = lax.axis_size("tensor")
    orders = []
    for flip in (False, True):
        places = [log2(n) - 1 - i if flip else i for i in line_steps()]
        orders.append(jnp.array([sum(1 << places[i] for i in line_steps() if s >> i & 1) for s in range(n)], jnp.int32))
    core = lax.axis_index("dp") % 2
    return jnp.where(core == 0, orders[0], orders[1]), jnp.where(core == 0, orders[1], orders[0])


def other_half_slots():
    n = lax.axis_size("tensor")
    return [sum(1 << (log2(n) - 1 - i) for i in line_steps() if s >> i & 1) for s in range(n)]


def moved_call(body, table, grid, ins, outs, operands, name):
    return pl.pallas_call(
        body,
        grid_spec=pltpu.PrefetchScalarGridSpec(
            num_scalar_prefetch=1,
            grid=grid,
            in_specs=[pl.BlockSpec(*spec) for spec in ins],
            out_specs=[pl.BlockSpec(*spec) for spec, _ in outs],
        ),
        out_shape=[shape for _, shape in outs],
        name=name,
    )(table, *operands)


def place(chunks, own, received):
    n, rows, width = chunks.shape
    half, others = own.shape[:2]
    swap = other_half_slots()
    source = arrival_sources()
    if rows % 16:
        received = jnp.stack([received[:, swap[s] - 1] for s in range(1, others + 1)], 1)
        moved = jnp.concatenate([own, received])[jnp.argsort(source)]
        return jnp.concatenate([chunks[None], moved.transpose(1, 0, 2, 3)])
    table = jnp.concatenate([source, jnp.array([max(s - 1, 0) for s in swap], jnp.int32)])

    def body(table_ref, chunks_ref, own_ref, received_ref, out_ref):
        slot = pl.program_id(0)

        @pl.when(slot == 0)
        def _():
            out_ref[0] = chunks_ref[...]

        @pl.when(slot > 0)
        def _():
            for p in range(half):
                out_ref[0, table_ref[p]] = own_ref[p, 0]
                out_ref[0, table_ref[half + p]] = received_ref[p, 0]

    block = (half, 1, rows, width)
    return moved_call(
        body, table, (others + 1,),
        [
            ((n, rows, width), lambda s, table: (0, 0, 0)),
            (block, lambda s, table: (0, jnp.maximum(s - 1, 0), 0, 0)),
            (block, lambda s, table: (0, table[n + s], 0, 0)),
        ],
        [(((1, n, rows, width), lambda s, table: (s, 0, 0, 0)), jax.ShapeDtypeStruct((others + 1, n, rows, width), BF16))],
        (chunks, own, received), "place",
    )[0]


def pack(total):
    slots, n, rows, width = total.shape
    half = n // 2
    swap = other_half_slots()
    source = arrival_sources()
    if rows % 16:
        moved = total.transpose(1, 0, 2, 3)[source]
        return moved[:half], jnp.stack([moved[half:, s] for s in swap], 1)
    table = jnp.concatenate([source, jnp.array(swap, jnp.int32)])

    def body(table_ref, mine_ref, theirs_ref, keep_ref, send_ref):
        for p in range(half):
            keep_ref[p, 0] = mine_ref[0, table_ref[p]]
            send_ref[p, 0] = theirs_ref[0, table_ref[half + p]]

    block = (1, n, rows, width)
    out = (((half, 1, rows, width), lambda s, table: (0, s, 0, 0)), jax.ShapeDtypeStruct((half, slots, rows, width), BF16))
    return moved_call(
        body, table, (slots,),
        [(block, lambda s, table: (s, 0, 0, 0)), (block, lambda s, table: (table[n + s], 0, 0, 0))],
        [out, out], (total, total), "pack",
    )


def finish(own, received):
    half, rows, width = own.shape
    source = arrival_sources()
    if rows % 16:
        return jnp.concatenate([own, received])[jnp.argsort(source)].astype(F32)

    def body(table_ref, own_ref, received_ref, out_ref):
        for p in range(half):
            out_ref[table_ref[p]] = own_ref[p].astype(F32)
            out_ref[table_ref[half + p]] = received_ref[p].astype(F32)

    whole = ((half, rows, width), lambda i, table: (0, 0, 0))
    out = ((2 * half, rows, width), lambda i, table: (0, 0, 0))
    return moved_call(
        body, source, (1,), [whole, whole], [(out, jax.ShapeDtypeStruct(out[0], F32))], (own, received), "finish"
    )[0]


def gather_chunks(chunks):
    slots = lax.dynamic_index_in_dim(chunks, lax.axis_index("dp"), 0)
    for step in line_steps():
        slots = jnp.concatenate([slots, line_exchange(slots, step)])
    rest = slots[None, 1:]
    for step in outer_steps():
        rest = jnp.concatenate([rest, outer_exchange(rest, step)])
    return place(chunks, rest, core_exchange(rest))


def plus(a, b):
    return (a.astype(F32) + b.astype(F32)).astype(BF16)


def reduce_core(packed):
    return plus(packed[0], core_exchange(packed[1]))


def reduce_outer(total):
    for step in reversed(outer_steps()):
        half = total.shape[0] // 2
        total = plus(total[:half], outer_exchange(total[half:], step))
    return total[0]


def reduce_line(total):
    for step in reversed(line_steps()):
        half = total.shape[0] // 2
        total = plus(total[:half], line_exchange(total[half:], step))
    return total


def spread(total):
    for step in outer_steps():
        total = jnp.concatenate([total, outer_exchange(total, step)])
    return finish(total, core_exchange(total))


def sum_small(value):
    for axis in ("dp", "tensor"):
        bit = 1
        while bit < lax.axis_size(axis):
            value = value + lax.ppermute(value, axis, [(i, i ^ bit) for i in range(lax.axis_size(axis))])
            bit *= 2
    return value


def ffn_forward(low, up, up_bias, down):
    rows, width = low.shape
    slots, part = up_bias.shape[0], up_bias.shape[2]

    def body(low_ref, up_ref, bias_ref, down_ref, act_ref, slope_ref, out_ref):
        @pl.when(pl.program_id(0) == 0)
        def _():
            out_ref[...] = jnp.zeros_like(out_ref)

        step = rows // 4
        for i in range(4):
            at = slice(i * step, (i + 1) * step)
            hidden = dot(low_ref[at, :], up_ref[0], 1, 0) + bias_ref[0]
            cdf = 0.5 * (1.0 + lax.erf(hidden * math.sqrt(0.5)))
            act = (hidden * cdf).astype(BF16)
            act_ref[at, :] = act
            pdf = jnp.exp(hidden * hidden * -0.5) * (1.0 / math.sqrt(2.0 * math.pi))
            slope_ref[at, :] = (cdf + hidden * pdf).astype(BF16)
            out_ref[at, :] += dot(act, down_ref[0], 1, 0)

    whole = pl.BlockSpec((rows, width), lambda s: (0, 0))
    slot = pl.BlockSpec((1, width, part), lambda s: (s, 0, 0))
    return pl.pallas_call(
        body,
        grid=(slots,),
        in_specs=[
            whole, slot, pl.BlockSpec((1, 1, part), lambda s: (s, 0, 0)), pl.BlockSpec((1, part, width), lambda s: (s, 0, 0))
        ],
        out_specs=[pl.BlockSpec((rows, part), lambda s: (0, s)), pl.BlockSpec((rows, part), lambda s: (0, s)), whole],
        out_shape=[
            jax.ShapeDtypeStruct((rows, slots * part), BF16),
            jax.ShapeDtypeStruct((rows, slots * part), BF16),
            jax.ShapeDtypeStruct((rows, width), F32),
        ],
        name="ffn_forward",
    )(low, up, up_bias, down)


def ffn_backward(g_ffn, low, act, slope, up, down, earlier):
    rows, width = low.shape
    slots, part = up.shape[0], up.shape[2]

    def body(g_ref, low_ref, act_ref, slope_ref, up_ref, down_ref, *refs):
        olds, (mid_ref, bias_ref, d_up_ref, d_down_ref) = refs[:-4], refs[-4:]
        g = g_ref[...]
        hid = (dot(g, down_ref[0], 1, 1) * slope_ref[...].astype(F32)).astype(BF16)
        bias_ref[0] = jnp.sum(hid.astype(F32), 0, keepdims=True)
        back = dot(hid, up_ref[0], 1, 1)

        @pl.when(pl.program_id(0) == 0)
        def _():
            mid_ref[...] = back

        @pl.when(pl.program_id(0) > 0)
        def _():
            mid_ref[...] += back

        d_up = dot(low_ref[...], hid, 0, 0)
        d_down = dot(act_ref[...], g, 0, 0)
        if olds:
            d_up = d_up + olds[0][0]
            d_down = d_down + olds[1][0]
        d_up_ref[0] = d_up.astype(d_up_ref.dtype)
        d_down_ref[0] = d_down.astype(d_down_ref.dtype)

    whole = pl.BlockSpec((rows, width), lambda s: (0, 0))
    units = pl.BlockSpec((rows, part), lambda s: (0, s))
    upper = pl.BlockSpec((1, width, part), lambda s: (s, 0, 0))
    lower = pl.BlockSpec((1, part, width), lambda s: (s, 0, 0))
    kind = BF16 if earlier else F32
    return pl.pallas_call(
        body,
        grid=(slots,),
        in_specs=[whole, whole, units, units, upper, lower] + ([upper, lower] if earlier else []),
        out_specs=[whole, pl.BlockSpec((1, 1, part), lambda s: (s, 0, 0)), upper, lower],
        out_shape=[
            jax.ShapeDtypeStruct((rows, width), F32),
            jax.ShapeDtypeStruct((slots, 1, part), F32),
            jax.ShapeDtypeStruct((slots, width, part), kind),
            jax.ShapeDtypeStruct((slots, part, width), kind),
        ],
        name="ffn_backward",
    )(g_ffn, low, act, slope, up, down, *earlier)


def lane_masks(rows):
    lane = lax.broadcasted_iota(jnp.int32, (rows, LANES), 1)
    return [(lane >= h * HEAD_DIM) & (lane < (h + 1) * HEAD_DIM) for h in range(LANES // HEAD_DIM)]


def only(mask, value):
    return jnp.where(mask, value, jnp.zeros_like(value))


def attention_forward(q, k, v, keys):
    rows, width = q.shape
    padded = k.shape[0]
    scale = 1.0 / math.sqrt(HEAD_DIM)

    def body(q_ref, k_ref, v_ref, out_ref, lse_ref):
        q = q_ref[...] * jnp.asarray(scale, BF16)
        k, v = k_ref[...], v_ref[...]
        live = lax.broadcasted_iota(jnp.int32, (1, padded), 1) < keys
        out = jnp.zeros((rows, LANES), F32)
        lses = jnp.zeros((rows, LANES), F32)
        for mine, theirs in zip(lane_masks(rows), lane_masks(padded)):
            scores = jnp.where(live, dot(only(mine, q), k, 1, 1), -jnp.inf)
            top = jnp.max(scores, -1, keepdims=True)
            weights = jnp.exp(scores - top)
            total = jnp.sum(weights, -1, keepdims=True)
            probs = (weights * (1.0 / total)).astype(BF16)
            out = out + dot(probs, only(theirs, v), 1, 0)
            lses = jnp.where(mine, top + jnp.log(total), lses)
        out_ref[...] = out.astype(BF16)
        lse_ref[...] = lses

    q_spec = pl.BlockSpec((rows, LANES), lambda h: (0, h))
    k_spec = pl.BlockSpec((padded, LANES), lambda h: (0, h))
    return pl.pallas_call(
        body,
        grid=(width // LANES,),
        in_specs=[q_spec, k_spec, k_spec],
        out_specs=[q_spec, q_spec],
        out_shape=[jax.ShapeDtypeStruct((rows, width), BF16), jax.ShapeDtypeStruct((rows, width), F32)],
        name="attention_forward",
    )(q, k, v)


def attention_backward(q, k, v, lse, g_att, keys):
    rows, width = q.shape
    padded = k.shape[0]
    scale = 1.0 / math.sqrt(HEAD_DIM)

    def body(q_ref, k_ref, v_ref, lse_ref, g_ref, gq_ref, gk_ref, gv_ref, sum_q_ref, sum_v_ref):
        q, g = q_ref[...] * jnp.asarray(scale, BF16), g_ref[...]
        k, v = k_ref[...], v_ref[...]
        live = lax.broadcasted_iota(jnp.int32, (1, padded), 1) < keys
        gq = jnp.zeros((rows, LANES), F32)
        gk = jnp.zeros((padded, LANES), F32)
        gv = jnp.zeros((padded, LANES), F32)
        for h, (mine, theirs) in enumerate(zip(lane_masks(rows), lane_masks(padded))):
            q_h, g_h = only(mine, q), only(mine, g)
            scores = dot(q_h, k, 1, 1)
            full = jnp.where(live, jnp.exp(scores - lse_ref[:, h * HEAD_DIM : h * HEAD_DIM + 1]), 0.0)
            g_probs = dot(g_h, v, 1, 1)
            inner = jnp.sum(g_probs * full, -1, keepdims=True)
            g_scores = (full * (g_probs - inner)).astype(BF16)
            gq = gq + dot(g_scores, only(theirs, k), 1, 0)
            gk = gk + dot(g_scores, q_h, 0, 0)
            gv = gv + dot(full.astype(BF16), g_h, 0, 0)
        gq = (gq * scale).astype(BF16)
        gv = gv.astype(BF16)
        gq_ref[...] = gq
        gk_ref[...] = gk.astype(BF16)
        gv_ref[...] = gv
        sum_q_ref[...] = jnp.sum(gq.astype(F32), 0, keepdims=True)
        sum_v_ref[...] = jnp.sum(gv.astype(F32), 0, keepdims=True)

    q_spec = pl.BlockSpec((rows, LANES), lambda h: (0, h))
    k_spec = pl.BlockSpec((padded, LANES), lambda h: (0, h))
    sum_spec = pl.BlockSpec((1, LANES), lambda h: (0, h))
    return pl.pallas_call(
        body,
        grid=(width // LANES,),
        in_specs=[q_spec, k_spec, k_spec, q_spec, q_spec],
        out_specs=[q_spec, k_spec, k_spec, sum_spec, sum_spec],
        out_shape=[
            jax.ShapeDtypeStruct((rows, width), BF16),
            jax.ShapeDtypeStruct((padded, width), BF16),
            jax.ShapeDtypeStruct((padded, width), BF16),
            jax.ShapeDtypeStruct((1, width), F32),
            jax.ShapeDtypeStruct((1, width), F32),
        ],
        name="attention_backward",
    )(q, k, v, lse, g_att)


def attention_weights(segments, slots):
    rows, width = segments[0][0].shape
    part = width // slots

    def body(*refs):
        out_ref = refs[-1]
        groups = [refs[i : i + 6] for i in range(0, len(refs) - 1, 6)]
        for kind in range(4):
            total = None
            for refs_of in groups:
                left = refs_of[4] if kind == 3 else refs_of[kind]
                right = refs_of[5][...] if kind == 3 else refs_of[3][: left.shape[0], :]
                one = dot(left[...], right, 0, 0)
                total = one if total is None else total + one
            for s in range(slots):
                out_ref[s, kind * part : (kind + 1) * part, :] = total[s * part : (s + 1) * part].astype(BF16)

    return pl.pallas_call(
        body, out_shape=jax.ShapeDtypeStruct((slots, 4 * part, width), BF16), name="attention_weights"
    )(*(a for segment in segments for a in segment))


def local(text_in, start_memory, w_qkv, b_qv, w_o, w_up, b_up, w_down, norm_gains, biases, cot_text, cot_memory):
    text, cot_rows, cot_mem = text_in[0], cot_text[0], cot_memory[0]
    text_total, width = text.shape
    mem = start_memory.shape[0]
    seg = text_total // SEGMENTS
    rows = seg + mem
    keys = rows + mem
    padded = -(-keys // LANES) * LANES
    n_t, n_dp = lax.axis_size("tensor"), lax.axis_size("dp")
    head_part = w_qkv.shape[2]
    part = b_up.shape[0]
    t = lax.axis_index("tensor")

    small = jnp.concatenate([b_qv.reshape(-1), b_up])[None]
    for step in line_steps():
        small = jnp.concatenate([small, line_exchange(small, step)])
    small = small.astype(F32)
    q_bias = small[:, :head_part].reshape(1, -1)
    v_bias = small[:, head_part : 2 * head_part].reshape(1, -1)
    up_bias = small[:, None, 2 * head_part :]
    kinds = jnp.concatenate([w_qkv.transpose(0, 2, 1).reshape(-1, width), w_o])
    kinds = gather_chunks(kinds.reshape(n_dp, -1, width)).reshape(n_t, 4, head_part, width)
    q_w, k_w, v_w, o_w = (kinds[:, i].reshape(width, width) for i in range(4))
    up_full = gather_chunks(w_up.reshape(n_dp, -1, part)).reshape(n_t, width, part)
    down_full = gather_chunks(w_down.reshape(n_dp, -1, width)).reshape(n_t, part, width)

    read = start_memory
    kept, pieces = [], []
    for s in range(SEGMENTS):
        x = jnp.concatenate([text[s * seg : (s + 1) * seg], start_memory, read, jnp.zeros((padded - keys, width), BF16)])
        q = (dot(x[:rows], q_w, 1, 1) + q_bias).astype(BF16)
        k = dot(x, k_w, 1, 1).astype(BF16)
        v = (dot(x, v_w, 1, 1) + v_bias).astype(BF16)
        att, lse = attention_forward(q, k, v, keys)
        n1, r1 = norm_stats(x[:rows].astype(F32) + dot(att, o_w, 1, 0) + biases[0])
        middle = n1 * norm_gains[0] + biases[1]
        low = middle.astype(BF16)
        act, slope, ffn = ffn_forward(low, up_full, up_bias, down_full)
        n2, r2 = norm_stats(middle + ffn + biases[2])
        result = (n2 * norm_gains[1] + biases[3]).astype(BF16)
        pieces.append(result[:seg])
        read = result[seg:]
        kept.append((x, q, k, v, lse, att, n1, r1, low, act, slope, n2, r2))

    d_gain, d_bias, d_bqv, d_bup, segments = [], [], [], [], []
    d_mem = jnp.zeros((mem, width), F32)
    carry = cot_mem.astype(F32)
    d_text = [None] * SEGMENTS
    earlier = ()
    for s in reversed(range(SEGMENTS)):
        x, q, k, v, lse, att, n1, r1, low, act, slope, n2, r2 = kept[s]
        g_res = jnp.concatenate([cot_rows[s * seg : (s + 1) * seg].astype(F32), carry])
        g_pre2 = norm_backward(g_res, n2, r2, norm_gains[1])
        g_mid, g_bup, d_up, d_down = ffn_backward(g_pre2.astype(BF16), low, act, slope, up_full, down_full, earlier)
        earlier = (d_up, d_down)
        g_mid = g_mid + g_pre2
        g_pre1 = norm_backward(g_mid, n1, r1, norm_gains[0])
        g_attn = g_pre1.astype(BF16)
        if s == 0:
            packed = [pack(d.reshape(n_t, n_dp, -1, d.shape[-1])) for d in earlier]
            g_attn, packed = lax.optimization_barrier((g_attn, packed))
        g_att = dot(g_attn, o_w, 1, 1).astype(BF16)
        if s == 0:
            totals = [reduce_core(p) for p in packed]
            g_att, totals = lax.optimization_barrier((g_att, totals))
        g_q, g_k, g_v, sum_q, sum_v = attention_backward(q, k, v, lse, g_att, keys)
        segments.append((g_q, g_k, g_v, x, att, g_attn))
        if s == 0:
            totals = [reduce_outer(p) for p in totals]
            segments, totals = lax.optimization_barrier((segments, totals))
            g_q, g_k, g_v = segments[-1][:3]
        g_x = dot(g_k, k_w, 1, 0) + dot(g_v, v_w, 1, 0)
        top = g_x[:rows] + dot(g_q, q_w, 1, 0) + g_pre1
        d_text[s] = top[:seg]
        d_mem = d_mem + top[seg:]
        if s > 0:
            carry = g_x[rows:keys]
        else:
            d_mem = d_mem + g_x[rows:keys]
        d_bqv.append(jnp.concatenate([sum_q, sum_v]))
        d_bup.append(g_bup[:, 0])
        d_gain.append(jnp.stack([jnp.sum(g_mid * n1, 0), jnp.sum(g_res * n2, 0)]))
        d_bias.append(jnp.stack([jnp.sum(g, 0) for g in (g_pre1, g_mid, g_pre2, g_res)]))

    d_kinds = attention_weights(segments, n_t)
    kinds = reduce_line(reduce_outer(reduce_core(pack(d_kinds.reshape(n_t, n_dp, -1, width)))))
    g_up, g_down = (spread(reduce_line(total)).reshape(-1, total.shape[-1]) for total in totals)
    g_kinds = spread(kinds).reshape(4, head_part, width)
    g_qkv, g_out = g_kinds[:3].transpose(0, 2, 1), g_kinds[3]

    total = lambda parts: parts[0] + parts[1]
    small = total(d_bqv).reshape(2, n_t, head_part).transpose(1, 0, 2).reshape(n_t, -1)
    small = jnp.concatenate([small, total(d_bup)], 1)
    pick = (jnp.arange(n_t)[:, None] == t ^ slot_masks()[0]).astype(F32)
    small = jnp.dot(pick, small, precision=lax.Precision.HIGHEST)
    vectors = jnp.concatenate([total(d_gain), total(d_bias), d_mem])
    count = vectors.size
    vectors = sum_small(jnp.concatenate([vectors.reshape(-1), small.reshape(-1)]).reshape(-1, LANES)).reshape(-1)
    own = lax.dynamic_slice_in_dim(vectors[count:].reshape(n_t, -1), t, 1, 0)[0]
    vectors = vectors[:count].reshape(-1, width)

    return (
        jnp.concatenate(pieces)[None],
        read[None],
        jnp.concatenate(d_text)[None],
        vectors[6 : 6 + mem],
        g_qkv,
        own[: 2 * head_part].reshape(2, head_part),
        g_out,
        g_up,
        own[2 * head_part :],
        g_down,
        vectors[:2],
        vectors[2:6],
    )


def solution(mesh):
    own = P(("dp", "tensor"), None, None)
    return jax.shard_map(
        local,
        mesh=mesh,
        in_specs=(
            own, P(), P(None, None, "tensor"), P(None, "tensor"), P("tensor", None), P(None, "tensor"),
            P("tensor"), P("tensor", None), P(), P(), own, own,
        ),
        out_specs=(
            own, own, own, P(), P(None, None, "tensor"), P(None, "tensor"), P("tensor", None),
            P(None, "tensor"), P("tensor"), P("tensor", None), P(), P(),
        ),
        check_vma=False,
    )
```

```python
import math

import jax
import jax.numpy as jnp
from jax import lax
from jax.experimental import pallas as pl
from jax.experimental.pallas import tpu as pltpu
from jax.sharding import PartitionSpec as P

HEAD_DIM = 64
SEGMENTS = 2
EPSILON = 1e-06
LANES = 128
F32 = jnp.float32
BF16 = jnp.bfloat16


def dot(a, b, ca, cb):
    return lax.dot_general(a, b, (((ca,), (cb,)), ((), ())), preferred_element_type=F32)


def norm_stats(value):
    centred = value - jnp.mean(value, -1, keepdims=True)
    rstd = lax.rsqrt(jnp.mean(centred * centred, -1, keepdims=True) + EPSILON)
    return centred * rstd, rstd


def norm_backward(grad_out, normed, rstd, gain):
    scaled = grad_out * gain
    first = jnp.mean(scaled, -1, keepdims=True)
    second = jnp.mean(scaled * normed, -1, keepdims=True)
    return rstd * (scaled - first - normed * second)


def log2(n):
    return n.bit_length() - 1


def outer_mask(core, step):
    outer = log2(lax.axis_size("dp")) - 1
    return 2 << (step if core == 0 else outer - 1 - step)


def outer_exchange(value, step):
    pairs = [(i, i ^ outer_mask(i & 1, step)) for i in range(lax.axis_size("dp"))]
    return lax.ppermute(value, "dp", pairs)


def core_exchange(value):
    return lax.ppermute(value, "dp", [(i, i ^ 1) for i in range(lax.axis_size("dp"))])


def line_exchange(value, step):
    n = lax.axis_size("tensor")
    pairs = []
    for i in range(lax.axis_size("dp")):
        mask = 1 << (step if i & 1 == 0 else log2(n) - 1 - step)
        pairs += [(i * n + t, i * n + (t ^ mask)) for t in range(n)]
    return lax.ppermute(value, ("dp", "tensor"), pairs)


def outer_steps():
    return range(log2(lax.axis_size("dp")) - 1)


def line_steps():
    return range(log2(lax.axis_size("tensor")))


def arrival_sources():
    half = lax.axis_size("dp") // 2
    tables = [
        jnp.array([sum(outer_mask(core, i) for i in outer_steps() if j >> i & 1) for j in range(half)], jnp.int32)
        for core in (0, 1)
    ]
    d = lax.axis_index("dp")
    core = d % 2
    mine = jnp.where(core == 0, tables[0], tables[1])
    theirs = jnp.where(core == 0, tables[1], tables[0])
    return jnp.concatenate([d ^ mine, d ^ 1 ^ theirs])


def slot_masks():
    n = lax.axis_size("tensor")
    orders = []
    for flip in (False, True):
        places = [log2(n) - 1 - i if flip else i for i in line_steps()]
        orders.append(jnp.array([sum(1 << places[i] for i in line_steps() if s >> i & 1) for s in range(n)], jnp.int32))
    core = lax.axis_index("dp") % 2
    return jnp.where(core == 0, orders[0], orders[1]), jnp.where(core == 0, orders[1], orders[0])


def other_half_slots():
    n = lax.axis_size("tensor")
    return [sum(1 << (log2(n) - 1 - i) for i in line_steps() if s >> i & 1) for s in range(n)]


def cost(flops, transcendentals, operands, shapes):
    moved = sum(a.size * a.dtype.itemsize for a in list(operands) + list(shapes))
    return pl.CostEstimate(flops=flops, transcendentals=transcendentals, bytes_accessed=moved)


def moved_call(body, table, grid, ins, outs, operands, name, scratch=(), flops=0, transcendentals=0):
    shapes = [shape for _, shape in outs]
    return pl.pallas_call(
        body,
        grid_spec=pltpu.PrefetchScalarGridSpec(
            num_scalar_prefetch=1,
            grid=grid,
            in_specs=[pl.BlockSpec(*spec) for spec in ins],
            out_specs=[pl.BlockSpec(*spec) for spec, _ in outs],
            scratch_shapes=list(scratch),
        ),
        out_shape=shapes,
        cost_estimate=cost(flops, transcendentals, operands, shapes),
        name=name,
    )(table, *operands)


def aligned(rows):
    return rows % 16 == 0


def place_table():
    return jnp.concatenate([arrival_sources(), jnp.array([max(s - 1, 0) for s in other_half_slots()], jnp.int32)])


def pack_table():
    return jnp.concatenate([arrival_sources(), jnp.array(other_half_slots(), jnp.int32)])


def raw_specs(chunks, own):
    n, rows, width = chunks.shape
    block = (n // 2, 1, rows, width)
    return [
        ((n, rows, width), lambda s, table: (0, 0, 0)),
        (block, lambda s, table: (0, jnp.maximum(s - 1, 0), 0, 0)),
        (block, lambda s, table: (0, table[n + s], 0, 0)),
    ]


def settle(table_ref, chunks_ref, own_ref, received_ref, out):
    half = own_ref.shape[0]

    @pl.when(pl.program_id(0) == 0)
    def _():
        out[...] = chunks_ref[...]

    @pl.when(pl.program_id(0) > 0)
    def _():
        for p in range(half):
            out[table_ref[p]] = own_ref[p, 0]
            out[table_ref[half + p]] = received_ref[p, 0]


def packed_outs(slots, n, rows, width):
    shape = jax.ShapeDtypeStruct((n // 2, slots, rows, width), BF16)
    block = (n // 2, 1, rows, width)
    return [
        ((block, lambda s, table: (0, s, 0, 0)), shape),
        ((block, lambda s, table: (0, table[n + s], 0, 0)), shape),
    ]


def place(chunks, own, received):
    others = own.shape[1]
    swap = other_half_slots()
    received = jnp.stack([received[:, swap[s] - 1] for s in range(1, others + 1)], 1)
    moved = jnp.concatenate([own, received])[jnp.argsort(arrival_sources())]
    return jnp.concatenate([chunks[None], moved.transpose(1, 0, 2, 3)])


def pack(total):
    half = total.shape[1] // 2
    moved = total.transpose(1, 0, 2, 3)[arrival_sources()]
    return moved[:half], jnp.stack([moved[half:, s] for s in other_half_slots()], 1)


def place_kinds(chunks, own, received):
    n, rows, width = chunks.shape
    slots = own.shape[1] + 1
    part = n * rows // 4
    if not (aligned(rows) and aligned(part)):
        full = place(chunks, own, received).reshape(slots, 4, part, width)
        return [full[:, i].reshape(-1, width) for i in range(4)]

    def body(table_ref, chunks_ref, own_ref, received_ref, *refs):
        settle(table_ref, chunks_ref, own_ref, received_ref, refs[-1])
        full = refs[-1][...].reshape(n * rows, width)
        for i in range(4):
            refs[i][...] = full[i * part : (i + 1) * part]

    out = (((part, width), lambda s, table: (s, 0)), jax.ShapeDtypeStruct((slots * part, width), BF16))
    return moved_call(
        body, place_table(), (slots,), raw_specs(chunks, own), [out] * 4, (chunks, own, received), "place_kinds",
        [pltpu.VMEM((n, rows, width), BF16)],
    )


def finish(own, received):
    half, rows, width = own.shape
    source = arrival_sources()
    if rows % 16:
        return jnp.concatenate([own, received])[jnp.argsort(source)].astype(F32)

    def body(table_ref, own_ref, received_ref, out_ref):
        for p in range(half):
            out_ref[table_ref[p]] = own_ref[p].astype(F32)
            out_ref[table_ref[half + p]] = received_ref[p].astype(F32)

    whole = ((half, rows, width), lambda i, table: (0, 0, 0))
    out = ((2 * half, rows, width), lambda i, table: (0, 0, 0))
    return moved_call(
        body, source, (1,), [whole, whole], [(out, jax.ShapeDtypeStruct(out[0], F32))], (own, received), "finish"
    )[0]


def gather_chunks(chunks, extra=None):
    rows = chunks.shape[1]
    slots = lax.dynamic_index_in_dim(chunks, lax.axis_index("dp"), 0)
    if extra is not None:
        slots = jnp.concatenate([slots, extra[None]], 1)
    for step in line_steps():
        slots = jnp.concatenate([slots, line_exchange(slots, step)])
    rest = slots[None, 1:, :rows]
    for step in outer_steps():
        rest = jnp.concatenate([rest, outer_exchange(rest, step)])
    return (chunks, rest, core_exchange(rest)), slots[:, rows:]


def plus(a, b):
    return (a.astype(F32) + b.astype(F32)).astype(BF16)


def reduce_core(packed):
    return plus(packed[0], core_exchange(packed[1]))


def reduce_outer(total):
    for step in reversed(outer_steps()):
        half = total.shape[0] // 2
        total = plus(total[:half], outer_exchange(total[half:], step))
    return total[0]


def reduce_line(total):
    for step in reversed(line_steps()):
        half = total.shape[0] // 2
        total = plus(total[:half], line_exchange(total[half:], step))
    return total


def spread(total):
    for step in outer_steps():
        total = jnp.concatenate([total, outer_exchange(total, step)])
    return total, core_exchange(total)


def sum_small(value):
    for axis in ("dp", "tensor"):
        bit = 1
        while bit < lax.axis_size(axis):
            value = value + lax.ppermute(value, axis, [(i, i ^ bit) for i in range(lax.axis_size(axis))])
            bit *= 2
    return value


def ffn_cost(rows, hidden, width, products):
    return 2 * rows * hidden * width * products


def ffn_slot(low_ref, up, bias_ref, down, act_ref, slope_ref, out_ref):
    @pl.when(pl.program_id(0) == 0)
    def _():
        out_ref[...] = jnp.zeros_like(out_ref)

    step = low_ref.shape[0] // 4
    for i in range(4):
        at = slice(i * step, (i + 1) * step)
        hidden = dot(low_ref[at, :], up, 1, 0) + bias_ref[0]
        cdf = 0.5 * (1.0 + lax.erf(hidden * math.sqrt(0.5)))
        act = (hidden * cdf).astype(BF16)
        act_ref[at, :] = act
        pdf = jnp.exp(hidden * hidden * -0.5) * (1.0 / math.sqrt(2.0 * math.pi))
        slope_ref[at, :] = (cdf + hidden * pdf).astype(BF16)
        out_ref[at, :] += dot(act, down, 1, 0)


def ffn_specs(rows, width, slots, part):
    whole = ((rows, width), lambda s, table: (0, 0))
    units = ((rows, part), lambda s, table: (0, s))
    shape = jax.ShapeDtypeStruct((rows, slots * part), BF16)
    return whole, units, [(units, shape), (units, shape), (whole, jax.ShapeDtypeStruct((rows, width), F32))]


def ffn_first(low, up_raw, up_bias, down_raw):
    rows, width = low.shape
    slots, part = up_bias.shape[0], up_bias.shape[2]
    if not all(aligned(raw[0].shape[1]) for raw in (up_raw, down_raw)):
        up, down = place(*up_raw).reshape(slots, width, part), place(*down_raw).reshape(slots, part, width)
        return (*ffn_forward(low, up, up_bias, down), up, down)

    def body(table_ref, low_ref, bias_ref, *refs):
        up_refs, down_refs, (act_ref, slope_ref, out_ref, up_ref, down_ref) = refs[:3], refs[3:6], refs[6:]
        settle(table_ref, *up_refs, up_ref.at[0])
        settle(table_ref, *down_refs, down_ref.at[0])
        up, down = up_ref[0].reshape(width, part), down_ref[0].reshape(part, width)
        ffn_slot(low_ref, up, bias_ref, down, act_ref, slope_ref, out_ref)

    whole, _, outs = ffn_specs(rows, width, slots, part)
    for raw in (up_raw, down_raw):
        shape = raw[0].shape
        outs.append((((1,) + shape, lambda s, table: (s, 0, 0, 0)), jax.ShapeDtypeStruct((slots,) + shape, BF16)))
    act, slope, out, up, down = moved_call(
        body, place_table(), (slots,),
        [whole, ((1, 1, part), lambda s, table: (s, 0, 0))] + raw_specs(*up_raw[:2]) + raw_specs(*down_raw[:2]),
        outs, (low, up_bias, *up_raw, *down_raw), "ffn_first",
        flops=ffn_cost(rows, slots * part, width, 2), transcendentals=rows * slots * part * 2,
    )
    return act, slope, out, up.reshape(slots, width, part), down.reshape(slots, part, width)


def ffn_forward(low, up, up_bias, down):
    rows, width = low.shape
    slots, part = up_bias.shape[0], up_bias.shape[2]

    def body(table_ref, low_ref, up_ref, bias_ref, down_ref, act_ref, slope_ref, out_ref):
        ffn_slot(low_ref, up_ref[0], bias_ref, down_ref[0], act_ref, slope_ref, out_ref)

    whole, _, outs = ffn_specs(rows, width, slots, part)
    slot = lambda s, table: (s, 0, 0)
    return moved_call(
        body, jnp.zeros((1,), jnp.int32), (slots,),
        [whole, ((1, width, part), slot), ((1, 1, part), slot), ((1, part, width), slot)],
        outs, (low, up, up_bias, down), "ffn_forward",
        flops=ffn_cost(rows, slots * part, width, 2), transcendentals=rows * slots * part * 2,
    )


def ffn_backward(g_ffn, low, act, slope, up, down, earlier):
    rows, width = low.shape
    slots, part = up.shape[0], up.shape[2]
    n = lax.axis_size("dp")
    fused = bool(earlier) and aligned(width // n) and aligned(part // n)
    half = n // 2

    def body(table_ref, g_ref, low_ref, act_ref, slope_ref, up_ref, down_ref, *refs):
        olds, refs = refs[: len(earlier)], refs[len(earlier) :]
        mid_ref, bias_ref, outs = refs[0], refs[1], refs[2:]
        g = g_ref[...]
        hid = (dot(g, down_ref[0], 1, 1) * slope_ref[...].astype(F32)).astype(BF16)
        bias_ref[0] = jnp.sum(hid.astype(F32), 0, keepdims=True)
        back = dot(hid, up_ref[0], 1, 1)

        @pl.when(pl.program_id(0) == 0)
        def _():
            mid_ref[...] = back

        @pl.when(pl.program_id(0) > 0)
        def _():
            mid_ref[...] += back

        for i, (left, right) in enumerate(((low_ref[...], hid), (act_ref[...], g))):
            total = dot(left, right, 0, 0)
            if olds:
                total = total + olds[i][0]
            if fused:
                keep_ref, send_ref, scratch = outs[2 * i], outs[2 * i + 1], outs[4 + i]
                scratch[...] = total.astype(BF16).reshape(scratch.shape)
                for p in range(half):
                    keep_ref[p, 0] = scratch[table_ref[p]]
                    send_ref[p, 0] = scratch[table_ref[half + p]]
            else:
                outs[i][0] = total.astype(outs[i].dtype)

    whole, units, _ = ffn_specs(rows, width, slots, part)
    slot = lambda s, table: (s, 0, 0)
    shapes = [(width, part), (part, width)]
    weights = [((1,) + shape, slot) for shape in shapes]
    outs = [
        (whole, jax.ShapeDtypeStruct((rows, width), F32)),
        (((1, 1, part), slot), jax.ShapeDtypeStruct((slots, 1, part), F32)),
    ]
    scratch = []
    for shape, spec in zip(shapes, weights):
        if fused:
            chunk = (n, shape[0] // n, shape[1])
            outs += packed_outs(slots, *chunk)
            scratch.append(pltpu.VMEM(chunk, BF16))
        else:
            outs.append((spec, jax.ShapeDtypeStruct((slots,) + shape, BF16 if earlier else F32)))
    got = moved_call(
        body, pack_table(), (slots,),
        [whole, whole, units, units] + weights + (weights if earlier else []),
        outs, (g_ffn, low, act, slope, up, down, *earlier), "ffn_backward", scratch,
        flops=ffn_cost(rows, slots * part, width, 4),
    )
    if fused:
        return got[0], got[1], got[2:4], got[4:6]
    if earlier:
        return got[0], got[1], *(pack(d.reshape(slots, n, -1, d.shape[-1])) for d in got[2:])
    return got


def lane_masks(rows):
    lane = lax.broadcasted_iota(jnp.int32, (rows, LANES), 1)
    return [(lane >= h * HEAD_DIM) & (lane < (h + 1) * HEAD_DIM) for h in range(LANES // HEAD_DIM)]


def only(mask, value):
    return jnp.where(mask, value, jnp.zeros_like(value))


def attention_forward(q, k, v, keys):
    rows, width = q.shape
    padded = k.shape[0]
    scale = 1.0 / math.sqrt(HEAD_DIM)

    def body(q_ref, k_ref, v_ref, out_ref, lse_ref):
        q = q_ref[...] * jnp.asarray(scale, BF16)
        k, v = k_ref[...], v_ref[...]
        live = lax.broadcasted_iota(jnp.int32, (1, padded), 1) < keys
        out = jnp.zeros((rows, LANES), F32)
        lses = jnp.zeros((rows, LANES), F32)
        for mine, theirs in zip(lane_masks(rows), lane_masks(padded)):
            scores = jnp.where(live, dot(only(mine, q), k, 1, 1), -jnp.inf)
            top = jnp.max(scores, -1, keepdims=True)
            weights = jnp.exp(scores - top)
            total = jnp.sum(weights, -1, keepdims=True)
            probs = (weights * (1.0 / total)).astype(BF16)
            out = out + dot(probs, only(theirs, v), 1, 0)
            lses = jnp.where(mine, top + jnp.log(total), lses)
        out_ref[...] = out.astype(BF16)
        lse_ref[...] = lses

    q_spec = pl.BlockSpec((rows, LANES), lambda h: (0, h))
    k_spec = pl.BlockSpec((padded, LANES), lambda h: (0, h))
    return pl.pallas_call(
        body,
        grid=(width // LANES,),
        in_specs=[q_spec, k_spec, k_spec],
        out_specs=[q_spec, q_spec],
        out_shape=[jax.ShapeDtypeStruct((rows, width), BF16), jax.ShapeDtypeStruct((rows, width), F32)],
        cost_estimate=cost(8 * rows * padded * width, rows * padded * width // HEAD_DIM, (q, k, v, q, q), ()),
        name="attention_forward",
    )(q, k, v)


def attention_backward(q, k, v, lse, g_att, keys):
    rows, width = q.shape
    padded = k.shape[0]
    scale = 1.0 / math.sqrt(HEAD_DIM)

    def body(q_ref, k_ref, v_ref, lse_ref, g_ref, gq_ref, gk_ref, gv_ref, sum_q_ref, sum_v_ref):
        q, g = q_ref[...] * jnp.asarray(scale, BF16), g_ref[...]
        k, v = k_ref[...], v_ref[...]
        live = lax.broadcasted_iota(jnp.int32, (1, padded), 1) < keys
        gq = jnp.zeros((rows, LANES), F32)
        gk = jnp.zeros((padded, LANES), F32)
        gv = jnp.zeros((padded, LANES), F32)
        for h, (mine, theirs) in enumerate(zip(lane_masks(rows), lane_masks(padded))):
            q_h, g_h = only(mine, q), only(mine, g)
            scores = dot(q_h, k, 1, 1)
            full = jnp.where(live, jnp.exp(scores - lse_ref[:, h * HEAD_DIM : h * HEAD_DIM + 1]), 0.0)
            g_probs = dot(g_h, v, 1, 1)
            inner = jnp.sum(g_probs * full, -1, keepdims=True)
            g_scores = (full * (g_probs - inner)).astype(BF16)
            gq = gq + dot(g_scores, only(theirs, k), 1, 0)
            gk = gk + dot(g_scores, q_h, 0, 0)
            gv = gv + dot(full.astype(BF16), g_h, 0, 0)
        gq = (gq * scale).astype(BF16)
        gv = gv.astype(BF16)
        gq_ref[...] = gq
        gk_ref[...] = gk.astype(BF16)
        gv_ref[...] = gv
        sum_q_ref[...] = jnp.sum(gq.astype(F32), 0, keepdims=True)
        sum_v_ref[...] = jnp.sum(gv.astype(F32), 0, keepdims=True)

    q_spec = pl.BlockSpec((rows, LANES), lambda h: (0, h))
    k_spec = pl.BlockSpec((padded, LANES), lambda h: (0, h))
    sum_spec = pl.BlockSpec((1, LANES), lambda h: (0, h))
    return pl.pallas_call(
        body,
        grid=(width // LANES,),
        in_specs=[q_spec, k_spec, k_spec, q_spec, q_spec],
        out_specs=[q_spec, k_spec, k_spec, sum_spec, sum_spec],
        out_shape=[
            jax.ShapeDtypeStruct((rows, width), BF16),
            jax.ShapeDtypeStruct((padded, width), BF16),
            jax.ShapeDtypeStruct((padded, width), BF16),
            jax.ShapeDtypeStruct((1, width), F32),
            jax.ShapeDtypeStruct((1, width), F32),
        ],
        cost_estimate=cost(20 * rows * padded * width, rows * padded * width // HEAD_DIM, (q, k, v, lse, g_att, q, k, v), ()),
        name="attention_backward",
    )(q, k, v, lse, g_att)


def attention_weights(segments, slots):
    width = segments[0][0].shape[1]
    part = width // slots
    n = lax.axis_size("dp")
    rows = 4 * part // n
    half = n // 2
    fused = aligned(rows)
    swap = other_half_slots()
    operands = [a for segment in segments for a in segment]

    def body(table_ref, *refs):
        out_refs = refs[len(operands) :]
        full = out_refs[-1]
        groups = [refs[i : i + 6] for i in range(0, len(operands), 6)]
        for kind in range(4):
            total = None
            for refs_of in groups:
                left = refs_of[4] if kind == 3 else refs_of[kind]
                right = refs_of[5][...] if kind == 3 else refs_of[3][: left.shape[0], :]
                one = dot(left[...], right, 0, 0)
                total = one if total is None else total + one
            for s in range(slots):
                full[s, kind * part : (kind + 1) * part, :] = total[s * part : (s + 1) * part].astype(BF16)
        if fused:
            for p in range(half):
                mine = pl.ds(pl.multiple_of(table_ref[p] * rows, 16), rows)
                theirs = pl.ds(pl.multiple_of(table_ref[half + p] * rows, 16), rows)
                for s in range(slots):
                    out_refs[0][p, s] = full[s, mine, :]
                    out_refs[1][p, s] = full[swap[s], theirs, :]

    everything = lambda a: (a.shape, lambda i, table: (0,) * len(a.shape))
    packed = jax.ShapeDtypeStruct((half, slots, rows, width), BF16)
    whole = jax.ShapeDtypeStruct((slots, 4 * part, width), BF16)
    shapes = [packed, packed] if fused else [whole]
    got = moved_call(
        body, arrival_sources(), (1,), [everything(a) for a in operands], [(everything(a), a) for a in shapes], operands,
        "attention_weights", [pltpu.VMEM(whole.shape, BF16)] if fused else [],
        flops=sum(2 * a.size * width for a in operands) * 2 // 3,
    )
    return got if fused else pack(got[0].reshape(slots, n, rows, width))


def finish_kinds(own, received, head_part):
    half, rows, width = own.shape
    n = 2 * half
    if not aligned(rows):
        full = finish(own, received).reshape(4, head_part, width)
        return full[:3].transpose(0, 2, 1), full[3]

    def body(table_ref, own_ref, received_ref, qkv_ref, out_ref, scratch):
        for p in range(half):
            scratch[table_ref[p]] = own_ref[p].astype(F32)
            scratch[table_ref[half + p]] = received_ref[p].astype(F32)
        full = scratch[...].reshape(n * rows, width)
        for i in range(3):
            qkv_ref[i] = full[i * head_part : (i + 1) * head_part].T
        out_ref[...] = full[3 * head_part :]

    whole = ((half, rows, width), lambda i, table: (0, 0, 0))
    shapes = [(3, width, head_part), (head_part, width)]
    outs = [
        ((shape, lambda i, table, rank=len(shape): (0,) * rank), jax.ShapeDtypeStruct(shape, F32)) for shape in shapes
    ]
    return moved_call(
        body, arrival_sources(), (1,), [whole, whole], outs, (own, received), "finish_kinds",
        [pltpu.VMEM((n, rows, width), F32)],
    )


def local(text_in, start_memory, w_qkv, b_qv, w_o, w_up, b_up, w_down, norm_gains, biases, cot_text, cot_memory):
    text, cot_rows, cot_mem = text_in[0], cot_text[0], cot_memory[0]
    text_total, width = text.shape
    mem = start_memory.shape[0]
    seg = text_total // SEGMENTS
    rows = seg + mem
    keys = rows + mem
    padded = -(-keys // LANES) * LANES
    n_t, n_dp = lax.axis_size("tensor"), lax.axis_size("dp")
    head_part = w_qkv.shape[2]
    part = b_up.shape[0]
    t = lax.axis_index("tensor")

    small = jnp.concatenate([b_qv.reshape(-1), b_up])
    small = jnp.pad(small, (0, 8 * width - small.shape[0])).reshape(8, width)
    kinds = jnp.concatenate([w_qkv.transpose(0, 2, 1).reshape(-1, width), w_o])
    kinds, small = gather_chunks(kinds.reshape(n_dp, -1, width), small)
    small = small.reshape(n_t, -1).astype(F32)
    q_bias = small[:, :head_part].reshape(1, -1)
    v_bias = small[:, head_part : 2 * head_part].reshape(1, -1)
    up_bias = small[:, None, 2 * head_part : 2 * head_part + part]
    up_raw = gather_chunks(w_up.reshape(n_dp, -1, part))[0]
    down_raw = gather_chunks(w_down.reshape(n_dp, -1, width))[0]
    q_w, k_w, v_w, o_w = place_kinds(*kinds)

    read = start_memory
    kept, pieces = [], []
    for s in range(SEGMENTS):
        x = jnp.concatenate([text[s * seg : (s + 1) * seg], start_memory, read, jnp.zeros((padded - keys, width), BF16)])
        q = (dot(x[:rows], q_w, 1, 1) + q_bias).astype(BF16)
        k = dot(x, k_w, 1, 1).astype(BF16)
        v = (dot(x, v_w, 1, 1) + v_bias).astype(BF16)
        att, lse = attention_forward(q, k, v, keys)
        n1, r1 = norm_stats(x[:rows].astype(F32) + dot(att, o_w, 1, 0) + biases[0])
        middle = n1 * norm_gains[0] + biases[1]
        low = middle.astype(BF16)
        if s == 0:
            act, slope, ffn, up_full, down_full = ffn_first(low, up_raw, up_bias, down_raw)
        else:
            act, slope, ffn = ffn_forward(low, up_full, up_bias, down_full)
        n2, r2 = norm_stats(middle + ffn + biases[2])
        result = (n2 * norm_gains[1] + biases[3]).astype(BF16)
        pieces.append(result[:seg])
        read = result[seg:]
        kept.append((x, q, k, v, lse, att, n1, r1, low, act, slope, n2, r2))

    d_gain, d_bias, d_bqv, d_bup, segments = [], [], [], [], []
    d_mem = jnp.zeros((mem, width), F32)
    carry = cot_mem.astype(F32)
    d_text = [None] * SEGMENTS
    earlier = ()
    for s in reversed(range(SEGMENTS)):
        x, q, k, v, lse, att, n1, r1, low, act, slope, n2, r2 = kept[s]
        g_res = jnp.concatenate([cot_rows[s * seg : (s + 1) * seg].astype(F32), carry])
        g_pre2 = norm_backward(g_res, n2, r2, norm_gains[1])
        g_mid, g_bup, d_up, d_down = ffn_backward(g_pre2.astype(BF16), low, act, slope, up_full, down_full, earlier)
        earlier = (d_up, d_down)
        g_mid = g_mid + g_pre2
        g_pre1 = norm_backward(g_mid, n1, r1, norm_gains[0])
        g_attn = g_pre1.astype(BF16)
        if s == 0:
            totals = [reduce_core(p) for p in earlier]
        g_att = dot(g_attn, o_w, 1, 1).astype(BF16)
        g_q, g_k, g_v, sum_q, sum_v = attention_backward(q, k, v, lse, g_att, keys)
        segments.append((g_q, g_k, g_v, x, att, g_attn))
        if s == 0:
            segments, totals = lax.optimization_barrier((segments, totals))
            g_q, g_k, g_v = segments[-1][:3]
            totals = [reduce_outer(p) for p in totals]
        g_x = dot(g_k, k_w, 1, 0) + dot(g_v, v_w, 1, 0)
        top = g_x[:rows] + dot(g_q, q_w, 1, 0) + g_pre1
        d_text[s] = top[:seg]
        d_mem = d_mem + top[seg:]
        if s > 0:
            carry = g_x[rows:keys]
        else:
            d_mem = d_mem + g_x[rows:keys]
        d_bqv.append(jnp.concatenate([sum_q, sum_v]))
        d_bup.append(g_bup[:, 0])
        d_gain.append(jnp.stack([jnp.sum(g_mid * n1, 0), jnp.sum(g_res * n2, 0)]))
        d_bias.append(jnp.stack([jnp.sum(g, 0) for g in (g_pre1, g_mid, g_pre2, g_res)]))

    kinds = reduce_core(attention_weights(segments, n_t))
    kinds = reduce_outer(kinds)
    g_up, g_down = (finish(*spread(reduce_line(total))).reshape(-1, total.shape[-1]) for total in totals)
    kinds, g_up, g_down = lax.optimization_barrier((reduce_line(kinds), g_up, g_down))
    g_qkv, g_out = finish_kinds(*spread(kinds), head_part)

    total = lambda parts: parts[0] + parts[1]
    pick = (jnp.arange(n_t)[:, None] == t ^ slot_masks()[0]).astype(F32)
    exact = lambda value: jnp.dot(pick, value, precision=lax.Precision.HIGHEST)
    by_index = total(d_bqv).reshape(2, n_t, head_part).transpose(1, 0, 2).reshape(n_t, -1)
    by_index = exact(by_index).reshape(n_t, 2, head_part).transpose(1, 0, 2).reshape(2, width)
    vectors = jnp.concatenate([total(d_gain), total(d_bias), d_mem, by_index, exact(total(d_bup)).reshape(-1, width)])
    vectors = sum_small(vectors)
    g_bqv = lax.dynamic_slice_in_dim(vectors[6 + mem : 8 + mem], t * head_part, head_part, 1)
    g_bup = lax.dynamic_slice_in_dim(vectors[8 + mem :].reshape(n_t, -1), t, 1, 0)[0]

    return (
        jnp.concatenate(pieces)[None],
        read[None],
        jnp.concatenate(d_text)[None],
        vectors[6 : 6 + mem],
        g_qkv,
        g_bqv,
        g_out,
        g_up,
        g_bup,
        g_down,
        vectors[:2],
        vectors[2:6],
    )


def solution(mesh):
    own = P(("dp", "tensor"), None, None)
    return jax.shard_map(
        local,
        mesh=mesh,
        in_specs=(
            own, P(), P(None, None, "tensor"), P(None, "tensor"), P("tensor", None), P(None, "tensor"),
            P("tensor"), P("tensor", None), P(), P(), own, own,
        ),
        out_specs=(
            own, own, own, P(), P(None, None, "tensor"), P(None, "tensor"), P("tensor", None),
            P(None, "tensor"), P("tensor"), P("tensor", None), P(), P(),
        ),
        check_vma=False,
    )
```

```python
import math

import jax
import jax.numpy as jnp
from jax import lax
from jax.experimental import pallas as pl
from jax.experimental.pallas import tpu as pltpu
from jax.sharding import PartitionSpec as P

HEAD_DIM = 64
SEGMENTS = 2
EPSILON = 1e-06
LANES = 128
F32 = jnp.float32
BF16 = jnp.bfloat16


def dot(a, b, ca, cb):
    return lax.dot_general(a, b, (((ca,), (cb,)), ((), ())), preferred_element_type=F32)


def norm_stats(value):
    centred = value - jnp.mean(value, -1, keepdims=True)
    rstd = lax.rsqrt(jnp.mean(centred * centred, -1, keepdims=True) + EPSILON)
    return centred * rstd, rstd


def norm_backward(grad_out, normed, rstd, gain):
    scaled = grad_out * gain
    first = jnp.mean(scaled, -1, keepdims=True)
    second = jnp.mean(scaled * normed, -1, keepdims=True)
    return rstd * (scaled - first - normed * second)


def log2(n):
    return n.bit_length() - 1


def outer_mask(core, step):
    outer = log2(lax.axis_size("dp")) - 1
    return 2 << (step if core == 0 else outer - 1 - step)


def outer_exchange(value, step):
    pairs = [(i, i ^ outer_mask(i & 1, step)) for i in range(lax.axis_size("dp"))]
    return lax.ppermute(value, "dp", pairs)


def core_exchange(value):
    return lax.ppermute(value, "dp", [(i, i ^ 1) for i in range(lax.axis_size("dp"))])


def line_exchange(value, step):
    n = lax.axis_size("tensor")
    pairs = []
    for i in range(lax.axis_size("dp")):
        mask = 1 << (step if i & 1 == 0 else log2(n) - 1 - step)
        pairs += [(i * n + t, i * n + (t ^ mask)) for t in range(n)]
    return lax.ppermute(value, ("dp", "tensor"), pairs)


def outer_steps():
    return range(log2(lax.axis_size("dp")) - 1)


def line_steps():
    return range(log2(lax.axis_size("tensor")))


def arrival_sources():
    half = lax.axis_size("dp") // 2
    tables = [
        jnp.array([sum(outer_mask(core, i) for i in outer_steps() if j >> i & 1) for j in range(half)], jnp.int32)
        for core in (0, 1)
    ]
    d = lax.axis_index("dp")
    core = d % 2
    mine = jnp.where(core == 0, tables[0], tables[1])
    theirs = jnp.where(core == 0, tables[1], tables[0])
    return jnp.concatenate([d ^ mine, d ^ 1 ^ theirs])


def slot_masks():
    n = lax.axis_size("tensor")
    orders = []
    for flip in (False, True):
        places = [log2(n) - 1 - i if flip else i for i in line_steps()]
        orders.append(jnp.array([sum(1 << places[i] for i in line_steps() if s >> i & 1) for s in range(n)], jnp.int32))
    core = lax.axis_index("dp") % 2
    return jnp.where(core == 0, orders[0], orders[1]), jnp.where(core == 0, orders[1], orders[0])


def other_half_slots():
    n = lax.axis_size("tensor")
    return [sum(1 << (log2(n) - 1 - i) for i in line_steps() if s >> i & 1) for s in range(n)]


def cost(flops, transcendentals, operands, shapes):
    moved = sum(a.size * a.dtype.itemsize for a in list(operands) + list(shapes))
    return pl.CostEstimate(flops=flops, transcendentals=transcendentals, bytes_accessed=moved)


def moved_call(body, table, grid, ins, outs, operands, name, scratch=(), flops=0, transcendentals=0):
    shapes = [shape for _, shape in outs]
    return pl.pallas_call(
        body,
        grid_spec=pltpu.PrefetchScalarGridSpec(
            num_scalar_prefetch=1,
            grid=grid,
            in_specs=[pl.BlockSpec(*spec) for spec in ins],
            out_specs=[pl.BlockSpec(*spec) for spec, _ in outs],
            scratch_shapes=list(scratch),
        ),
        out_shape=shapes,
        cost_estimate=cost(flops, transcendentals, operands, shapes),
        name=name,
    )(table, *operands)


def aligned(rows):
    return rows % 16 == 0


def place_table():
    return jnp.concatenate([arrival_sources(), jnp.array([max(s - 1, 0) for s in other_half_slots()], jnp.int32)])


def pack_table():
    return jnp.concatenate([arrival_sources(), jnp.array(other_half_slots(), jnp.int32)])


def raw_specs(chunks, at=0):
    n, rows, width = chunks.shape
    block = (n // 2, 1, rows, width)
    return [
        ((n, rows, width), lambda s, table: (0, 0, 0)),
        (block, lambda s, table: (0, jnp.maximum(s - 1, 0), at, 0)),
        (block, lambda s, table: (0, table[n + s], at, 0)),
    ]


def settle(table_ref, chunks_ref, own_ref, received_ref, out):
    half = own_ref.shape[0]

    @pl.when(pl.program_id(0) == 0)
    def _():
        out[...] = chunks_ref[...]

    @pl.when(pl.program_id(0) > 0)
    def _():
        for p in range(half):
            out[table_ref[p]] = own_ref[p, 0]
            out[table_ref[half + p]] = received_ref[p, 0]


def packed_outs(slots, n, rows, width):
    shape = jax.ShapeDtypeStruct((n // 2, slots, rows, width), BF16)
    block = (n // 2, 1, rows, width)
    return [
        ((block, lambda s, table: (0, s, 0, 0)), shape),
        ((block, lambda s, table: (0, table[n + s], 0, 0)), shape),
    ]


def place(chunks, own, received):
    others = own.shape[1]
    swap = other_half_slots()
    received = jnp.stack([received[:, swap[s] - 1] for s in range(1, others + 1)], 1)
    moved = jnp.concatenate([own, received])[jnp.argsort(arrival_sources())]
    return jnp.concatenate([chunks[None], moved.transpose(1, 0, 2, 3)])


def pack(total):
    half = total.shape[1] // 2
    moved = total.transpose(1, 0, 2, 3)[arrival_sources()]
    return moved[:half], jnp.stack([moved[half:, s] for s in other_half_slots()], 1)


def finish(own, received, count):
    half, rows, width = own.shape
    rows = rows // count
    source = arrival_sources()
    if not aligned(rows):
        full = jnp.concatenate([own, received])[jnp.argsort(source)].astype(F32)
        return [full[:, i * rows : (i + 1) * rows] for i in range(count)]

    def body(table_ref, own_ref, received_ref, *out_refs):
        for p in range(half):
            for i, out_ref in enumerate(out_refs):
                at = slice(i * rows, (i + 1) * rows)
                out_ref[table_ref[p]] = own_ref[p, at].astype(F32)
                out_ref[table_ref[half + p]] = received_ref[p, at].astype(F32)

    whole = (own.shape, lambda i, table: (0, 0, 0))
    shape = (2 * half, rows, width)
    out = ((shape, lambda i, table: (0, 0, 0)), jax.ShapeDtypeStruct(shape, F32))
    return moved_call(body, source, (1,), [whole, whole], [out] * count, (own, received), "finish")


def place_kinds(chunks, own, received):
    n, rows, width = chunks.shape
    slots = own.shape[1] + 1
    part = n * rows // 4
    if not (aligned(rows) and aligned(part)):
        full = place(chunks, own, received).reshape(slots, 4, part, width)
        return [full[:, i].reshape(-1, width) for i in range(4)]

    def body(table_ref, chunks_ref, own_ref, received_ref, *refs):
        settle(table_ref, chunks_ref, own_ref, received_ref, refs[-1])
        full = refs[-1][...].reshape(n * rows, width)
        for i in range(4):
            refs[i][...] = full[i * part : (i + 1) * part]

    out = (((part, width), lambda s, table: (s, 0)), jax.ShapeDtypeStruct((slots * part, width), BF16))
    return moved_call(
        body, place_table(), (slots,), raw_specs(chunks), [out] * 4, (chunks, own, received), "place_kinds",
        [pltpu.VMEM((n, rows, width), BF16)],
    )


def gather_line(slots):
    for step in line_steps():
        slots = jnp.concatenate([slots, line_exchange(slots, step)])
    return slots


def gather_outer(rest, steps):
    for step in steps:
        rest = jnp.concatenate([rest, outer_exchange(rest, step)])
    return rest


def plus(a, b):
    return (a.astype(F32) + b.astype(F32)).astype(BF16)


def core_step(packed):
    return plus(packed[0], core_exchange(packed[1]))


def reduce_steps():
    def outer(step):
        def run(total):
            half = total.shape[0] // 2
            return plus(total[:half], outer_exchange(total[half:], step))

        return run

    def line(step):
        def run(total):
            half = total.shape[1] // 2
            return plus(total[:, :half], line_exchange(total[:, half:], step))

        return run

    return [outer(step) for step in reversed(outer_steps())], [line(step) for step in reversed(line_steps())]


def small_steps():
    def run(axis, bit):
        return lambda value: value + lax.ppermute(value, axis, [(i, i ^ bit) for i in range(lax.axis_size(axis))])

    return [run(axis, 1 << i) for axis in ("dp", "tensor") for i in range(log2(lax.axis_size(axis)))]


def chain(steps):
    def run(value):
        for step in steps:
            value = step(value)
        return value

    return run


def lockstep(values, chains):
    for stage in range(max(len(chain) for chain in chains)):
        values = [
            chain[stage](value) if stage < len(chain) and chain[stage] else value
            for value, chain in zip(values, chains)
        ]
        values = lax.optimization_barrier(values)
    return values


def ffn_cost(rows, hidden, width, products):
    return 2 * rows * hidden * width * products


def ffn_slot(low_ref, up, bias_ref, down, act_ref, slope_ref, out_ref):
    @pl.when(pl.program_id(0) == 0)
    def _():
        out_ref[...] = jnp.zeros_like(out_ref)

    step = low_ref.shape[0] // 4
    for i in range(4):
        at = slice(i * step, (i + 1) * step)
        hidden = dot(low_ref[at, :], up, 1, 0) + bias_ref[0]
        cdf = 0.5 * (1.0 + lax.erf(hidden * math.sqrt(0.5)))
        act = (hidden * cdf).astype(BF16)
        act_ref[at, :] = act
        pdf = jnp.exp(hidden * hidden * -0.5) * (1.0 / math.sqrt(2.0 * math.pi))
        slope_ref[at, :] = (cdf + hidden * pdf).astype(BF16)
        out_ref[at, :] += dot(act, down, 1, 0)


def ffn_specs(rows, width, slots, part):
    whole = ((rows, width), lambda s, table: (0, 0))
    units = ((rows, part), lambda s, table: (0, s))
    shape = jax.ShapeDtypeStruct((rows, slots * part), BF16)
    return whole, units, [(units, shape), (units, shape), (whole, jax.ShapeDtypeStruct((rows, width), F32))]


def ffn_first(low, up_bias, chunks, own, received):
    rows, width = low.shape
    slots, part = up_bias.shape[0], up_bias.shape[2]
    count = chunks[0].shape[1]
    if not aligned(count):
        up, down = (place(c, *(h[:, :, i * count : (i + 1) * count] for h in (own, received))) for i, c in enumerate(chunks))
        up, down = up.reshape(slots, width, part), down.reshape(slots, part, width)
        return (*ffn_forward(low, up, up_bias, down), up, down)

    def body(table_ref, low_ref, bias_ref, *refs):
        up_refs, down_refs, (act_ref, slope_ref, out_ref, up_ref, down_ref) = refs[:3], refs[3:6], refs[6:]
        settle(table_ref, *up_refs, up_ref.at[0])
        settle(table_ref, *down_refs, down_ref.at[0])
        up, down = up_ref[0].reshape(width, part), down_ref[0].reshape(part, width)
        ffn_slot(low_ref, up, bias_ref, down, act_ref, slope_ref, out_ref)

    whole, _, outs = ffn_specs(rows, width, slots, part)
    for c in chunks:
        outs.append((((1,) + c.shape, lambda s, table: (s, 0, 0, 0)), jax.ShapeDtypeStruct((slots,) + c.shape, BF16)))
    act, slope, out, up, down = moved_call(
        body, place_table(), (slots,),
        [whole, ((1, 1, part), lambda s, table: (s, 0, 0))] + raw_specs(chunks[0], 0) + raw_specs(chunks[1], 1),
        outs, (low, up_bias, chunks[0], own, received, chunks[1], own, received), "ffn_first",
        flops=ffn_cost(rows, slots * part, width, 2), transcendentals=rows * slots * part * 2,
    )
    return act, slope, out, up.reshape(slots, width, part), down.reshape(slots, part, width)


def ffn_forward(low, up, up_bias, down):
    rows, width = low.shape
    slots, part = up_bias.shape[0], up_bias.shape[2]

    def body(table_ref, low_ref, up_ref, bias_ref, down_ref, act_ref, slope_ref, out_ref):
        ffn_slot(low_ref, up_ref[0], bias_ref, down_ref[0], act_ref, slope_ref, out_ref)

    whole, _, outs = ffn_specs(rows, width, slots, part)
    slot = lambda s, table: (s, 0, 0)
    return moved_call(
        body, jnp.zeros((1,), jnp.int32), (slots,),
        [whole, ((1, width, part), slot), ((1, 1, part), slot), ((1, part, width), slot)],
        outs, (low, up, up_bias, down), "ffn_forward",
        flops=ffn_cost(rows, slots * part, width, 2), transcendentals=rows * slots * part * 2,
    )


def ffn_backward(g_ffn, low, act, slope, up, down, earlier):
    rows, width = low.shape
    slots, part = up.shape[0], up.shape[2]
    n = lax.axis_size("dp")
    fused = bool(earlier) and aligned(width // n) and aligned(part // n)
    half = n // 2

    def body(table_ref, g_ref, low_ref, act_ref, slope_ref, up_ref, down_ref, *refs):
        olds, refs = refs[: len(earlier)], refs[len(earlier) :]
        mid_ref, bias_ref, outs = refs[0], refs[1], refs[2:]
        g = g_ref[...]
        hid = (dot(g, down_ref[0], 1, 1) * slope_ref[...].astype(F32)).astype(BF16)
        bias_ref[0] = jnp.sum(hid.astype(F32), 0, keepdims=True)
        back = dot(hid, up_ref[0], 1, 1)

        @pl.when(pl.program_id(0) == 0)
        def _():
            mid_ref[...] = back

        @pl.when(pl.program_id(0) > 0)
        def _():
            mid_ref[...] += back

        for i, (left, right) in enumerate(((low_ref[...], hid), (act_ref[...], g))):
            total = dot(left, right, 0, 0)
            if olds:
                total = total + olds[i][0]
            if fused:
                keep_ref, send_ref, scratch = outs[2 * i], outs[2 * i + 1], outs[4 + i]
                scratch[...] = total.astype(BF16).reshape(scratch.shape)
                for p in range(half):
                    keep_ref[p, 0] = scratch[table_ref[p]]
                    send_ref[p, 0] = scratch[table_ref[half + p]]
            else:
                outs[i][0] = total.astype(outs[i].dtype)

    whole, units, _ = ffn_specs(rows, width, slots, part)
    slot = lambda s, table: (s, 0, 0)
    shapes = [(width, part), (part, width)]
    weights = [((1,) + shape, slot) for shape in shapes]
    outs = [
        (whole, jax.ShapeDtypeStruct((rows, width), F32)),
        (((1, 1, part), slot), jax.ShapeDtypeStruct((slots, 1, part), F32)),
    ]
    scratch = []
    for shape, spec in zip(shapes, weights):
        if fused:
            chunk = (n, shape[0] // n, shape[1])
            outs += packed_outs(slots, *chunk)
            scratch.append(pltpu.VMEM(chunk, BF16))
        else:
            outs.append((spec, jax.ShapeDtypeStruct((slots,) + shape, BF16 if earlier else F32)))
    got = moved_call(
        body, pack_table(), (slots,),
        [whole, whole, units, units] + weights + (weights if earlier else []),
        outs, (g_ffn, low, act, slope, up, down, *earlier), "ffn_backward", scratch,
        flops=ffn_cost(rows, slots * part, width, 4),
    )
    if fused:
        return got[0], got[1], got[2:4], got[4:6]
    if earlier:
        return got[0], got[1], *(pack(d.reshape(slots, n, -1, d.shape[-1])) for d in got[2:])
    return got


def lane_masks(rows):
    lane = lax.broadcasted_iota(jnp.int32, (rows, LANES), 1)
    return [(lane >= h * HEAD_DIM) & (lane < (h + 1) * HEAD_DIM) for h in range(LANES // HEAD_DIM)]


def only(mask, value):
    return jnp.where(mask, value, jnp.zeros_like(value))


def attention_forward(q, k, v, keys):
    rows, width = q.shape
    padded = k.shape[0]
    scale = 1.0 / math.sqrt(HEAD_DIM)

    def body(q_ref, k_ref, v_ref, out_ref, lse_ref):
        q = q_ref[...] * jnp.asarray(scale, BF16)
        k, v = k_ref[...], v_ref[...]
        live = lax.broadcasted_iota(jnp.int32, (1, padded), 1) < keys
        out = jnp.zeros((rows, LANES), F32)
        lses = jnp.zeros((rows, LANES), F32)
        for mine, theirs in zip(lane_masks(rows), lane_masks(padded)):
            scores = jnp.where(live, dot(only(mine, q), k, 1, 1), -jnp.inf)
            top = jnp.max(scores, -1, keepdims=True)
            weights = jnp.exp(scores - top)
            total = jnp.sum(weights, -1, keepdims=True)
            probs = (weights * (1.0 / total)).astype(BF16)
            out = out + dot(probs, only(theirs, v), 1, 0)
            lses = jnp.where(mine, top + jnp.log(total), lses)
        out_ref[...] = out.astype(BF16)
        lse_ref[...] = lses

    q_spec = pl.BlockSpec((rows, LANES), lambda h: (0, h))
    k_spec = pl.BlockSpec((padded, LANES), lambda h: (0, h))
    return pl.pallas_call(
        body,
        grid=(width // LANES,),
        in_specs=[q_spec, k_spec, k_spec],
        out_specs=[q_spec, q_spec],
        out_shape=[jax.ShapeDtypeStruct((rows, width), BF16), jax.ShapeDtypeStruct((rows, width), F32)],
        cost_estimate=cost(8 * rows * padded * width, rows * padded * width // HEAD_DIM, (q, k, v, q, q), ()),
        name="attention_forward",
    )(q, k, v)


def attention_backward(q, k, v, lse, g_att, keys):
    rows, width = q.shape
    padded = k.shape[0]
    scale = 1.0 / math.sqrt(HEAD_DIM)

    def body(q_ref, k_ref, v_ref, lse_ref, g_ref, gq_ref, gk_ref, gv_ref, sum_q_ref, sum_v_ref):
        q, g = q_ref[...] * jnp.asarray(scale, BF16), g_ref[...]
        k, v = k_ref[...], v_ref[...]
        live = lax.broadcasted_iota(jnp.int32, (1, padded), 1) < keys
        gq = jnp.zeros((rows, LANES), F32)
        gk = jnp.zeros((padded, LANES), F32)
        gv = jnp.zeros((padded, LANES), F32)
        for h, (mine, theirs) in enumerate(zip(lane_masks(rows), lane_masks(padded))):
            q_h, g_h = only(mine, q), only(mine, g)
            scores = dot(q_h, k, 1, 1)
            full = jnp.where(live, jnp.exp(scores - lse_ref[:, h * HEAD_DIM : h * HEAD_DIM + 1]), 0.0)
            g_probs = dot(g_h, v, 1, 1)
            inner = jnp.sum(g_probs * full, -1, keepdims=True)
            g_scores = (full * (g_probs - inner)).astype(BF16)
            gq = gq + dot(g_scores, only(theirs, k), 1, 0)
            gk = gk + dot(g_scores, q_h, 0, 0)
            gv = gv + dot(full.astype(BF16), g_h, 0, 0)
        gq = (gq * scale).astype(BF16)
        gv = gv.astype(BF16)
        gq_ref[...] = gq
        gk_ref[...] = gk.astype(BF16)
        gv_ref[...] = gv
        sum_q_ref[...] = jnp.sum(gq.astype(F32), 0, keepdims=True)
        sum_v_ref[...] = jnp.sum(gv.astype(F32), 0, keepdims=True)

    q_spec = pl.BlockSpec((rows, LANES), lambda h: (0, h))
    k_spec = pl.BlockSpec((padded, LANES), lambda h: (0, h))
    sum_spec = pl.BlockSpec((1, LANES), lambda h: (0, h))
    return pl.pallas_call(
        body,
        grid=(width // LANES,),
        in_specs=[q_spec, k_spec, k_spec, q_spec, q_spec],
        out_specs=[q_spec, k_spec, k_spec, sum_spec, sum_spec],
        out_shape=[
            jax.ShapeDtypeStruct((rows, width), BF16),
            jax.ShapeDtypeStruct((padded, width), BF16),
            jax.ShapeDtypeStruct((padded, width), BF16),
            jax.ShapeDtypeStruct((1, width), F32),
            jax.ShapeDtypeStruct((1, width), F32),
        ],
        cost_estimate=cost(20 * rows * padded * width, rows * padded * width // HEAD_DIM, (q, k, v, lse, g_att, q, k, v), ()),
        name="attention_backward",
    )(q, k, v, lse, g_att)


def attention_weights(segments, slots):
    width = segments[0][0].shape[1]
    part = width // slots
    n = lax.axis_size("dp")
    rows = 4 * part // n
    half = n // 2
    fused = aligned(rows)
    swap = other_half_slots()
    operands = [a for segment in segments for a in segment]

    def body(table_ref, *refs):
        out_refs = refs[len(operands) :]
        full = out_refs[-1]
        groups = [refs[i : i + 6] for i in range(0, len(operands), 6)]
        for kind in range(4):
            total = None
            for refs_of in groups:
                left = refs_of[4] if kind == 3 else refs_of[kind]
                right = refs_of[5][...] if kind == 3 else refs_of[3][: left.shape[0], :]
                one = dot(left[...], right, 0, 0)
                total = one if total is None else total + one
            for s in range(slots):
                full[s, kind * part : (kind + 1) * part, :] = total[s * part : (s + 1) * part].astype(BF16)
        if fused:
            for p in range(half):
                mine = pl.ds(pl.multiple_of(table_ref[p] * rows, 16), rows)
                theirs = pl.ds(pl.multiple_of(table_ref[half + p] * rows, 16), rows)
                for s in range(slots):
                    out_refs[0][p, s] = full[s, mine, :]
                    out_refs[1][p, s] = full[swap[s], theirs, :]

    everything = lambda a: (a.shape, lambda i, table: (0,) * len(a.shape))
    packed = jax.ShapeDtypeStruct((half, slots, rows, width), BF16)
    whole = jax.ShapeDtypeStruct((slots, 4 * part, width), BF16)
    shapes = [packed, packed] if fused else [whole]
    got = moved_call(
        body, arrival_sources(), (1,), [everything(a) for a in operands], [(everything(a), a) for a in shapes], operands,
        "attention_weights", [pltpu.VMEM(whole.shape, BF16)] if fused else [],
        flops=sum(2 * a.size * width for a in operands) * 2 // 3,
    )
    return got if fused else pack(got[0].reshape(slots, n, rows, width))


def local(text_in, start_memory, w_qkv, b_qv, w_o, w_up, b_up, w_down, norm_gains, biases, cot_text, cot_memory):
    text, cot_rows, cot_mem = text_in[0], cot_text[0], cot_memory[0]
    text_total, width = text.shape
    mem = start_memory.shape[0]
    seg = text_total // SEGMENTS
    rows = seg + mem
    keys = rows + mem
    padded = -(-keys // LANES) * LANES
    n_t, n_dp = lax.axis_size("tensor"), lax.axis_size("dp")
    head_part = w_qkv.shape[2]
    part = b_up.shape[0]
    t = lax.axis_index("tensor")

    small = jnp.concatenate([b_qv.reshape(-1), b_up])
    small = jnp.pad(small, (0, 8 * width - small.shape[0])).reshape(1, 8, width)
    d = lax.axis_index("dp")
    own_chunk = lambda chunks: lax.dynamic_index_in_dim(chunks, d, 0)
    kinds = jnp.concatenate([w_qkv.transpose(0, 2, 1).reshape(-1, width), w_o]).reshape(n_dp, -1, width)
    chunks = [w_up.reshape(n_dp, -1, part), w_down.reshape(n_dp, -1, width)]
    lined = gather_line(jnp.concatenate([own_chunk(kinds), small], 1))
    grow = lambda exchange, step: lambda value: jnp.concatenate([value, exchange(value, step)])
    rest, ffn_rest = lockstep(
        [lined[None, 1:, : kinds.shape[1]], jnp.concatenate([own_chunk(c) for c in chunks], 1)],
        [[grow(outer_exchange, step) for step in outer_steps()], [grow(line_exchange, step) for step in line_steps()]],
    )
    small = lined[:, kinds.shape[1] :].reshape(n_t, -1).astype(F32)
    q_bias = small[:, :head_part].reshape(1, -1)
    v_bias = small[:, head_part : 2 * head_part].reshape(1, -1)
    up_bias = small[:, None, 2 * head_part : 2 * head_part + part]
    received = core_exchange(rest)
    ffn_rest = ffn_rest[None, 1:]
    first, *middle, last = outer_steps()
    (q_w, k_w, v_w, o_w), ffn_received = lax.optimization_barrier(
        (place_kinds(kinds, rest, received), outer_exchange(ffn_rest, first))
    )
    ffn_rest = gather_outer(jnp.concatenate([ffn_rest, ffn_received]), middle)

    read = start_memory
    kept, pieces = [], []
    for s in range(SEGMENTS):
        x = jnp.concatenate([text[s * seg : (s + 1) * seg], start_memory, read, jnp.zeros((padded - keys, width), BF16)])
        q = (dot(x[:rows], q_w, 1, 1) + q_bias).astype(BF16)
        k = dot(x, k_w, 1, 1).astype(BF16)
        v = (dot(x, v_w, 1, 1) + v_bias).astype(BF16)
        att, lse = attention_forward(q, k, v, keys)
        if s == 0:
            att, ffn_received = lax.optimization_barrier((att, outer_exchange(ffn_rest, last)))
            ffn_rest = jnp.concatenate([ffn_rest, ffn_received])
        n1, r1 = norm_stats(x[:rows].astype(F32) + dot(att, o_w, 1, 0) + biases[0])
        middle = n1 * norm_gains[0] + biases[1]
        low = middle.astype(BF16)
        if s == 0:
            act, slope, ffn, up_full, down_full = ffn_first(low, up_bias, chunks, ffn_rest, core_exchange(ffn_rest))
        else:
            act, slope, ffn = ffn_forward(low, up_full, up_bias, down_full)
        n2, r2 = norm_stats(middle + ffn + biases[2])
        result = (n2 * norm_gains[1] + biases[3]).astype(BF16)
        pieces.append(result[:seg])
        read = result[seg:]
        kept.append((x, q, k, v, lse, att, n1, r1, low, act, slope, n2, r2))

    segments, sums, ends = [], [], []
    carry = cot_mem.astype(F32)
    d_text = [None] * SEGMENTS
    outers, lines = reduce_steps()
    earlier = ()
    for s in reversed(range(SEGMENTS)):
        x, q, k, v, lse, att, n1, r1, low, act, slope, n2, r2 = kept[s]
        g_res = jnp.concatenate([cot_rows[s * seg : (s + 1) * seg].astype(F32), carry])
        g_pre2 = norm_backward(g_res, n2, r2, norm_gains[1])
        g_mid, g_bup, d_up, d_down = ffn_backward(g_pre2.astype(BF16), low, act, slope, up_full, down_full, earlier)
        earlier = (d_up, d_down)
        g_mid = g_mid + g_pre2
        g_pre1 = norm_backward(g_mid, n1, r1, norm_gains[0])
        g_attn = g_pre1.astype(BF16)
        g_att = dot(g_attn, o_w, 1, 1).astype(BF16)
        if s == 0:
            g_att, total_down = lax.optimization_barrier((g_att, core_step(d_down)))
            total_down, total_up = lines[0](total_down), core_step(d_up)
        g_q, g_k, g_v, sum_q, sum_v = attention_backward(q, k, v, lse, g_att, keys)
        if s == 0:
            (g_q, g_k, g_v), total_up = lax.optimization_barrier(((g_q, g_k, g_v), total_up))
            total_up = outers[0](total_up)
        segments.append((g_q, g_k, g_v, x, att, g_attn))
        g_x = dot(g_k, k_w, 1, 0) + dot(g_v, v_w, 1, 0)
        top = g_x[:rows] + dot(g_q, q_w, 1, 0) + g_pre1
        d_text[s] = top[:seg]
        carry = g_x[rows:keys]
        ends += [top[seg:]] if s > 0 else [top[seg:], carry]
        over = lambda value: jnp.sum(value, 0)
        sums.append(
            [over(g_mid * n1), over(g_res * n2), over(g_pre1), over(g_mid), over(g_pre2), over(g_res)]
            + [sum_q[0], sum_v[0], g_bup[:, 0]]
        )

    packed = attention_weights(segments, n_t)
    sums = [a + b for a, b in zip(*sums)]
    pick = (jnp.arange(n_t)[:, None] == t ^ slot_masks()[0]).astype(F32)
    by_slot = jnp.concatenate([sums[6].reshape(n_t, -1), sums[7].reshape(n_t, -1), sums[8]], 1)
    by_index = jnp.dot(pick, by_slot, precision=lax.Precision.HIGHEST)
    d_mem = sum(ends[1:], ends[0])
    vectors = jnp.concatenate(
        [jnp.stack(sums[:6]), d_mem]
        + [by_index[:, i * head_part : (i + 1) * head_part].reshape(1, width) for i in (0, 1)]
        + [by_index[:, 2 * head_part :].reshape(-1, width)]
    )
    smalls = small_steps()
    inside = len(outers) + len(lines)
    total, total_up, total_down, vectors = lockstep(
        [packed, total_up, total_down, vectors],
        [
            [core_step] + outers + lines,
            [chain(outers[1:]), None] + lines,
            [None] + lines[1:] + outers,
            [None] + smalls[:inside],
        ],
    )
    vectors = chain(smalls[inside:])(vectors)
    summed = jnp.concatenate([a.reshape(1, -1, width) for a in (total_up, total_down, total)], 1)
    summed = gather_outer(summed, outer_steps())
    g_up, g_down, g_kinds = (a.reshape(-1, width) for a in finish(summed, core_exchange(summed), 3))
    g_kinds = g_kinds.reshape(4, head_part, width)
    g_qkv, g_out = g_kinds[:3].transpose(0, 2, 1), g_kinds[3]
    g_bqv = lax.dynamic_slice_in_dim(vectors[6 + mem : 8 + mem], t * head_part, head_part, 1)
    g_bup = lax.dynamic_slice_in_dim(vectors[8 + mem :].reshape(n_t, -1), t, 1, 0)[0]

    return (
        jnp.concatenate(pieces)[None],
        read[None],
        jnp.concatenate(d_text)[None],
        vectors[6 : 6 + mem],
        g_qkv,
        g_bqv,
        g_out,
        g_up,
        g_bup,
        g_down,
        vectors[:2],
        vectors[2:6],
    )


def solution(mesh):
    own = P(("dp", "tensor"), None, None)
    return jax.shard_map(
        local,
        mesh=mesh,
        in_specs=(
            own, P(), P(None, None, "tensor"), P(None, "tensor"), P("tensor", None), P(None, "tensor"),
            P("tensor"), P("tensor", None), P(), P(), own, own,
        ),
        out_specs=(
            own, own, own, P(), P(None, None, "tensor"), P(None, "tensor"), P("tensor", None),
            P(None, "tensor"), P("tensor"), P("tensor", None), P(), P(),
        ),
        check_vma=False,
    )
```

```python
import math

import jax
import jax.numpy as jnp
from jax import lax
from jax.experimental import pallas as pl
from jax.experimental.pallas import tpu as pltpu
from jax.sharding import PartitionSpec as P

HEAD_DIM = 64
SEGMENTS = 2
EPSILON = 1e-06
LANES = 128
F32 = jnp.float32
BF16 = jnp.bfloat16


def dot(a, b, ca, cb):
    return lax.dot_general(a, b, (((ca,), (cb,)), ((), ())), preferred_element_type=F32)


def norm_stats(value):
    centred = value - jnp.mean(value, -1, keepdims=True)
    rstd = lax.rsqrt(jnp.mean(centred * centred, -1, keepdims=True) + EPSILON)
    return centred * rstd, rstd


def norm_backward(grad_out, normed, rstd, gain):
    scaled = grad_out * gain
    first = jnp.mean(scaled, -1, keepdims=True)
    second = jnp.mean(scaled * normed, -1, keepdims=True)
    return rstd * (scaled - first - normed * second)


def log2(n):
    return n.bit_length() - 1


def outer_mask(core, step):
    outer = log2(lax.axis_size("dp")) - 1
    return 2 << (step if core == 0 else outer - 1 - step)


def outer_exchange(value, step):
    pairs = [(i, i ^ outer_mask(i & 1, step)) for i in range(lax.axis_size("dp"))]
    return lax.ppermute(value, "dp", pairs)


def core_exchange(value):
    return lax.ppermute(value, "dp", [(i, i ^ 1) for i in range(lax.axis_size("dp"))])


def line_exchange(value, step):
    n = lax.axis_size("tensor")
    pairs = []
    for i in range(lax.axis_size("dp")):
        mask = 1 << (step if i & 1 == 0 else log2(n) - 1 - step)
        pairs += [(i * n + t, i * n + (t ^ mask)) for t in range(n)]
    return lax.ppermute(value, ("dp", "tensor"), pairs)


def outer_steps():
    return range(log2(lax.axis_size("dp")) - 1)


def line_steps():
    return range(log2(lax.axis_size("tensor")))


def arrival_sources():
    half = lax.axis_size("dp") // 2
    tables = [
        jnp.array([sum(outer_mask(core, i) for i in outer_steps() if j >> i & 1) for j in range(half)], jnp.int32)
        for core in (0, 1)
    ]
    d = lax.axis_index("dp")
    core = d % 2
    mine = jnp.where(core == 0, tables[0], tables[1])
    theirs = jnp.where(core == 0, tables[1], tables[0])
    return jnp.concatenate([d ^ mine, d ^ 1 ^ theirs])


def slot_masks():
    n = lax.axis_size("tensor")
    orders = []
    for flip in (False, True):
        places = [log2(n) - 1 - i if flip else i for i in line_steps()]
        orders.append(jnp.array([sum(1 << places[i] for i in line_steps() if s >> i & 1) for s in range(n)], jnp.int32))
    core = lax.axis_index("dp") % 2
    return jnp.where(core == 0, orders[0], orders[1]), jnp.where(core == 0, orders[1], orders[0])


def other_half_slots():
    n = lax.axis_size("tensor")
    return [sum(1 << (log2(n) - 1 - i) for i in line_steps() if s >> i & 1) for s in range(n)]


def cost(flops, transcendentals, operands, shapes):
    moved = sum(a.size * a.dtype.itemsize for a in list(operands) + list(shapes))
    return pl.CostEstimate(flops=flops, transcendentals=transcendentals, bytes_accessed=moved)


def moved_call(body, table, grid, ins, outs, operands, name, scratch=(), flops=0, transcendentals=0):
    shapes = [shape for _, shape in outs]
    return pl.pallas_call(
        body,
        grid_spec=pltpu.PrefetchScalarGridSpec(
            num_scalar_prefetch=1,
            grid=grid,
            in_specs=[pl.BlockSpec(*spec) for spec in ins],
            out_specs=[pl.BlockSpec(*spec) for spec, _ in outs],
            scratch_shapes=list(scratch),
        ),
        out_shape=shapes,
        cost_estimate=cost(flops, transcendentals, operands, shapes),
        name=name,
    )(table, *operands)


def aligned(rows):
    return rows % 16 == 0


def place_table():
    return jnp.concatenate([arrival_sources(), jnp.array([max(s - 1, 0) for s in other_half_slots()], jnp.int32)])


def pack_table():
    return jnp.concatenate([arrival_sources(), jnp.array(other_half_slots(), jnp.int32)])


def raw_specs(chunks, at=0):
    n, rows, width = chunks.shape
    block = (n // 2, 1, rows, width)
    return [
        ((n, rows, width), lambda s, table: (0, 0, 0)),
        (block, lambda s, table: (0, jnp.maximum(s - 1, 0), at, 0)),
        (block, lambda s, table: (0, table[n + s], at, 0)),
    ]


def settle(table_ref, chunks_ref, own_ref, received_ref, out):
    half = own_ref.shape[0]

    @pl.when(pl.program_id(0) == 0)
    def _():
        out[...] = chunks_ref[...]

    @pl.when(pl.program_id(0) > 0)
    def _():
        for p in range(half):
            out[table_ref[p]] = own_ref[p, 0]
            out[table_ref[half + p]] = received_ref[p, 0]


def packed_outs(slots, n, rows, width):
    shape = jax.ShapeDtypeStruct((n // 2, slots, rows, width), BF16)
    block = (n // 2, 1, rows, width)
    return [
        ((block, lambda s, table: (0, s, 0, 0)), shape),
        ((block, lambda s, table: (0, table[n + s], 0, 0)), shape),
    ]


def place(chunks, own, received):
    others = own.shape[1]
    swap = other_half_slots()
    received = jnp.stack([received[:, swap[s] - 1] for s in range(1, others + 1)], 1)
    moved = jnp.concatenate([own, received])[jnp.argsort(arrival_sources())]
    return jnp.concatenate([chunks[None], moved.transpose(1, 0, 2, 3)])


def pack(total):
    half = total.shape[1] // 2
    moved = total.transpose(1, 0, 2, 3)[arrival_sources()]
    return moved[:half], jnp.stack([moved[half:, s] for s in other_half_slots()], 1)


def finish(own, received, count):
    half, rows, width = own.shape
    rows = rows // count
    source = arrival_sources()
    if not aligned(rows):
        full = jnp.concatenate([own, received])[jnp.argsort(source)].astype(F32)
        return [full[:, i * rows : (i + 1) * rows] for i in range(count)]

    def body(table_ref, own_ref, received_ref, *out_refs):
        for p in range(half):
            for i, out_ref in enumerate(out_refs):
                at = slice(i * rows, (i + 1) * rows)
                out_ref[table_ref[p]] = own_ref[p, at].astype(F32)
                out_ref[table_ref[half + p]] = received_ref[p, at].astype(F32)

    whole = (own.shape, lambda i, table: (0, 0, 0))
    shape = (2 * half, rows, width)
    out = ((shape, lambda i, table: (0, 0, 0)), jax.ShapeDtypeStruct(shape, F32))
    return moved_call(body, source, (1,), [whole, whole], [out] * count, (own, received), "finish")


def finish_kinds(own, received, head_part):
    half, rows, width = own.shape
    n = 2 * half
    if not aligned(rows):
        full = finish(own, received, 1)[0].reshape(4, head_part, width)
        return full[:3], full[3]

    def body(table_ref, own_ref, received_ref, qkv_ref, out_ref, scratch):
        for p in range(half):
            scratch[table_ref[p]] = own_ref[p].astype(F32)
            scratch[table_ref[half + p]] = received_ref[p].astype(F32)
        full = scratch[...].reshape(n * rows, width)
        for i in range(3):
            qkv_ref[i] = full[i * head_part : (i + 1) * head_part]
        out_ref[...] = full[3 * head_part :]

    whole = (own.shape, lambda i, table: (0, 0, 0))
    shapes = [(3, head_part, width), (head_part, width)]
    outs = [
        ((shape, lambda i, table, rank=len(shape): (0,) * rank), jax.ShapeDtypeStruct(shape, F32)) for shape in shapes
    ]
    return moved_call(
        body, arrival_sources(), (1,), [whole, whole], outs, (own, received), "finish_kinds",
        [pltpu.VMEM((n, rows, width), F32)],
    )


def place_kinds(chunks, own, received):
    n, rows, width = chunks.shape
    slots = own.shape[1] + 1
    part = n * rows // 4
    if not (aligned(rows) and aligned(part)):
        full = place(chunks, own, received).reshape(slots, 4, part, width)
        return [full[:, i].reshape(-1, width) for i in range(4)]

    def body(table_ref, chunks_ref, own_ref, received_ref, *refs):
        settle(table_ref, chunks_ref, own_ref, received_ref, refs[-1])
        full = refs[-1][...].reshape(n * rows, width)
        for i in range(4):
            refs[i][...] = full[i * part : (i + 1) * part]

    out = (((part, width), lambda s, table: (s, 0)), jax.ShapeDtypeStruct((slots * part, width), BF16))
    return moved_call(
        body, place_table(), (slots,), raw_specs(chunks), [out] * 4, (chunks, own, received), "place_kinds",
        [pltpu.VMEM((n, rows, width), BF16)],
    )


def gather_outer(rest, steps):
    for step in steps:
        rest = jnp.concatenate([rest, outer_exchange(rest, step)])
    return rest


def plus(a, b):
    return (a.astype(F32) + b.astype(F32)).astype(BF16)


def core_step(packed):
    return plus(packed[0], core_exchange(packed[1]))


def reduce_steps():
    def outer(step):
        def run(total):
            half = total.shape[0] // 2
            return plus(total[:half], outer_exchange(total[half:], step))

        return run

    def line(step):
        def run(total):
            half = total.shape[1] // 2
            return plus(total[:, :half], line_exchange(total[:, half:], step))

        return run

    return [outer(step) for step in reversed(outer_steps())], [line(step) for step in reversed(line_steps())]


def small_steps():
    def run(axis, bit):
        return lambda value: value + lax.ppermute(value, axis, [(i, i ^ bit) for i in range(lax.axis_size(axis))])

    return [run(axis, 1 << i) for axis in ("dp", "tensor") for i in range(log2(lax.axis_size(axis)))]


def chain(steps):
    def run(value):
        for step in steps:
            value = step(value)
        return value

    return run


def lockstep(values, chains):
    for stage in range(max(len(chain) for chain in chains)):
        values = [
            chain[stage](value) if stage < len(chain) and chain[stage] else value
            for value, chain in zip(values, chains)
        ]
        values = lax.optimization_barrier(values)
    return values


def ffn_cost(rows, hidden, width, products):
    return 2 * rows * hidden * width * products


def ffn_slot(low_ref, up, bias_ref, down, act_ref, slope_ref, out_ref):
    @pl.when(pl.program_id(0) == 0)
    def _():
        out_ref[...] = jnp.zeros_like(out_ref)

    step = low_ref.shape[0] // 4
    for i in range(4):
        at = slice(i * step, (i + 1) * step)
        hidden = dot(low_ref[at, :], up, 1, 0) + bias_ref[0]
        cdf = 0.5 * (1.0 + lax.erf(hidden * math.sqrt(0.5)))
        act = (hidden * cdf).astype(BF16)
        act_ref[at, :] = act
        pdf = jnp.exp(hidden * hidden * -0.5) * (1.0 / math.sqrt(2.0 * math.pi))
        slope_ref[at, :] = (cdf + hidden * pdf).astype(BF16)
        out_ref[at, :] += dot(act, down, 1, 0)


def ffn_specs(rows, width, slots, part):
    whole = ((rows, width), lambda s, table: (0, 0))
    units = ((rows, part), lambda s, table: (0, s))
    shape = jax.ShapeDtypeStruct((rows, slots * part), BF16)
    return whole, units, [(units, shape), (units, shape), (whole, jax.ShapeDtypeStruct((rows, width), F32))]


def ffn_first(low, up_bias, chunks, own, received):
    rows, width = low.shape
    slots, part = up_bias.shape[0], up_bias.shape[2]
    count = chunks[0].shape[1]
    if not aligned(count):
        up, down = (place(c, *(h[:, :, i * count : (i + 1) * count] for h in (own, received))) for i, c in enumerate(chunks))
        up, down = up.reshape(slots, width, part), down.reshape(slots, part, width)
        return (*ffn_forward(low, up, up_bias, down), up, down)

    def body(table_ref, low_ref, bias_ref, *refs):
        up_refs, down_refs, (act_ref, slope_ref, out_ref, up_ref, down_ref) = refs[:3], refs[3:6], refs[6:]
        settle(table_ref, *up_refs, up_ref.at[0])
        settle(table_ref, *down_refs, down_ref.at[0])
        up, down = up_ref[0].reshape(width, part), down_ref[0].reshape(part, width)
        ffn_slot(low_ref, up, bias_ref, down, act_ref, slope_ref, out_ref)

    whole, _, outs = ffn_specs(rows, width, slots, part)
    for c in chunks:
        outs.append((((1,) + c.shape, lambda s, table: (s, 0, 0, 0)), jax.ShapeDtypeStruct((slots,) + c.shape, BF16)))
    act, slope, out, up, down = moved_call(
        body, place_table(), (slots,),
        [whole, ((1, 1, part), lambda s, table: (s, 0, 0))] + raw_specs(chunks[0], 0) + raw_specs(chunks[1], 1),
        outs, (low, up_bias, chunks[0], own, received, chunks[1], own, received), "ffn_first",
        flops=ffn_cost(rows, slots * part, width, 2), transcendentals=rows * slots * part * 2,
    )
    return act, slope, out, up.reshape(slots, width, part), down.reshape(slots, part, width)


def ffn_forward(low, up, up_bias, down):
    rows, width = low.shape
    slots, part = up_bias.shape[0], up_bias.shape[2]

    def body(table_ref, low_ref, up_ref, bias_ref, down_ref, act_ref, slope_ref, out_ref):
        ffn_slot(low_ref, up_ref[0], bias_ref, down_ref[0], act_ref, slope_ref, out_ref)

    whole, _, outs = ffn_specs(rows, width, slots, part)
    slot = lambda s, table: (s, 0, 0)
    return moved_call(
        body, jnp.zeros((1,), jnp.int32), (slots,),
        [whole, ((1, width, part), slot), ((1, 1, part), slot), ((1, part, width), slot)],
        outs, (low, up, up_bias, down), "ffn_forward",
        flops=ffn_cost(rows, slots * part, width, 2), transcendentals=rows * slots * part * 2,
    )


def ffn_backward(g_ffn, low, act, slope, up, down, earlier):
    rows, width = low.shape
    slots, part = up.shape[0], up.shape[2]
    n = lax.axis_size("dp")
    fused = bool(earlier) and aligned(width // n) and aligned(part // n)
    half = n // 2

    def body(table_ref, g_ref, low_ref, act_ref, slope_ref, up_ref, down_ref, *refs):
        olds, refs = refs[: len(earlier)], refs[len(earlier) :]
        mid_ref, bias_ref, outs = refs[0], refs[1], refs[2:]
        g = g_ref[...]
        hid = (dot(g, down_ref[0], 1, 1) * slope_ref[...].astype(F32)).astype(BF16)
        bias_ref[0] = jnp.sum(hid.astype(F32), 0, keepdims=True)
        back = dot(hid, up_ref[0], 1, 1)

        @pl.when(pl.program_id(0) == 0)
        def _():
            mid_ref[...] = back

        @pl.when(pl.program_id(0) > 0)
        def _():
            mid_ref[...] += back

        for i, (left, right) in enumerate(((low_ref[...], hid), (act_ref[...], g))):
            total = dot(left, right, 0, 0)
            if olds:
                total = total + olds[i][0]
            if fused:
                keep_ref, send_ref, scratch = outs[2 * i], outs[2 * i + 1], outs[4 + i]
                scratch[...] = total.astype(BF16).reshape(scratch.shape)
                for p in range(half):
                    keep_ref[p, 0] = scratch[table_ref[p]]
                    send_ref[p, 0] = scratch[table_ref[half + p]]
            else:
                outs[i][0] = total.astype(outs[i].dtype)

    whole, units, _ = ffn_specs(rows, width, slots, part)
    slot = lambda s, table: (s, 0, 0)
    shapes = [(width, part), (part, width)]
    weights = [((1,) + shape, slot) for shape in shapes]
    outs = [
        (whole, jax.ShapeDtypeStruct((rows, width), F32)),
        (((1, 1, part), slot), jax.ShapeDtypeStruct((slots, 1, part), F32)),
    ]
    scratch = []
    for shape, spec in zip(shapes, weights):
        if fused:
            chunk = (n, shape[0] // n, shape[1])
            outs += packed_outs(slots, *chunk)
            scratch.append(pltpu.VMEM(chunk, BF16))
        else:
            outs.append((spec, jax.ShapeDtypeStruct((slots,) + shape, BF16 if earlier else F32)))
    got = moved_call(
        body, pack_table(), (slots,),
        [whole, whole, units, units] + weights + (weights if earlier else []),
        outs, (g_ffn, low, act, slope, up, down, *earlier), "ffn_backward", scratch,
        flops=ffn_cost(rows, slots * part, width, 4),
    )
    if fused:
        return got[0], got[1], got[2:4], got[4:6]
    if earlier:
        return got[0], got[1], *(pack(d.reshape(slots, n, -1, d.shape[-1])) for d in got[2:])
    return got


def lane_masks(rows):
    lane = lax.broadcasted_iota(jnp.int32, (rows, LANES), 1)
    return [(lane >= h * HEAD_DIM) & (lane < (h + 1) * HEAD_DIM) for h in range(LANES // HEAD_DIM)]


def only(mask, value):
    return jnp.where(mask, value, jnp.zeros_like(value))


def attention_forward(q, k, v, keys):
    rows, width = q.shape
    padded = k.shape[0]
    scale = 1.0 / math.sqrt(HEAD_DIM)

    def body(q_ref, k_ref, v_ref, out_ref, lse_ref):
        q = q_ref[...] * jnp.asarray(scale, BF16)
        k, v = k_ref[...], v_ref[...]
        live = lax.broadcasted_iota(jnp.int32, (1, padded), 1) < keys
        out = jnp.zeros((rows, LANES), F32)
        lses = jnp.zeros((rows, LANES), F32)
        for mine, theirs in zip(lane_masks(rows), lane_masks(padded)):
            scores = jnp.where(live, dot(only(mine, q), k, 1, 1), -jnp.inf)
            top = jnp.max(scores, -1, keepdims=True)
            weights = jnp.exp(scores - top)
            total = jnp.sum(weights, -1, keepdims=True)
            probs = (weights * (1.0 / total)).astype(BF16)
            out = out + dot(probs, only(theirs, v), 1, 0)
            lses = jnp.where(mine, top + jnp.log(total), lses)
        out_ref[...] = out.astype(BF16)
        lse_ref[...] = lses

    q_spec = pl.BlockSpec((rows, LANES), lambda h: (0, h))
    k_spec = pl.BlockSpec((padded, LANES), lambda h: (0, h))
    return pl.pallas_call(
        body,
        grid=(width // LANES,),
        in_specs=[q_spec, k_spec, k_spec],
        out_specs=[q_spec, q_spec],
        out_shape=[jax.ShapeDtypeStruct((rows, width), BF16), jax.ShapeDtypeStruct((rows, width), F32)],
        cost_estimate=cost(8 * rows * padded * width, rows * padded * width // HEAD_DIM, (q, k, v, q, q), ()),
        name="attention_forward",
    )(q, k, v)


def attention_backward(q, k, v, lse, g_att, keys):
    rows, width = q.shape
    padded = k.shape[0]
    scale = 1.0 / math.sqrt(HEAD_DIM)

    def body(q_ref, k_ref, v_ref, lse_ref, g_ref, gq_ref, gk_ref, gv_ref, sum_q_ref, sum_v_ref):
        q, g = q_ref[...] * jnp.asarray(scale, BF16), g_ref[...]
        k, v = k_ref[...], v_ref[...]
        live = lax.broadcasted_iota(jnp.int32, (1, padded), 1) < keys
        gq = jnp.zeros((rows, LANES), F32)
        gk = jnp.zeros((padded, LANES), F32)
        gv = jnp.zeros((padded, LANES), F32)
        for h, (mine, theirs) in enumerate(zip(lane_masks(rows), lane_masks(padded))):
            q_h, g_h = only(mine, q), only(mine, g)
            scores = dot(q_h, k, 1, 1)
            full = jnp.where(live, jnp.exp(scores - lse_ref[:, h * HEAD_DIM : h * HEAD_DIM + 1]), 0.0)
            g_probs = dot(g_h, v, 1, 1)
            inner = jnp.sum(g_probs * full, -1, keepdims=True)
            g_scores = (full * (g_probs - inner)).astype(BF16)
            gq = gq + dot(g_scores, only(theirs, k), 1, 0)
            gk = gk + dot(g_scores, q_h, 0, 0)
            gv = gv + dot(full.astype(BF16), g_h, 0, 0)
        gq = (gq * scale).astype(BF16)
        gv = gv.astype(BF16)
        gq_ref[...] = gq
        gk_ref[...] = gk.astype(BF16)
        gv_ref[...] = gv
        sum_q_ref[...] = jnp.sum(gq.astype(F32), 0, keepdims=True)
        sum_v_ref[...] = jnp.sum(gv.astype(F32), 0, keepdims=True)

    q_spec = pl.BlockSpec((rows, LANES), lambda h: (0, h))
    k_spec = pl.BlockSpec((padded, LANES), lambda h: (0, h))
    sum_spec = pl.BlockSpec((1, LANES), lambda h: (0, h))
    return pl.pallas_call(
        body,
        grid=(width // LANES,),
        in_specs=[q_spec, k_spec, k_spec, q_spec, q_spec],
        out_specs=[q_spec, k_spec, k_spec, sum_spec, sum_spec],
        out_shape=[
            jax.ShapeDtypeStruct((rows, width), BF16),
            jax.ShapeDtypeStruct((padded, width), BF16),
            jax.ShapeDtypeStruct((padded, width), BF16),
            jax.ShapeDtypeStruct((1, width), F32),
            jax.ShapeDtypeStruct((1, width), F32),
        ],
        cost_estimate=cost(20 * rows * padded * width, rows * padded * width // HEAD_DIM, (q, k, v, lse, g_att, q, k, v), ()),
        name="attention_backward",
    )(q, k, v, lse, g_att)


def attention_weights(segments, slots):
    width = segments[0][0].shape[1]
    part = width // slots
    n = lax.axis_size("dp")
    rows = 4 * part // n
    half = n // 2
    fused = aligned(rows)
    swap = other_half_slots()
    operands = [a for segment in segments for a in segment]

    def body(table_ref, *refs):
        out_refs = refs[len(operands) :]
        full = out_refs[-1]
        groups = [refs[i : i + 6] for i in range(0, len(operands), 6)]
        for kind in range(4):
            total = None
            for refs_of in groups:
                left = refs_of[4] if kind == 3 else refs_of[kind]
                right = refs_of[5][...] if kind == 3 else refs_of[3][: left.shape[0], :]
                one = dot(left[...], right, 0, 0)
                total = one if total is None else total + one
            for s in range(slots):
                full[s, kind * part : (kind + 1) * part, :] = total[s * part : (s + 1) * part].astype(BF16)
        if fused:
            for p in range(half):
                mine = pl.ds(pl.multiple_of(table_ref[p] * rows, 16), rows)
                theirs = pl.ds(pl.multiple_of(table_ref[half + p] * rows, 16), rows)
                for s in range(slots):
                    out_refs[0][p, s] = full[s, mine, :]
                    out_refs[1][p, s] = full[swap[s], theirs, :]

    everything = lambda a: (a.shape, lambda i, table: (0,) * len(a.shape))
    packed = jax.ShapeDtypeStruct((half, slots, rows, width), BF16)
    whole = jax.ShapeDtypeStruct((slots, 4 * part, width), BF16)
    shapes = [packed, packed] if fused else [whole]
    got = moved_call(
        body, arrival_sources(), (1,), [everything(a) for a in operands], [(everything(a), a) for a in shapes], operands,
        "attention_weights", [pltpu.VMEM(whole.shape, BF16)] if fused else [],
        flops=sum(2 * a.size * width for a in operands) * 2 // 3,
    )
    return got if fused else pack(got[0].reshape(slots, n, rows, width))


def local(text_in, start_memory, w_qkv, b_qv, w_o, w_up, b_up, w_down, norm_gains, biases, cot_text, cot_memory):
    text, cot_rows, cot_mem = text_in[0], cot_text[0], cot_memory[0]
    text_total, width = text.shape
    mem = start_memory.shape[0]
    seg = text_total // SEGMENTS
    rows = seg + mem
    keys = rows + mem
    padded = -(-keys // LANES) * LANES
    n_t, n_dp = lax.axis_size("tensor"), lax.axis_size("dp")
    head_part = w_qkv.shape[2]
    part = b_up.shape[0]
    t = lax.axis_index("tensor")

    small = jnp.concatenate([b_qv.reshape(-1), b_up])
    small = jnp.pad(small, (0, 8 * width - small.shape[0])).reshape(1, 8, width)
    d = lax.axis_index("dp")
    own_chunk = lambda chunks: lax.dynamic_index_in_dim(chunks, d, 0)
    kinds = jnp.concatenate([w_qkv.transpose(0, 2, 1).reshape(-1, width), w_o]).reshape(n_dp, -1, width)
    chunks = [w_up.reshape(n_dp, -1, part), w_down.reshape(n_dp, -1, width)]
    lined = jnp.concatenate([own_chunk(kinds), small], 1)
    ffn_own = jnp.concatenate([own_chunk(c) for c in chunks], 1)
    grow = lambda exchange, step: lambda value: jnp.concatenate([value, exchange(value, step)])
    grow_line = [grow(line_exchange, step) for step in line_steps()]
    lined, ffn_own = lax.optimization_barrier((grow_line[0](lined), ffn_own))
    lined, ffn_own = lockstep([lined, ffn_own], [grow_line[1:], grow_line[:1]])
    rest = gather_outer(lined[None, 1:, : kinds.shape[1]], outer_steps())
    rest, ffn_rest = lax.optimization_barrier((rest, chain(grow_line[1:])(ffn_own)))
    small = lined[:, kinds.shape[1] :].reshape(n_t, -1).astype(F32)
    q_bias = small[:, :head_part].reshape(1, -1)
    v_bias = small[:, head_part : 2 * head_part].reshape(1, -1)
    up_bias = small[:, None, 2 * head_part : 2 * head_part + part]
    received = core_exchange(rest)
    ffn_rest = ffn_rest[None, 1:]
    first, *middle, last = outer_steps()
    (q_w, k_w, v_w, o_w), ffn_received = lax.optimization_barrier(
        (place_kinds(kinds, rest, received), outer_exchange(ffn_rest, first))
    )
    ffn_rest = gather_outer(jnp.concatenate([ffn_rest, ffn_received]), middle)

    read = start_memory
    kept, pieces = [], []
    for s in range(SEGMENTS):
        x = jnp.concatenate([text[s * seg : (s + 1) * seg], start_memory, read, jnp.zeros((padded - keys, width), BF16)])
        q = (dot(x[:rows], q_w, 1, 1) + q_bias).astype(BF16)
        k = dot(x, k_w, 1, 1).astype(BF16)
        v = (dot(x, v_w, 1, 1) + v_bias).astype(BF16)
        att, lse = attention_forward(q, k, v, keys)
        if s == 0:
            att, ffn_received = lax.optimization_barrier((att, outer_exchange(ffn_rest, last)))
            ffn_rest = jnp.concatenate([ffn_rest, ffn_received])
        n1, r1 = norm_stats(x[:rows].astype(F32) + dot(att, o_w, 1, 0) + biases[0])
        middle = n1 * norm_gains[0] + biases[1]
        low = middle.astype(BF16)
        if s == 0:
            act, slope, ffn, up_full, down_full = ffn_first(low, up_bias, chunks, ffn_rest, core_exchange(ffn_rest))
        else:
            act, slope, ffn = ffn_forward(low, up_full, up_bias, down_full)
        n2, r2 = norm_stats(middle + ffn + biases[2])
        result = (n2 * norm_gains[1] + biases[3]).astype(BF16)
        pieces.append(result[:seg])
        read = result[seg:]
        kept.append((x, q, k, v, lse, att, n1, r1, low, act, slope, n2, r2))

    segments, sums, ends = [], [], []
    carry = cot_mem.astype(F32)
    d_text = [None] * SEGMENTS
    outers, lines = reduce_steps()
    earlier = ()
    for s in reversed(range(SEGMENTS)):
        x, q, k, v, lse, att, n1, r1, low, act, slope, n2, r2 = kept[s]
        g_res = jnp.concatenate([cot_rows[s * seg : (s + 1) * seg].astype(F32), carry])
        g_pre2 = norm_backward(g_res, n2, r2, norm_gains[1])
        g_mid, g_bup, d_up, d_down = ffn_backward(g_pre2.astype(BF16), low, act, slope, up_full, down_full, earlier)
        earlier = (d_up, d_down)
        g_mid = g_mid + g_pre2
        g_pre1 = norm_backward(g_mid, n1, r1, norm_gains[0])
        g_attn = g_pre1.astype(BF16)
        g_att = dot(g_attn, o_w, 1, 1).astype(BF16)
        if s == 0:
            g_att, total_up = lax.optimization_barrier((g_att, core_step(d_up)))
            total_up, total_down = outers[0](total_up), core_step(d_down)
        g_q, g_k, g_v, sum_q, sum_v = attention_backward(q, k, v, lse, g_att, keys)
        if s == 0:
            (g_q, g_k, g_v), total_up, total_down = lax.optimization_barrier(((g_q, g_k, g_v), total_up, total_down))
            total_up, total_down = chain(outers[1:])(total_up), outers[0](total_down)
        segments.append((g_q, g_k, g_v, x, att, g_attn))
        g_x = dot(g_k, k_w, 1, 0) + dot(g_v, v_w, 1, 0)
        top = g_x[:rows] + dot(g_q, q_w, 1, 0) + g_pre1
        d_text[s] = top[:seg]
        carry = g_x[rows:keys]
        ends += [top[seg:]] if s > 0 else [top[seg:], carry]
        over = lambda value: jnp.sum(value, 0)
        sums.append(
            [over(g_mid * n1), over(g_res * n2), over(g_pre1), over(g_mid), over(g_pre2), over(g_res)]
            + [sum_q[0], sum_v[0], g_bup[:, 0]]
        )

    packed = attention_weights(segments, n_t)
    packed, total_down, sums = lax.optimization_barrier((packed, total_down, sums))
    sums = [a + b for a, b in zip(*sums)]
    pick = (jnp.arange(n_t)[:, None] == t ^ slot_masks()[0]).astype(F32)
    by_slot = jnp.concatenate([sums[6].reshape(n_t, -1), sums[7].reshape(n_t, -1), sums[8]], 1)
    by_index = jnp.dot(pick, by_slot, precision=lax.Precision.HIGHEST)
    d_mem = sum(ends[1:], ends[0])
    vectors = jnp.concatenate(
        [jnp.stack(sums[:6]), d_mem]
        + [by_index[:, i * head_part : (i + 1) * head_part].reshape(1, width) for i in (0, 1)]
        + [by_index[:, 2 * head_part :].reshape(-1, width)]
    )
    spread = [grow(outer_exchange, step) for step in outer_steps()]
    smalls = small_steps()
    total, total_down = lockstep([packed, total_down], [[core_step], [chain(outers[1:])]])
    ffn = jnp.concatenate([total_up, total_down], 2)
    merge = lambda value: value.reshape(1, -1, width)
    total, ffn, vectors = lockstep(
        [total, ffn, vectors],
        [
            outers + lines,
            lines + [chain([merge] + spread[:1])] + spread[1:],
            [None] + smalls,
        ],
    )
    total = merge(total)
    total, ffn_received = lax.optimization_barrier((spread[0](total), core_exchange(ffn)))
    g_up, g_down = (a.reshape(-1, width) for a in finish(ffn, ffn_received, 2))
    total = chain(spread[1:])(total)
    g_qkv, g_out = finish_kinds(total, core_exchange(total), head_part)
    g_qkv = g_qkv.transpose(0, 2, 1)
    g_bqv = lax.dynamic_slice_in_dim(vectors[6 + mem : 8 + mem], t * head_part, head_part, 1)
    g_bup = lax.dynamic_slice_in_dim(vectors[8 + mem :].reshape(n_t, -1), t, 1, 0)[0]

    return (
        jnp.concatenate(pieces)[None],
        read[None],
        jnp.concatenate(d_text)[None],
        vectors[6 : 6 + mem],
        g_qkv,
        g_bqv,
        g_out,
        g_up,
        g_bup,
        g_down,
        vectors[:2],
        vectors[2:6],
    )


def solution(mesh):
    own = P(("dp", "tensor"), None, None)
    return jax.shard_map(
        local,
        mesh=mesh,
        in_specs=(
            own, P(), P(None, None, "tensor"), P(None, "tensor"), P("tensor", None), P(None, "tensor"),
            P("tensor"), P("tensor", None), P(), P(), own, own,
        ),
        out_specs=(
            own, own, own, P(), P(None, None, "tensor"), P(None, "tensor"), P("tensor", None),
            P(None, "tensor"), P("tensor"), P("tensor", None), P(), P(),
        ),
        check_vma=False,
    )
```

```python
import math

import jax
import jax.numpy as jnp
from jax import lax
from jax.experimental import pallas as pl
from jax.experimental.pallas import tpu as pltpu
from jax.sharding import PartitionSpec as P

HEAD_DIM = 64
SEGMENTS = 2
EPSILON = 1e-06
LANES = 128
F32 = jnp.float32
BF16 = jnp.bfloat16


def dot(a, b, ca, cb):
    return lax.dot_general(a, b, (((ca,), (cb,)), ((), ())), preferred_element_type=F32)


def norm_stats(value):
    centred = value - jnp.mean(value, -1, keepdims=True)
    rstd = lax.rsqrt(jnp.mean(centred * centred, -1, keepdims=True) + EPSILON)
    return centred * rstd, rstd


def norm_backward(grad_out, normed, rstd, gain):
    scaled = grad_out * gain
    first = jnp.mean(scaled, -1, keepdims=True)
    second = jnp.mean(scaled * normed, -1, keepdims=True)
    return rstd * (scaled - first - normed * second)


def log2(n):
    return n.bit_length() - 1


def outer_mask(core, step):
    outer = log2(lax.axis_size("dp")) - 1
    return 2 << (step if core == 0 else outer - 1 - step)


def outer_exchange(value, step):
    pairs = [(i, i ^ outer_mask(i & 1, step)) for i in range(lax.axis_size("dp"))]
    return lax.ppermute(value, "dp", pairs)


def core_exchange(value):
    return lax.ppermute(value, "dp", [(i, i ^ 1) for i in range(lax.axis_size("dp"))])


def line_exchange(value, step):
    n = lax.axis_size("tensor")
    pairs = []
    for i in range(lax.axis_size("dp")):
        mask = 1 << (step if i & 1 == 0 else log2(n) - 1 - step)
        pairs += [(i * n + t, i * n + (t ^ mask)) for t in range(n)]
    return lax.ppermute(value, ("dp", "tensor"), pairs)


def outer_steps():
    return range(log2(lax.axis_size("dp")) - 1)


def line_steps():
    return range(log2(lax.axis_size("tensor")))


def arrival_sources():
    half = lax.axis_size("dp") // 2
    tables = [
        jnp.array([sum(outer_mask(core, i) for i in outer_steps() if j >> i & 1) for j in range(half)], jnp.int32)
        for core in (0, 1)
    ]
    d = lax.axis_index("dp")
    core = d % 2
    mine = jnp.where(core == 0, tables[0], tables[1])
    theirs = jnp.where(core == 0, tables[1], tables[0])
    return jnp.concatenate([d ^ mine, d ^ 1 ^ theirs])


def slot_masks():
    n = lax.axis_size("tensor")
    orders = []
    for flip in (False, True):
        places = [log2(n) - 1 - i if flip else i for i in line_steps()]
        orders.append(jnp.array([sum(1 << places[i] for i in line_steps() if s >> i & 1) for s in range(n)], jnp.int32))
    core = lax.axis_index("dp") % 2
    return jnp.where(core == 0, orders[0], orders[1]), jnp.where(core == 0, orders[1], orders[0])


def other_half_slots():
    n = lax.axis_size("tensor")
    return [sum(1 << (log2(n) - 1 - i) for i in line_steps() if s >> i & 1) for s in range(n)]


def cost(flops, transcendentals, operands, shapes):
    moved = sum(a.size * a.dtype.itemsize for a in list(operands) + list(shapes))
    return pl.CostEstimate(flops=flops, transcendentals=transcendentals, bytes_accessed=moved)


def moved_call(body, table, grid, ins, outs, operands, name, scratch=(), flops=0, transcendentals=0):
    shapes = [shape for _, shape in outs]
    return pl.pallas_call(
        body,
        grid_spec=pltpu.PrefetchScalarGridSpec(
            num_scalar_prefetch=1,
            grid=grid,
            in_specs=[pl.BlockSpec(*spec) for spec in ins],
            out_specs=[pl.BlockSpec(*spec) for spec, _ in outs],
            scratch_shapes=list(scratch),
        ),
        out_shape=shapes,
        cost_estimate=cost(flops, transcendentals, operands, shapes),
        name=name,
    )(table, *operands)


def aligned(rows):
    return rows % 16 == 0


def place_table():
    return jnp.concatenate([arrival_sources(), jnp.array([max(s - 1, 0) for s in other_half_slots()], jnp.int32)])


def pack_table():
    return jnp.concatenate([arrival_sources(), jnp.array(other_half_slots(), jnp.int32)])


def raw_specs(chunks, at=0):
    n, rows, width = chunks.shape
    block = (n // 2, 1, rows, width)
    return [
        ((n, rows, width), lambda s, table: (0, 0, 0)),
        (block, lambda s, table: (0, jnp.maximum(s - 1, 0), at, 0)),
        (block, lambda s, table: (0, table[n + s], at, 0)),
    ]


def settle(table_ref, chunks_ref, own_ref, received_ref, out):
    half = own_ref.shape[0]

    @pl.when(pl.program_id(0) == 0)
    def _():
        out[...] = chunks_ref[...]

    @pl.when(pl.program_id(0) > 0)
    def _():
        for p in range(half):
            out[table_ref[p]] = own_ref[p, 0]
            out[table_ref[half + p]] = received_ref[p, 0]


def packed_outs(slots, n, rows, width):
    shape = jax.ShapeDtypeStruct((n // 2, slots, rows, width), BF16)
    block = (n // 2, 1, rows, width)
    return [
        ((block, lambda s, table: (0, s, 0, 0)), shape),
        ((block, lambda s, table: (0, table[n + s], 0, 0)), shape),
    ]


def place(chunks, own, received):
    others = own.shape[1]
    swap = other_half_slots()
    received = jnp.stack([received[:, swap[s] - 1] for s in range(1, others + 1)], 1)
    moved = jnp.concatenate([own, received])[jnp.argsort(arrival_sources())]
    return jnp.concatenate([chunks[None], moved.transpose(1, 0, 2, 3)])


def pack(total):
    half = total.shape[1] // 2
    moved = total.transpose(1, 0, 2, 3)[arrival_sources()]
    return moved[:half], jnp.stack([moved[half:, s] for s in other_half_slots()], 1)


def finish(own, received, count):
    half, rows, width = own.shape
    rows = rows // count
    source = arrival_sources()
    if not aligned(rows):
        full = jnp.concatenate([own, received])[jnp.argsort(source)].astype(F32)
        return [full[:, i * rows : (i + 1) * rows] for i in range(count)]

    def body(table_ref, own_ref, received_ref, *out_refs):
        for p in range(half):
            for i, out_ref in enumerate(out_refs):
                at = slice(i * rows, (i + 1) * rows)
                out_ref[table_ref[p]] = own_ref[p, at].astype(F32)
                out_ref[table_ref[half + p]] = received_ref[p, at].astype(F32)

    whole = (own.shape, lambda i, table: (0, 0, 0))
    shape = (2 * half, rows, width)
    out = ((shape, lambda i, table: (0, 0, 0)), jax.ShapeDtypeStruct(shape, F32))
    return moved_call(body, source, (1,), [whole, whole], [out] * count, (own, received), "finish")


def finish_kinds(own, received, head_part):
    half, rows, width = own.shape
    n = 2 * half
    if not aligned(rows):
        full = finish(own, received, 1)[0].reshape(4, head_part, width)
        return full[:3], full[3]

    def body(table_ref, own_ref, received_ref, qkv_ref, out_ref, scratch):
        for p in range(half):
            scratch[table_ref[p]] = own_ref[p].astype(F32)
            scratch[table_ref[half + p]] = received_ref[p].astype(F32)
        full = scratch[...].reshape(n * rows, width)
        for i in range(3):
            qkv_ref[i] = full[i * head_part : (i + 1) * head_part]
        out_ref[...] = full[3 * head_part :]

    whole = (own.shape, lambda i, table: (0, 0, 0))
    shapes = [(3, head_part, width), (head_part, width)]
    outs = [
        ((shape, lambda i, table, rank=len(shape): (0,) * rank), jax.ShapeDtypeStruct(shape, F32)) for shape in shapes
    ]
    return moved_call(
        body, arrival_sources(), (1,), [whole, whole], outs, (own, received), "finish_kinds",
        [pltpu.VMEM((n, rows, width), F32)],
    )


def place_kinds(chunks, own, received):
    n, rows, width = chunks.shape
    slots = own.shape[1] + 1
    part = n * rows // 4
    if not (aligned(rows) and aligned(part)):
        full = place(chunks, own, received).reshape(slots, 4, part, width)
        return [full[:, i].reshape(-1, width) for i in range(4)]

    def body(table_ref, chunks_ref, own_ref, received_ref, *refs):
        settle(table_ref, chunks_ref, own_ref, received_ref, refs[-1])
        full = refs[-1][...].reshape(n * rows, width)
        for i in range(4):
            refs[i][...] = full[i * part : (i + 1) * part]

    out = (((part, width), lambda s, table: (s, 0)), jax.ShapeDtypeStruct((slots * part, width), BF16))
    return moved_call(
        body, place_table(), (slots,), raw_specs(chunks), [out] * 4, (chunks, own, received), "place_kinds",
        [pltpu.VMEM((n, rows, width), BF16)],
    )


def gather_outer(rest, steps):
    for step in steps:
        rest = jnp.concatenate([rest, outer_exchange(rest, step)])
    return rest


def plus(a, b):
    return (a.astype(F32) + b.astype(F32)).astype(BF16)


def core_step(packed):
    return plus(packed[0], core_exchange(packed[1]))


def reduce_steps():
    def outer(step):
        def run(total):
            half = total.shape[0] // 2
            return plus(total[:half], outer_exchange(total[half:], step))

        return run

    def line(step):
        def run(total):
            half = total.shape[1] // 2
            return plus(total[:, :half], line_exchange(total[:, half:], step))

        return run

    return [outer(step) for step in reversed(outer_steps())], [line(step) for step in reversed(line_steps())]


def small_steps():
    def run(axis, bit):
        return lambda value: value + lax.ppermute(value, axis, [(i, i ^ bit) for i in range(lax.axis_size(axis))])

    return [run(axis, 1 << i) for axis in ("dp", "tensor") for i in range(log2(lax.axis_size(axis)))]


def chain(steps):
    def run(value):
        for step in steps:
            value = step(value)
        return value

    return run


def lockstep(values, chains):
    for stage in range(max(len(chain) for chain in chains)):
        values = [
            chain[stage](value) if stage < len(chain) and chain[stage] else value
            for value, chain in zip(values, chains)
        ]
        values = lax.optimization_barrier(values)
    return values


def ffn_cost(rows, hidden, width, products):
    return 2 * rows * hidden * width * products


def ffn_slot(low_ref, up, bias_ref, down, act_ref, slope_ref, out_ref):
    @pl.when(pl.program_id(0) == 0)
    def _():
        out_ref[...] = jnp.zeros_like(out_ref)

    step = low_ref.shape[0] // 4
    for i in range(4):
        at = slice(i * step, (i + 1) * step)
        hidden = dot(low_ref[at, :], up, 1, 0) + bias_ref[0]
        cdf = 0.5 * (1.0 + lax.erf(hidden * math.sqrt(0.5)))
        act = (hidden * cdf).astype(BF16)
        act_ref[at, :] = act
        pdf = jnp.exp(hidden * hidden * -0.5) * (1.0 / math.sqrt(2.0 * math.pi))
        slope_ref[at, :] = (cdf + hidden * pdf).astype(BF16)
        out_ref[at, :] += dot(act, down, 1, 0)


def ffn_specs(rows, width, slots, part):
    whole = ((rows, width), lambda s, table: (0, 0))
    units = ((rows, part), lambda s, table: (0, s))
    shape = jax.ShapeDtypeStruct((rows, slots * part), BF16)
    return whole, units, [(units, shape), (units, shape), (whole, jax.ShapeDtypeStruct((rows, width), F32))]


def ffn_first(low, up_bias, chunks, own, received):
    rows, width = low.shape
    slots, part = up_bias.shape[0], up_bias.shape[2]
    count = chunks[0].shape[1]
    if not aligned(count):
        up, down = (place(c, *(h[:, :, i * count : (i + 1) * count] for h in (own, received))) for i, c in enumerate(chunks))
        up, down = up.reshape(slots, width, part), down.reshape(slots, part, width)
        return (*ffn_forward(low, up, up_bias, down), up, down)

    def body(table_ref, low_ref, bias_ref, *refs):
        up_refs, down_refs, (act_ref, slope_ref, out_ref, up_ref, down_ref) = refs[:3], refs[3:6], refs[6:]
        settle(table_ref, *up_refs, up_ref.at[0])
        settle(table_ref, *down_refs, down_ref.at[0])
        up, down = up_ref[0].reshape(width, part), down_ref[0].reshape(part, width)
        ffn_slot(low_ref, up, bias_ref, down, act_ref, slope_ref, out_ref)

    whole, _, outs = ffn_specs(rows, width, slots, part)
    for c in chunks:
        outs.append((((1,) + c.shape, lambda s, table: (s, 0, 0, 0)), jax.ShapeDtypeStruct((slots,) + c.shape, BF16)))
    act, slope, out, up, down = moved_call(
        body, place_table(), (slots,),
        [whole, ((1, 1, part), lambda s, table: (s, 0, 0))] + raw_specs(chunks[0], 0) + raw_specs(chunks[1], 1),
        outs, (low, up_bias, chunks[0], own, received, chunks[1], own, received), "ffn_first",
        flops=ffn_cost(rows, slots * part, width, 2), transcendentals=rows * slots * part * 2,
    )
    return act, slope, out, up.reshape(slots, width, part), down.reshape(slots, part, width)


def ffn_forward(low, up, up_bias, down):
    rows, width = low.shape
    slots, part = up_bias.shape[0], up_bias.shape[2]

    def body(table_ref, low_ref, up_ref, bias_ref, down_ref, act_ref, slope_ref, out_ref):
        ffn_slot(low_ref, up_ref[0], bias_ref, down_ref[0], act_ref, slope_ref, out_ref)

    whole, _, outs = ffn_specs(rows, width, slots, part)
    slot = lambda s, table: (s, 0, 0)
    return moved_call(
        body, jnp.zeros((1,), jnp.int32), (slots,),
        [whole, ((1, width, part), slot), ((1, 1, part), slot), ((1, part, width), slot)],
        outs, (low, up, up_bias, down), "ffn_forward",
        flops=ffn_cost(rows, slots * part, width, 2), transcendentals=rows * slots * part * 2,
    )


def ffn_backward(g_ffn, low, act, slope, up, down, earlier):
    rows, width = low.shape
    slots, part = up.shape[0], up.shape[2]
    n = lax.axis_size("dp")
    fused = bool(earlier) and aligned(width // n) and aligned(part // n)
    half = n // 2

    def body(table_ref, g_ref, low_ref, act_ref, slope_ref, up_ref, down_ref, *refs):
        olds, refs = refs[: len(earlier)], refs[len(earlier) :]
        mid_ref, bias_ref, outs = refs[0], refs[1], refs[2:]
        g = g_ref[...]
        hid = (dot(g, down_ref[0], 1, 1) * slope_ref[...].astype(F32)).astype(BF16)
        bias_ref[0] = jnp.sum(hid.astype(F32), 0, keepdims=True)
        back = dot(hid, up_ref[0], 1, 1)

        @pl.when(pl.program_id(0) == 0)
        def _():
            mid_ref[...] = back

        @pl.when(pl.program_id(0) > 0)
        def _():
            mid_ref[...] += back

        if not olds:
            outs[0][...] = hid
            return
        old_g, old_low, old_act, old_hid = (ref[...] for ref in olds)
        products = ((low_ref[...], hid, old_low, old_hid), (act_ref[...], g, old_act, old_g))
        for i, (left, right, old_left, old_right) in enumerate(products):
            total = dot(left, right, 0, 0) + dot(old_left, old_right, 0, 0)
            if fused:
                keep_ref, send_ref, scratch = outs[2 * i], outs[2 * i + 1], outs[4 + i]
                scratch[...] = total.astype(BF16).reshape(scratch.shape)
                for p in range(half):
                    keep_ref[p, 0] = scratch[table_ref[p]]
                    send_ref[p, 0] = scratch[table_ref[half + p]]
            else:
                outs[i][0] = total.astype(BF16)

    whole, units, _ = ffn_specs(rows, width, slots, part)
    slot = lambda s, table: (s, 0, 0)
    shapes = [(width, part), (part, width)]
    weights = [((1,) + shape, slot) for shape in shapes]
    outs = [
        (whole, jax.ShapeDtypeStruct((rows, width), F32)),
        (((1, 1, part), slot), jax.ShapeDtypeStruct((slots, 1, part), F32)),
    ]
    scratch = []
    if not earlier:
        outs.append((units, jax.ShapeDtypeStruct((rows, slots * part), BF16)))
    for shape, spec in zip(shapes, weights) if earlier else ():
        if fused:
            chunk = (n, shape[0] // n, shape[1])
            outs += packed_outs(slots, *chunk)
            scratch.append(pltpu.VMEM(chunk, BF16))
        else:
            outs.append((spec, jax.ShapeDtypeStruct((slots,) + shape, BF16)))
    got = moved_call(
        body, pack_table(), (slots,),
        [whole, whole, units, units] + weights + ([whole, whole, units, units] if earlier else []),
        outs, (g_ffn, low, act, slope, up, down, *earlier), "ffn_backward", scratch,
        flops=ffn_cost(rows, slots * part, width, 6 if earlier else 2),
    )
    if fused:
        return got[0], got[1], got[2:4], got[4:6]
    if earlier:
        return got[0], got[1], *(pack(d.reshape(slots, n, -1, d.shape[-1])) for d in got[2:])
    return got


def lane_masks(rows):
    lane = lax.broadcasted_iota(jnp.int32, (rows, LANES), 1)
    return [(lane >= h * HEAD_DIM) & (lane < (h + 1) * HEAD_DIM) for h in range(LANES // HEAD_DIM)]


def only(mask, value):
    return jnp.where(mask, value, jnp.zeros_like(value))


def attention_forward(q, k, v, keys):
    rows, width = q.shape
    padded = k.shape[0]
    scale = 1.0 / math.sqrt(HEAD_DIM)

    def body(q_ref, k_ref, v_ref, out_ref, lse_ref):
        q = q_ref[...] * jnp.asarray(scale, BF16)
        k, v = k_ref[...], v_ref[...]
        live = lax.broadcasted_iota(jnp.int32, (1, padded), 1) < keys
        out = jnp.zeros((rows, LANES), F32)
        lses = jnp.zeros((rows, LANES), F32)
        for mine, theirs in zip(lane_masks(rows), lane_masks(padded)):
            scores = jnp.where(live, dot(only(mine, q), k, 1, 1), -jnp.inf)
            top = jnp.max(scores, -1, keepdims=True)
            weights = jnp.exp(scores - top)
            total = jnp.sum(weights, -1, keepdims=True)
            probs = (weights * (1.0 / total)).astype(BF16)
            out = out + dot(probs, only(theirs, v), 1, 0)
            lses = jnp.where(mine, top + jnp.log(total), lses)
        out_ref[...] = out.astype(BF16)
        lse_ref[...] = lses

    q_spec = pl.BlockSpec((rows, LANES), lambda h: (0, h))
    k_spec = pl.BlockSpec((padded, LANES), lambda h: (0, h))
    return pl.pallas_call(
        body,
        grid=(width // LANES,),
        in_specs=[q_spec, k_spec, k_spec],
        out_specs=[q_spec, q_spec],
        out_shape=[jax.ShapeDtypeStruct((rows, width), BF16), jax.ShapeDtypeStruct((rows, width), F32)],
        cost_estimate=cost(8 * rows * padded * width, rows * padded * width // HEAD_DIM, (q, k, v, q, q), ()),
        name="attention_forward",
    )(q, k, v)


def attention_backward(q, k, v, lse, g_att, keys):
    rows, width = q.shape
    padded = k.shape[0]
    scale = 1.0 / math.sqrt(HEAD_DIM)

    def body(q_ref, k_ref, v_ref, lse_ref, g_ref, gq_ref, gk_ref, gv_ref, sum_q_ref, sum_v_ref):
        q, g = q_ref[...] * jnp.asarray(scale, BF16), g_ref[...]
        k, v = k_ref[...], v_ref[...]
        live = lax.broadcasted_iota(jnp.int32, (1, padded), 1) < keys
        gq = jnp.zeros((rows, LANES), F32)
        gk = jnp.zeros((padded, LANES), F32)
        gv = jnp.zeros((padded, LANES), F32)
        for h, (mine, theirs) in enumerate(zip(lane_masks(rows), lane_masks(padded))):
            q_h, g_h = only(mine, q), only(mine, g)
            scores = dot(q_h, k, 1, 1)
            full = jnp.where(live, jnp.exp(scores - lse_ref[:, h * HEAD_DIM : h * HEAD_DIM + 1]), 0.0)
            g_probs = dot(g_h, v, 1, 1)
            inner = jnp.sum(g_probs * full, -1, keepdims=True)
            g_scores = (full * (g_probs - inner)).astype(BF16)
            gq = gq + dot(g_scores, only(theirs, k), 1, 0)
            gk = gk + dot(g_scores, q_h, 0, 0)
            gv = gv + dot(full.astype(BF16), g_h, 0, 0)
        gq = (gq * scale).astype(BF16)
        gv = gv.astype(BF16)
        gq_ref[...] = gq
        gk_ref[...] = gk.astype(BF16)
        gv_ref[...] = gv
        sum_q_ref[...] = jnp.sum(gq.astype(F32), 0, keepdims=True)
        sum_v_ref[...] = jnp.sum(gv.astype(F32), 0, keepdims=True)

    q_spec = pl.BlockSpec((rows, LANES), lambda h: (0, h))
    k_spec = pl.BlockSpec((padded, LANES), lambda h: (0, h))
    sum_spec = pl.BlockSpec((1, LANES), lambda h: (0, h))
    return pl.pallas_call(
        body,
        grid=(width // LANES,),
        in_specs=[q_spec, k_spec, k_spec, q_spec, q_spec],
        out_specs=[q_spec, k_spec, k_spec, sum_spec, sum_spec],
        out_shape=[
            jax.ShapeDtypeStruct((rows, width), BF16),
            jax.ShapeDtypeStruct((padded, width), BF16),
            jax.ShapeDtypeStruct((padded, width), BF16),
            jax.ShapeDtypeStruct((1, width), F32),
            jax.ShapeDtypeStruct((1, width), F32),
        ],
        cost_estimate=cost(20 * rows * padded * width, rows * padded * width // HEAD_DIM, (q, k, v, lse, g_att, q, k, v), ()),
        name="attention_backward",
    )(q, k, v, lse, g_att)


def attention_weights(segments, slots):
    width = segments[0][0].shape[1]
    part = width // slots
    n = lax.axis_size("dp")
    rows = 4 * part // n
    half = n // 2
    fused = aligned(rows)
    swap = other_half_slots()
    operands = [a for segment in segments for a in segment]

    def body(table_ref, *refs):
        out_refs = refs[len(operands) :]
        full = out_refs[-1]
        groups = [refs[i : i + 6] for i in range(0, len(operands), 6)]
        for kind in range(4):
            total = None
            for refs_of in groups:
                left = refs_of[4] if kind == 3 else refs_of[kind]
                right = refs_of[5][...] if kind == 3 else refs_of[3][: left.shape[0], :]
                one = dot(left[...], right, 0, 0)
                total = one if total is None else total + one
            for s in range(slots):
                full[s, kind * part : (kind + 1) * part, :] = total[s * part : (s + 1) * part].astype(BF16)
        if fused:
            for p in range(half):
                mine = pl.ds(pl.multiple_of(table_ref[p] * rows, 16), rows)
                theirs = pl.ds(pl.multiple_of(table_ref[half + p] * rows, 16), rows)
                for s in range(slots):
                    out_refs[0][p, s] = full[s, mine, :]
                    out_refs[1][p, s] = full[swap[s], theirs, :]

    everything = lambda a: (a.shape, lambda i, table: (0,) * len(a.shape))
    packed = jax.ShapeDtypeStruct((half, slots, rows, width), BF16)
    whole = jax.ShapeDtypeStruct((slots, 4 * part, width), BF16)
    shapes = [packed, packed] if fused else [whole]
    got = moved_call(
        body, arrival_sources(), (1,), [everything(a) for a in operands], [(everything(a), a) for a in shapes], operands,
        "attention_weights", [pltpu.VMEM(whole.shape, BF16)] if fused else [],
        flops=sum(2 * a.size * width for a in operands) * 2 // 3,
    )
    return got if fused else pack(got[0].reshape(slots, n, rows, width))


def local(text_in, start_memory, w_qkv, b_qv, w_o, w_up, b_up, w_down, norm_gains, biases, cot_text, cot_memory):
    text, cot_rows, cot_mem = text_in[0], cot_text[0], cot_memory[0]
    text_total, width = text.shape
    mem = start_memory.shape[0]
    seg = text_total // SEGMENTS
    rows = seg + mem
    keys = rows + mem
    padded = -(-keys // LANES) * LANES
    n_t, n_dp = lax.axis_size("tensor"), lax.axis_size("dp")
    head_part = w_qkv.shape[2]
    part = b_up.shape[0]
    t = lax.axis_index("tensor")

    small = jnp.concatenate([b_qv.reshape(-1), b_up])
    small = jnp.pad(small, (0, 8 * width - small.shape[0])).reshape(1, 8, width)
    d = lax.axis_index("dp")
    own_chunk = lambda chunks: lax.dynamic_index_in_dim(chunks, d, 0)
    kinds = jnp.concatenate([w_qkv.transpose(0, 2, 1).reshape(-1, width), w_o]).reshape(n_dp, -1, width)
    chunks = [w_up.reshape(n_dp, -1, part), w_down.reshape(n_dp, -1, width)]
    lined = jnp.concatenate([own_chunk(kinds), small], 1)
    ffn_own = jnp.concatenate([own_chunk(c) for c in chunks], 1)
    grow = lambda exchange, step: lambda value: jnp.concatenate([value, exchange(value, step)])
    grow_line = [grow(line_exchange, step) for step in line_steps()]
    lined = chain(grow_line)(lined)
    rest, ffn_rest = lockstep(
        [lined[None, 1:, : kinds.shape[1]], ffn_own], [[grow(outer_exchange, step) for step in outer_steps()], grow_line]
    )
    small = lined[:, kinds.shape[1] :].reshape(n_t, -1).astype(F32)
    q_bias = small[:, :head_part].reshape(1, -1)
    v_bias = small[:, head_part : 2 * head_part].reshape(1, -1)
    up_bias = small[:, None, 2 * head_part : 2 * head_part + part]
    received = core_exchange(rest)
    ffn_rest = ffn_rest[None, 1:]
    first, *middle, last = outer_steps()
    (q_w, k_w, v_w, o_w), ffn_received = lax.optimization_barrier(
        (place_kinds(kinds, rest, received), outer_exchange(ffn_rest, first))
    )
    ffn_rest = gather_outer(jnp.concatenate([ffn_rest, ffn_received]), middle)

    read = start_memory
    kept, pieces = [], []
    for s in range(SEGMENTS):
        x = jnp.concatenate([text[s * seg : (s + 1) * seg], start_memory, read, jnp.zeros((padded - keys, width), BF16)])
        q = (dot(x[:rows], q_w, 1, 1) + q_bias).astype(BF16)
        k = dot(x, k_w, 1, 1).astype(BF16)
        v = (dot(x, v_w, 1, 1) + v_bias).astype(BF16)
        att, lse = attention_forward(q, k, v, keys)
        if s == 0:
            att, ffn_received = lax.optimization_barrier((att, outer_exchange(ffn_rest, last)))
            ffn_rest = jnp.concatenate([ffn_rest, ffn_received])
        n1, r1 = norm_stats(x[:rows].astype(F32) + dot(att, o_w, 1, 0) + biases[0])
        middle = n1 * norm_gains[0] + biases[1]
        low = middle.astype(BF16)
        if s == 0:
            act, slope, ffn, up_full, down_full = ffn_first(low, up_bias, chunks, ffn_rest, core_exchange(ffn_rest))
        else:
            act, slope, ffn = ffn_forward(low, up_full, up_bias, down_full)
        n2, r2 = norm_stats(middle + ffn + biases[2])
        result = (n2 * norm_gains[1] + biases[3]).astype(BF16)
        pieces.append(result[:seg])
        read = result[seg:]
        kept.append((x, q, k, v, lse, att, n1, r1, low, act, slope, n2, r2))

    segments, sums, ends = [], [], []
    carry = cot_mem.astype(F32)
    d_text = [None] * SEGMENTS
    outers, lines = reduce_steps()
    earlier = ()
    for s in reversed(range(SEGMENTS)):
        x, q, k, v, lse, att, n1, r1, low, act, slope, n2, r2 = kept[s]
        g_res = jnp.concatenate([cot_rows[s * seg : (s + 1) * seg].astype(F32), carry])
        g_pre2 = norm_backward(g_res, n2, r2, norm_gains[1])
        g_ffn = g_pre2.astype(BF16)
        g_mid, g_bup, *got = ffn_backward(g_ffn, low, act, slope, up_full, down_full, earlier)
        if s == 0:
            d_up, d_down = got
        else:
            earlier = (g_ffn, low, act, got[0])
        g_mid = g_mid + g_pre2
        g_pre1 = norm_backward(g_mid, n1, r1, norm_gains[0])
        g_attn = g_pre1.astype(BF16)
        g_att = dot(g_attn, o_w, 1, 1).astype(BF16)
        if s == 0:
            g_att, total_up = lax.optimization_barrier((g_att, core_step(d_up)))
            total_up, total_down = outers[0](total_up), core_step(d_down)
        g_q, g_k, g_v, sum_q, sum_v = attention_backward(q, k, v, lse, g_att, keys)
        if s == 0:
            (g_q, g_k, g_v), total_up, total_down = lax.optimization_barrier(((g_q, g_k, g_v), total_up, total_down))
            total_up, total_down = chain(outers[1:])(total_up), outers[0](total_down)
        segments.append((g_q, g_k, g_v, x, att, g_attn))
        g_x = dot(g_k, k_w, 1, 0) + dot(g_v, v_w, 1, 0)
        top = g_x[:rows] + dot(g_q, q_w, 1, 0) + g_pre1
        d_text[s] = top[:seg]
        carry = g_x[rows:keys]
        ends += [top[seg:]] if s > 0 else [top[seg:], carry]
        over = lambda value: jnp.sum(value, 0, keepdims=True)
        sums.append(
            [over(g_mid * n1), over(g_res * n2), over(g_pre1), over(g_mid), over(g_pre2), over(g_res)]
            + [sum_q, sum_v, g_bup[:, 0]]
        )

    packed = attention_weights(segments, n_t)
    packed, total_up, total_down = lax.optimization_barrier((packed, total_up, total_down))
    total, total_down = lockstep([packed, total_down], [[core_step], [chain(outers[1:])]])
    total, sums, ends = lax.optimization_barrier((total, sums, ends))
    sums = [a + b for a, b in zip(*sums)]
    pick = (jnp.arange(n_t)[:, None] == t ^ slot_masks()[0]).astype(F32)
    by_slot = jnp.concatenate([sums[6].reshape(n_t, -1), sums[7].reshape(n_t, -1), sums[8]], 1)
    by_index = jnp.dot(pick, by_slot, precision=lax.Precision.HIGHEST)
    d_mem = sum(ends[1:], ends[0])
    vectors = jnp.concatenate(
        sums[:6] + [d_mem]
        + [by_index[:, i * head_part : (i + 1) * head_part].reshape(1, width) for i in (0, 1)]
        + [by_index[:, 2 * head_part :].reshape(-1, width)]
    )
    spread = [grow(outer_exchange, step) for step in outer_steps()]
    smalls = small_steps()
    ffn = jnp.concatenate([total_up, total_down], 2)
    merge = lambda value: value.reshape(1, -1, width)
    main = outers + lines
    per = -(-len(smalls) // (len(main) - 1))
    total, ffn, vectors = lockstep(
        [total, ffn, vectors],
        [
            main,
            lines + [chain([merge] + spread[:1])] + spread[1:],
            [None] + [chain(smalls[i : i + per]) for i in range(0, len(smalls), per)],
        ],
    )
    g_bqv = lax.dynamic_slice_in_dim(vectors[6 + mem : 8 + mem], t * head_part, head_part, 1)
    g_bup = lax.dynamic_slice_in_dim(vectors[8 + mem :].reshape(n_t, -1), t, 1, 0)[0]
    total = merge(total)
    total, ffn_received = lax.optimization_barrier((spread[0](total), core_exchange(ffn)))
    g_up, g_down = (a.reshape(-1, width) for a in finish(ffn, ffn_received, 2))
    total, g_up, g_down, g_bqv, g_bup = lax.optimization_barrier((chain(spread[1:])(total), g_up, g_down, g_bqv, g_bup))
    g_qkv, g_out = finish_kinds(total, core_exchange(total), head_part)
    g_qkv = g_qkv.transpose(0, 2, 1)

    return (
        jnp.concatenate(pieces)[None],
        read[None],
        jnp.concatenate(d_text)[None],
        vectors[6 : 6 + mem],
        g_qkv,
        g_bqv,
        g_out,
        g_up,
        g_bup,
        g_down,
        vectors[:2],
        vectors[2:6],
    )


def solution(mesh):
    own = P(("dp", "tensor"), None, None)
    return jax.shard_map(
        local,
        mesh=mesh,
        in_specs=(
            own, P(), P(None, None, "tensor"), P(None, "tensor"), P("tensor", None), P(None, "tensor"),
            P("tensor"), P("tensor", None), P(), P(), own, own,
        ),
        out_specs=(
            own, own, own, P(), P(None, None, "tensor"), P(None, "tensor"), P("tensor", None),
            P(None, "tensor"), P("tensor"), P("tensor", None), P(), P(),
        ),
        check_vma=False,
    )
```

```python
import math

import jax
import jax.numpy as jnp
from jax import lax
from jax.experimental import pallas as pl
from jax.experimental.pallas import tpu as pltpu
from jax.sharding import PartitionSpec as P

HEAD_DIM = 64
SEGMENTS = 2
EPSILON = 1e-06
LANES = 128
F32 = jnp.float32
BF16 = jnp.bfloat16


def dot(a, b, ca, cb):
    return lax.dot_general(a, b, (((ca,), (cb,)), ((), ())), preferred_element_type=F32)


def norm_stats(value):
    centred = value - jnp.mean(value, -1, keepdims=True)
    rstd = lax.rsqrt(jnp.mean(centred * centred, -1, keepdims=True) + EPSILON)
    return centred * rstd, rstd


def norm_backward(grad_out, normed, rstd, gain):
    scaled = grad_out * gain
    first = jnp.mean(scaled, -1, keepdims=True)
    second = jnp.mean(scaled * normed, -1, keepdims=True)
    return rstd * (scaled - first - normed * second)


def log2(n):
    return n.bit_length() - 1


def outer_mask(core, step):
    outer = log2(lax.axis_size("dp")) - 1
    return 2 << (step if core == 0 else outer - 1 - step)


def outer_exchange(value, step):
    pairs = [(i, i ^ outer_mask(i & 1, step)) for i in range(lax.axis_size("dp"))]
    return lax.ppermute(value, "dp", pairs)


def core_exchange(value):
    return lax.ppermute(value, "dp", [(i, i ^ 1) for i in range(lax.axis_size("dp"))])


def line_exchange(value, step):
    n = lax.axis_size("tensor")
    pairs = []
    for i in range(lax.axis_size("dp")):
        mask = 1 << (step if i & 1 == 0 else log2(n) - 1 - step)
        pairs += [(i * n + t, i * n + (t ^ mask)) for t in range(n)]
    return lax.ppermute(value, ("dp", "tensor"), pairs)


def outer_steps():
    return range(log2(lax.axis_size("dp")) - 1)


def line_steps():
    return range(log2(lax.axis_size("tensor")))


def arrival_sources():
    half = lax.axis_size("dp") // 2
    tables = [
        jnp.array([sum(outer_mask(core, i) for i in outer_steps() if j >> i & 1) for j in range(half)], jnp.int32)
        for core in (0, 1)
    ]
    d = lax.axis_index("dp")
    core = d % 2
    mine = jnp.where(core == 0, tables[0], tables[1])
    theirs = jnp.where(core == 0, tables[1], tables[0])
    return jnp.concatenate([d ^ mine, d ^ 1 ^ theirs])


def slot_masks():
    n = lax.axis_size("tensor")
    orders = []
    for flip in (False, True):
        places = [log2(n) - 1 - i if flip else i for i in line_steps()]
        orders.append(jnp.array([sum(1 << places[i] for i in line_steps() if s >> i & 1) for s in range(n)], jnp.int32))
    core = lax.axis_index("dp") % 2
    return jnp.where(core == 0, orders[0], orders[1]), jnp.where(core == 0, orders[1], orders[0])


def other_half_slots():
    n = lax.axis_size("tensor")
    return [sum(1 << (log2(n) - 1 - i) for i in line_steps() if s >> i & 1) for s in range(n)]


def cost(flops, transcendentals, operands, shapes):
    moved = sum(a.size * a.dtype.itemsize for a in list(operands) + list(shapes))
    return pl.CostEstimate(flops=flops, transcendentals=transcendentals, bytes_accessed=moved)


def moved_call(body, table, grid, ins, outs, operands, name, scratch=(), flops=0, transcendentals=0):
    shapes = [shape for _, shape in outs]
    return pl.pallas_call(
        body,
        grid_spec=pltpu.PrefetchScalarGridSpec(
            num_scalar_prefetch=1,
            grid=grid,
            in_specs=[pl.BlockSpec(*spec) for spec in ins],
            out_specs=[pl.BlockSpec(*spec) for spec, _ in outs],
            scratch_shapes=list(scratch),
        ),
        out_shape=shapes,
        cost_estimate=cost(flops, transcendentals, operands, shapes),
        name=name,
    )(table, *operands)


def aligned(rows):
    return rows % 16 == 0


def place_table():
    return jnp.concatenate([arrival_sources(), jnp.array([max(s - 1, 0) for s in other_half_slots()], jnp.int32)])


def pack_table():
    return jnp.concatenate([arrival_sources(), jnp.array(other_half_slots(), jnp.int32)])


def raw_specs(chunks, at=0):
    n, rows, width = chunks.shape
    block = (n // 2, 1, rows, width)
    return [
        ((n, rows, width), lambda s, table: (0, 0, 0)),
        (block, lambda s, table: (0, jnp.maximum(s - 1, 0), at, 0)),
        (block, lambda s, table: (0, table[n + s], at, 0)),
    ]


def settle(table_ref, chunks_ref, own_ref, received_ref, out):
    half = own_ref.shape[0]

    @pl.when(pl.program_id(0) == 0)
    def _():
        out[...] = chunks_ref[...]

    @pl.when(pl.program_id(0) > 0)
    def _():
        for p in range(half):
            out[table_ref[p]] = own_ref[p, 0]
            out[table_ref[half + p]] = received_ref[p, 0]


def packed_outs(slots, n, rows, width):
    shape = jax.ShapeDtypeStruct((n // 2, slots, rows, width), BF16)
    block = (n // 2, 1, rows, width)
    return [
        ((block, lambda s, table: (0, s, 0, 0)), shape),
        ((block, lambda s, table: (0, table[n + s], 0, 0)), shape),
    ]


def place(chunks, own, received):
    others = own.shape[1]
    swap = other_half_slots()
    received = jnp.stack([received[:, swap[s] - 1] for s in range(1, others + 1)], 1)
    moved = jnp.concatenate([own, received])[jnp.argsort(arrival_sources())]
    return jnp.concatenate([chunks[None], moved.transpose(1, 0, 2, 3)])


def pack(total):
    half = total.shape[1] // 2
    moved = total.transpose(1, 0, 2, 3)[arrival_sources()]
    return moved[:half], jnp.stack([moved[half:, s] for s in other_half_slots()], 1)


def finish(own, received, count):
    half, rows, width = own.shape
    rows = rows // count
    source = arrival_sources()
    if not aligned(rows):
        full = jnp.concatenate([own, received])[jnp.argsort(source)].astype(F32)
        return [full[:, i * rows : (i + 1) * rows] for i in range(count)]

    def body(table_ref, own_ref, received_ref, *out_refs):
        for p in range(half):
            for i, out_ref in enumerate(out_refs):
                at = slice(i * rows, (i + 1) * rows)
                out_ref[table_ref[p]] = own_ref[p, at].astype(F32)
                out_ref[table_ref[half + p]] = received_ref[p, at].astype(F32)

    whole = (own.shape, lambda i, table: (0, 0, 0))
    shape = (2 * half, rows, width)
    out = ((shape, lambda i, table: (0, 0, 0)), jax.ShapeDtypeStruct(shape, F32))
    return moved_call(body, source, (1,), [whole, whole], [out] * count, (own, received), "finish")


def finish_kinds(own, received, head_part):
    half, rows, width = own.shape
    n = 2 * half
    if not aligned(rows):
        full = finish(own, received, 1)[0].reshape(4, head_part, width)
        return full[:3], full[3]

    def body(table_ref, own_ref, received_ref, qkv_ref, out_ref, scratch):
        for p in range(half):
            scratch[table_ref[p]] = own_ref[p].astype(F32)
            scratch[table_ref[half + p]] = received_ref[p].astype(F32)
        full = scratch[...].reshape(n * rows, width)
        for i in range(3):
            qkv_ref[i] = full[i * head_part : (i + 1) * head_part]
        out_ref[...] = full[3 * head_part :]

    whole = (own.shape, lambda i, table: (0, 0, 0))
    shapes = [(3, head_part, width), (head_part, width)]
    outs = [
        ((shape, lambda i, table, rank=len(shape): (0,) * rank), jax.ShapeDtypeStruct(shape, F32)) for shape in shapes
    ]
    return moved_call(
        body, arrival_sources(), (1,), [whole, whole], outs, (own, received), "finish_kinds",
        [pltpu.VMEM((n, rows, width), F32)],
    )


def place_kinds(chunks, own, received):
    n, rows, width = chunks.shape
    slots = own.shape[1] + 1
    part = n * rows // 4
    if not (aligned(rows) and aligned(part)):
        full = place(chunks, own, received).reshape(slots, 4, part, width)
        return [full[:, i].reshape(-1, width) for i in range(4)]

    def body(table_ref, chunks_ref, own_ref, received_ref, *refs):
        settle(table_ref, chunks_ref, own_ref, received_ref, refs[-1])
        full = refs[-1][...].reshape(n * rows, width)
        for i in range(4):
            refs[i][...] = full[i * part : (i + 1) * part]

    out = (((part, width), lambda s, table: (s, 0)), jax.ShapeDtypeStruct((slots * part, width), BF16))
    return moved_call(
        body, place_table(), (slots,), raw_specs(chunks), [out] * 4, (chunks, own, received), "place_kinds",
        [pltpu.VMEM((n, rows, width), BF16)],
    )


def gather_outer(rest, steps):
    for step in steps:
        rest = jnp.concatenate([rest, outer_exchange(rest, step)])
    return rest


def plus(a, b):
    return (a.astype(F32) + b.astype(F32)).astype(BF16)


def core_step(packed):
    return plus(packed[0], core_exchange(packed[1]))


def reduce_steps():
    def outer(step):
        def run(total):
            half = total.shape[0] // 2
            return plus(total[:half], outer_exchange(total[half:], step))

        return run

    def line(step):
        def run(total):
            half = total.shape[1] // 2
            return plus(total[:, :half], line_exchange(total[:, half:], step))

        return run

    return [outer(step) for step in reversed(outer_steps())], [line(step) for step in reversed(line_steps())]


def small_steps():
    def run(axis, bit):
        return lambda value: value + lax.ppermute(value, axis, [(i, i ^ bit) for i in range(lax.axis_size(axis))])

    return [run(axis, 1 << i) for axis in ("dp", "tensor") for i in range(log2(lax.axis_size(axis)))]


def chain(steps):
    def run(value):
        for step in steps:
            value = step(value)
        return value

    return run


def lockstep(values, chains):
    for stage in range(max(len(chain) for chain in chains)):
        values = [
            chain[stage](value) if stage < len(chain) and chain[stage] else value
            for value, chain in zip(values, chains)
        ]
        values = lax.optimization_barrier(values)
    return values


def ffn_cost(rows, hidden, width, products):
    return 2 * rows * hidden * width * products


def ffn_slot(low_ref, up, bias_ref, down, act_ref, slope_ref, out_ref):
    @pl.when(pl.program_id(0) == 0)
    def _():
        out_ref[...] = jnp.zeros_like(out_ref)

    step = low_ref.shape[0] // 4
    for i in range(4):
        at = slice(i * step, (i + 1) * step)
        hidden = dot(low_ref[at, :], up, 1, 0) + bias_ref[0]
        cdf = 0.5 * (1.0 + lax.erf(hidden * math.sqrt(0.5)))
        act = (hidden * cdf).astype(BF16)
        act_ref[0, at, :] = act
        pdf = jnp.exp(hidden * hidden * -0.5) * (1.0 / math.sqrt(2.0 * math.pi))
        slope_ref[0, at, :] = (cdf + hidden * pdf).astype(BF16)
        out_ref[at, :] += dot(act, down, 1, 0)


def ffn_specs(rows, width, slots, part):
    whole = ((rows, width), lambda s, table: (0, 0))
    units = ((1, rows, part), lambda s, table: (s, 0, 0))
    shape = jax.ShapeDtypeStruct((slots, rows, part), BF16)
    return whole, units, [(units, shape), (units, shape), (whole, jax.ShapeDtypeStruct((rows, width), F32))]


def ffn_first(low, up_bias, chunks, own, received):
    rows, width = low.shape
    slots, part = up_bias.shape[0], up_bias.shape[2]
    count = chunks[0].shape[1]
    if not aligned(count):
        up, down = (place(c, *(h[:, :, i * count : (i + 1) * count] for h in (own, received))) for i, c in enumerate(chunks))
        up, down = up.reshape(slots, width, part), down.reshape(slots, part, width)
        return (*ffn_forward(low, up, up_bias, down), up, down)

    def body(table_ref, low_ref, bias_ref, *refs):
        up_refs, down_refs, (act_ref, slope_ref, out_ref, up_ref, down_ref) = refs[:3], refs[3:6], refs[6:]
        settle(table_ref, *up_refs, up_ref.at[0])
        settle(table_ref, *down_refs, down_ref.at[0])
        up, down = up_ref[0].reshape(width, part), down_ref[0].reshape(part, width)
        ffn_slot(low_ref, up, bias_ref, down, act_ref, slope_ref, out_ref)

    whole, _, outs = ffn_specs(rows, width, slots, part)
    for c in chunks:
        outs.append((((1,) + c.shape, lambda s, table: (s, 0, 0, 0)), jax.ShapeDtypeStruct((slots,) + c.shape, BF16)))
    act, slope, out, up, down = moved_call(
        body, place_table(), (slots,),
        [whole, ((1, 1, part), lambda s, table: (s, 0, 0))] + raw_specs(chunks[0], 0) + raw_specs(chunks[1], 1),
        outs, (low, up_bias, chunks[0], own, received, chunks[1], own, received), "ffn_first",
        flops=ffn_cost(rows, slots * part, width, 2), transcendentals=rows * slots * part * 2,
    )
    return act, slope, out, up.reshape(slots, width, part), down.reshape(slots, part, width)


def ffn_forward(low, up, up_bias, down):
    rows, width = low.shape
    slots, part = up_bias.shape[0], up_bias.shape[2]

    def body(table_ref, low_ref, up_ref, bias_ref, down_ref, act_ref, slope_ref, out_ref):
        ffn_slot(low_ref, up_ref[0], bias_ref, down_ref[0], act_ref, slope_ref, out_ref)

    whole, _, outs = ffn_specs(rows, width, slots, part)
    slot = lambda s, table: (s, 0, 0)
    return moved_call(
        body, jnp.zeros((1,), jnp.int32), (slots,),
        [whole, ((1, width, part), slot), ((1, 1, part), slot), ((1, part, width), slot)],
        outs, (low, up, up_bias, down), "ffn_forward",
        flops=ffn_cost(rows, slots * part, width, 2), transcendentals=rows * slots * part * 2,
    )


def ffn_backward(g_ffn, low, act, slope, up, down, earlier):
    rows, width = low.shape
    slots, part = up.shape[0], up.shape[2]
    n = lax.axis_size("dp")
    fused = bool(earlier) and aligned(width // n) and aligned(part // n)
    half = n // 2
    old_operands = (low, act, *earlier) if earlier else ()

    def body(table_ref, g_ref, slope_ref, up_ref, down_ref, *refs):
        olds, refs = refs[: len(old_operands)], refs[len(old_operands) :]
        mid_ref, bias_ref, outs = refs[0], refs[1], refs[2:]
        g = g_ref[...]
        hid = (dot(g, down_ref[0], 1, 1) * slope_ref[0].astype(F32)).astype(BF16)
        bias_ref[0] = jnp.sum(hid.astype(F32), 0, keepdims=True)
        back = dot(hid, up_ref[0], 1, 1)

        @pl.when(pl.program_id(0) == 0)
        def _():
            mid_ref[...] = back

        @pl.when(pl.program_id(0) > 0)
        def _():
            mid_ref[...] += back

        if not olds:
            outs[0][0] = hid
            return
        low, act, old_g, old_low, old_act, old_hid = olds
        products = (
            (low[...], hid, old_low[...], old_hid[0]),
            (act[0], g, old_act[0], old_g[...]),
        )
        for i, (left, right, old_left, old_right) in enumerate(products):
            total = dot(left, right, 0, 0) + dot(old_left, old_right, 0, 0)
            if fused:
                keep_ref, send_ref, scratch = outs[2 * i], outs[2 * i + 1], outs[4 + i]
                scratch[...] = total.astype(BF16).reshape(scratch.shape)
                for p in range(half):
                    keep_ref[p, 0] = scratch[table_ref[p]]
                    send_ref[p, 0] = scratch[table_ref[half + p]]
            else:
                outs[i][0] = total.astype(BF16)

    whole, units, _ = ffn_specs(rows, width, slots, part)
    slot = lambda s, table: (s, 0, 0)
    shapes = [(width, part), (part, width)]
    weights = [((1,) + shape, slot) for shape in shapes]
    outs = [
        (whole, jax.ShapeDtypeStruct((rows, width), F32)),
        (((1, 1, part), slot), jax.ShapeDtypeStruct((slots, 1, part), F32)),
    ]
    scratch = []
    if not earlier:
        outs.append((units, jax.ShapeDtypeStruct((slots, rows, part), BF16)))
    for shape, spec in zip(shapes, weights) if earlier else ():
        if fused:
            chunk = (n, shape[0] // n, shape[1])
            outs += packed_outs(slots, *chunk)
            scratch.append(pltpu.VMEM(chunk, BF16))
        else:
            outs.append((spec, jax.ShapeDtypeStruct((slots,) + shape, BF16)))
    got = moved_call(
        body, pack_table(), (slots,),
        [whole, units] + weights + ([whole, units, whole, whole, units, units] if earlier else []),
        outs, (g_ffn, slope, up, down, *old_operands), "ffn_backward", scratch,
        flops=ffn_cost(rows, slots * part, width, 6 if earlier else 2),
    )
    if fused:
        return got[0], got[1], got[2:4], got[4:6]
    if earlier:
        return got[0], got[1], *(pack(d.reshape(slots, n, -1, d.shape[-1])) for d in got[2:])
    return got


def lane_masks(rows):
    lane = lax.broadcasted_iota(jnp.int32, (rows, LANES), 1)
    return [(lane >= h * HEAD_DIM) & (lane < (h + 1) * HEAD_DIM) for h in range(LANES // HEAD_DIM)]


def only(mask, value):
    return jnp.where(mask, value, jnp.zeros_like(value))


def attention_forward(q, k, v, keys):
    rows, width = q.shape
    padded = k.shape[0]
    scale = 1.0 / math.sqrt(HEAD_DIM)

    def body(q_ref, k_ref, v_ref, out_ref, lse_ref):
        q = q_ref[...] * jnp.asarray(scale, BF16)
        k, v = k_ref[...], v_ref[...]
        live = lax.broadcasted_iota(jnp.int32, (1, padded), 1) < keys
        out = jnp.zeros((rows, LANES), F32)
        lses = jnp.zeros((rows, LANES), F32)
        for mine, theirs in zip(lane_masks(rows), lane_masks(padded)):
            scores = jnp.where(live, dot(only(mine, q), k, 1, 1), -jnp.inf)
            top = jnp.max(scores, -1, keepdims=True)
            weights = jnp.exp(scores - top)
            total = jnp.sum(weights, -1, keepdims=True)
            probs = (weights * (1.0 / total)).astype(BF16)
            out = out + dot(probs, only(theirs, v), 1, 0)
            lses = jnp.where(mine, top + jnp.log(total), lses)
        out_ref[...] = out.astype(BF16)
        lse_ref[...] = lses

    q_spec = pl.BlockSpec((rows, LANES), lambda h: (0, h))
    k_spec = pl.BlockSpec((padded, LANES), lambda h: (0, h))
    return pl.pallas_call(
        body,
        grid=(width // LANES,),
        in_specs=[q_spec, k_spec, k_spec],
        out_specs=[q_spec, q_spec],
        out_shape=[jax.ShapeDtypeStruct((rows, width), BF16), jax.ShapeDtypeStruct((rows, width), F32)],
        cost_estimate=cost(8 * rows * padded * width, rows * padded * width // HEAD_DIM, (q, k, v, q, q), ()),
        name="attention_forward",
    )(q, k, v)


def attention_backward(q, k, v, lse, g_att, keys):
    rows, width = q.shape
    padded = k.shape[0]
    scale = 1.0 / math.sqrt(HEAD_DIM)

    def body(q_ref, k_ref, v_ref, lse_ref, g_ref, gq_ref, gk_ref, gv_ref, sum_q_ref, sum_v_ref):
        q, g = q_ref[...] * jnp.asarray(scale, BF16), g_ref[...]
        k, v = k_ref[...], v_ref[...]
        live = lax.broadcasted_iota(jnp.int32, (1, padded), 1) < keys
        gq = jnp.zeros((rows, LANES), F32)
        gk = jnp.zeros((padded, LANES), F32)
        gv = jnp.zeros((padded, LANES), F32)
        for h, (mine, theirs) in enumerate(zip(lane_masks(rows), lane_masks(padded))):
            q_h, g_h = only(mine, q), only(mine, g)
            scores = dot(q_h, k, 1, 1)
            full = jnp.where(live, jnp.exp(scores - lse_ref[:, h * HEAD_DIM : h * HEAD_DIM + 1]), 0.0)
            g_probs = dot(g_h, v, 1, 1)
            inner = jnp.sum(g_probs * full, -1, keepdims=True)
            g_scores = (full * (g_probs - inner)).astype(BF16)
            gq = gq + dot(g_scores, only(theirs, k), 1, 0)
            gk = gk + dot(g_scores, q_h, 0, 0)
            gv = gv + dot(full.astype(BF16), g_h, 0, 0)
        gq = (gq * scale).astype(BF16)
        gv = gv.astype(BF16)
        gq_ref[...] = gq
        gk_ref[...] = gk.astype(BF16)
        gv_ref[...] = gv
        sum_q_ref[...] = jnp.sum(gq.astype(F32), 0, keepdims=True)
        sum_v_ref[...] = jnp.sum(gv.astype(F32), 0, keepdims=True)

    q_spec = pl.BlockSpec((rows, LANES), lambda h: (0, h))
    k_spec = pl.BlockSpec((padded, LANES), lambda h: (0, h))
    sum_spec = pl.BlockSpec((1, LANES), lambda h: (0, h))
    return pl.pallas_call(
        body,
        grid=(width // LANES,),
        in_specs=[q_spec, k_spec, k_spec, q_spec, q_spec],
        out_specs=[q_spec, k_spec, k_spec, sum_spec, sum_spec],
        out_shape=[
            jax.ShapeDtypeStruct((rows, width), BF16),
            jax.ShapeDtypeStruct((padded, width), BF16),
            jax.ShapeDtypeStruct((padded, width), BF16),
            jax.ShapeDtypeStruct((1, width), F32),
            jax.ShapeDtypeStruct((1, width), F32),
        ],
        cost_estimate=cost(20 * rows * padded * width, rows * padded * width // HEAD_DIM, (q, k, v, lse, g_att, q, k, v), ()),
        name="attention_backward",
    )(q, k, v, lse, g_att)


def attention_weights(segments, slots):
    width = segments[0][0].shape[1]
    part = width // slots
    n = lax.axis_size("dp")
    rows = 4 * part // n
    half = n // 2
    fused = aligned(rows)
    swap = other_half_slots()
    operands = [a for segment in segments for a in segment]

    def body(table_ref, *refs):
        out_refs = refs[len(operands) :]
        full = out_refs[-1]
        groups = [refs[i : i + 6] for i in range(0, len(operands), 6)]
        for kind in range(4):
            total = None
            for refs_of in groups:
                left = refs_of[4] if kind == 3 else refs_of[kind]
                right = refs_of[5][...] if kind == 3 else refs_of[3][: left.shape[0], :]
                one = dot(left[...], right, 0, 0)
                total = one if total is None else total + one
            for s in range(slots):
                full[s, kind * part : (kind + 1) * part, :] = total[s * part : (s + 1) * part].astype(BF16)
        if fused:
            for p in range(half):
                mine = pl.ds(pl.multiple_of(table_ref[p] * rows, 16), rows)
                theirs = pl.ds(pl.multiple_of(table_ref[half + p] * rows, 16), rows)
                for s in range(slots):
                    out_refs[0][p, s] = full[s, mine, :]
                    out_refs[1][p, s] = full[swap[s], theirs, :]

    everything = lambda a: (a.shape, lambda i, table: (0,) * len(a.shape))
    packed = jax.ShapeDtypeStruct((half, slots, rows, width), BF16)
    whole = jax.ShapeDtypeStruct((slots, 4 * part, width), BF16)
    shapes = [packed, packed] if fused else [whole]
    got = moved_call(
        body, arrival_sources(), (1,), [everything(a) for a in operands], [(everything(a), a) for a in shapes], operands,
        "attention_weights", [pltpu.VMEM(whole.shape, BF16)] if fused else [],
        flops=sum(2 * a.size * width for a in operands) * 2 // 3,
    )
    return got if fused else pack(got[0].reshape(slots, n, rows, width))


def local(text_in, start_memory, w_qkv, b_qv, w_o, w_up, b_up, w_down, norm_gains, biases, cot_text, cot_memory):
    text, cot_rows, cot_mem = text_in[0], cot_text[0], cot_memory[0]
    text_total, width = text.shape
    mem = start_memory.shape[0]
    seg = text_total // SEGMENTS
    rows = seg + mem
    keys = rows + mem
    padded = -(-keys // LANES) * LANES
    n_t, n_dp = lax.axis_size("tensor"), lax.axis_size("dp")
    head_part = w_qkv.shape[2]
    part = b_up.shape[0]
    t = lax.axis_index("tensor")

    small = jnp.concatenate([b_qv.reshape(-1), b_up])
    small = jnp.pad(small, (0, 8 * width - small.shape[0])).reshape(1, 8, width)
    d = lax.axis_index("dp")
    own_chunk = lambda chunks: lax.dynamic_index_in_dim(chunks, d, 0)
    kinds = jnp.concatenate([w_qkv.transpose(0, 2, 1).reshape(-1, width), w_o]).reshape(n_dp, -1, width)
    chunks = [w_up.reshape(n_dp, -1, part), w_down.reshape(n_dp, -1, width)]
    lined = jnp.concatenate([own_chunk(kinds), small], 1)
    ffn_own = jnp.concatenate([own_chunk(c) for c in chunks], 1)
    grow = lambda exchange, step: lambda value: jnp.concatenate([value, exchange(value, step)])
    grow_line = [grow(line_exchange, step) for step in line_steps()]
    lined = chain(grow_line)(lined)
    rest, ffn_rest = lockstep(
        [lined[None, 1:, : kinds.shape[1]], ffn_own], [[grow(outer_exchange, step) for step in outer_steps()], grow_line]
    )
    small = lined[:, kinds.shape[1] :].reshape(n_t, -1).astype(F32)
    q_bias = small[:, :head_part].reshape(1, -1)
    v_bias = small[:, head_part : 2 * head_part].reshape(1, -1)
    up_bias = small[:, None, 2 * head_part : 2 * head_part + part]
    received = core_exchange(rest)
    ffn_rest = ffn_rest[None, 1:]
    first, *middle, last = outer_steps()
    (q_w, k_w, v_w, o_w), ffn_received = lax.optimization_barrier(
        (place_kinds(kinds, rest, received), outer_exchange(ffn_rest, first))
    )
    ffn_rest = gather_outer(jnp.concatenate([ffn_rest, ffn_received]), middle)

    read = start_memory
    kept, pieces = [], []
    for s in range(SEGMENTS):
        x = jnp.concatenate([text[s * seg : (s + 1) * seg], start_memory, read, jnp.zeros((padded - keys, width), BF16)])
        q = (dot(x[:rows], q_w, 1, 1) + q_bias).astype(BF16)
        k = dot(x, k_w, 1, 1).astype(BF16)
        v = (dot(x, v_w, 1, 1) + v_bias).astype(BF16)
        att, lse = attention_forward(q, k, v, keys)
        if s == 0:
            att, ffn_received = lax.optimization_barrier((att, outer_exchange(ffn_rest, last)))
            ffn_rest = jnp.concatenate([ffn_rest, ffn_received])
        n1, r1 = norm_stats(x[:rows].astype(F32) + dot(att, o_w, 1, 0) + biases[0])
        middle = n1 * norm_gains[0] + biases[1]
        low = middle.astype(BF16)
        if s == 0:
            act, slope, ffn, up_full, down_full = ffn_first(low, up_bias, chunks, ffn_rest, core_exchange(ffn_rest))
        else:
            act, slope, ffn = ffn_forward(low, up_full, up_bias, down_full)
        n2, r2 = norm_stats(middle + ffn + biases[2])
        result = (n2 * norm_gains[1] + biases[3]).astype(BF16)
        pieces.append(result[:seg])
        read = result[seg:]
        kept.append((x, q, k, v, lse, att, n1, r1, low, act, slope, n2, r2))

    segments, sums, ends = [], [], []
    carry = cot_mem.astype(F32)
    d_text = [None] * SEGMENTS
    outers, lines = reduce_steps()
    earlier = ()
    for s in reversed(range(SEGMENTS)):
        x, q, k, v, lse, att, n1, r1, low, act, slope, n2, r2 = kept[s]
        g_res = jnp.concatenate([cot_rows[s * seg : (s + 1) * seg].astype(F32), carry])
        g_pre2 = norm_backward(g_res, n2, r2, norm_gains[1])
        g_ffn = g_pre2.astype(BF16)
        g_mid, g_bup, *got = ffn_backward(g_ffn, low, act, slope, up_full, down_full, earlier)
        if s == 0:
            d_up, d_down = got
        else:
            earlier = (g_ffn, low, act, got[0])
        g_mid = g_mid + g_pre2
        g_pre1 = norm_backward(g_mid, n1, r1, norm_gains[0])
        g_attn = g_pre1.astype(BF16)
        g_att = dot(g_attn, o_w, 1, 1).astype(BF16)
        if s == 0:
            g_att, total_up = lax.optimization_barrier((g_att, core_step(d_up)))
            total_up, total_down = outers[0](total_up), core_step(d_down)
        g_q, g_k, g_v, sum_q, sum_v = attention_backward(q, k, v, lse, g_att, keys)
        if s == 0:
            (g_q, g_k, g_v), total_up, total_down = lax.optimization_barrier(((g_q, g_k, g_v), total_up, total_down))
            total_up, total_down = chain(outers[1:])(total_up), outers[0](total_down)
        segments.append((g_q, g_k, g_v, x, att, g_attn))
        g_x = dot(g_k, k_w, 1, 0) + dot(g_v, v_w, 1, 0)
        top = g_x[:rows] + dot(g_q, q_w, 1, 0) + g_pre1
        d_text[s] = top[:seg]
        carry = g_x[rows:keys]
        ends += [top[seg:]] if s > 0 else [top[seg:], carry]
        over = lambda value: jnp.sum(value, 0, keepdims=True)
        sums.append(
            [over(g_mid * n1), over(g_res * n2), over(g_pre1), over(g_mid), over(g_pre2), over(g_res)]
            + [sum_q, sum_v, g_bup[:, 0]]
        )

    packed = attention_weights(segments, n_t)
    packed, total_up, total_down = lax.optimization_barrier((packed, total_up, total_down))
    total, total_down = lockstep([packed, total_down], [[core_step], [chain(outers[1:])]])
    total, sums, ends = lax.optimization_barrier((total, sums, ends))
    sums = [a + b for a, b in zip(*sums)]
    pick = (jnp.arange(n_t)[:, None] == t ^ slot_masks()[0]).astype(F32)
    by_slot = jnp.concatenate([sums[6].reshape(n_t, -1), sums[7].reshape(n_t, -1), sums[8]], 1)
    by_index = jnp.dot(pick, by_slot, precision=lax.Precision.HIGHEST)
    d_mem = sum(ends[1:], ends[0])
    vectors = jnp.concatenate(
        sums[:6] + [d_mem]
        + [by_index[:, i * head_part : (i + 1) * head_part].reshape(1, width) for i in (0, 1)]
        + [by_index[:, 2 * head_part :].reshape(-1, width)]
    )
    spread = [grow(outer_exchange, step) for step in outer_steps()]
    smalls = small_steps()
    ffn = jnp.concatenate([total_up, total_down], 2)
    merge = lambda value: value.reshape(1, -1, width)
    main = outers + lines
    inside = len(main) - 1
    total, ffn, vectors = lockstep(
        [total, ffn, vectors],
        [main, lines + [chain([merge] + spread[:1])] + spread[1:], [None] + smalls[:inside]],
    )
    first, *rest = smalls[inside:]
    total, ffn_received, vectors = lax.optimization_barrier(
        (spread[0](merge(total)), core_exchange(ffn), first(vectors))
    )
    g_up, g_down = (a.reshape(-1, width) for a in finish(ffn, ffn_received, 2))
    total, g_up, g_down, vectors = lax.optimization_barrier(
        (chain(spread[1:])(total), g_up, g_down, chain(rest)(vectors))
    )
    g_bqv = lax.dynamic_slice_in_dim(vectors[6 + mem : 8 + mem], t * head_part, head_part, 1)
    g_bup = lax.dynamic_slice_in_dim(vectors[8 + mem :].reshape(n_t, -1), t, 1, 0)[0]
    g_qkv, g_out = finish_kinds(total, core_exchange(total), head_part)
    g_qkv = g_qkv.transpose(0, 2, 1)

    return (
        jnp.concatenate(pieces)[None],
        read[None],
        jnp.concatenate(d_text)[None],
        vectors[6 : 6 + mem],
        g_qkv,
        g_bqv,
        g_out,
        g_up,
        g_bup,
        g_down,
        vectors[:2],
        vectors[2:6],
    )


def solution(mesh):
    own = P(("dp", "tensor"), None, None)
    return jax.shard_map(
        local,
        mesh=mesh,
        in_specs=(
            own, P(), P(None, None, "tensor"), P(None, "tensor"), P("tensor", None), P(None, "tensor"),
            P("tensor"), P("tensor", None), P(), P(), own, own,
        ),
        out_specs=(
            own, own, own, P(), P(None, None, "tensor"), P(None, "tensor"), P("tensor", None),
            P(None, "tensor"), P("tensor"), P("tensor", None), P(), P(),
        ),
        check_vma=False,
    )
```

```python
import math

import jax
import jax.numpy as jnp
from jax import lax
from jax.experimental import pallas as pl
from jax.experimental.pallas import tpu as pltpu
from jax.sharding import PartitionSpec as P

HEAD_DIM = 64
SEGMENTS = 2
EPSILON = 1e-06
LANES = 128
F32 = jnp.float32
BF16 = jnp.bfloat16


def dot(a, b, ca, cb):
    return lax.dot_general(a, b, (((ca,), (cb,)), ((), ())), preferred_element_type=F32)


def norm_stats(value):
    centred = value - jnp.mean(value, -1, keepdims=True)
    rstd = lax.rsqrt(jnp.mean(centred * centred, -1, keepdims=True) + EPSILON)
    return centred * rstd, rstd


def norm_backward(grad_out, normed, rstd, gain):
    scaled = grad_out * gain
    first = jnp.mean(scaled, -1, keepdims=True)
    second = jnp.mean(scaled * normed, -1, keepdims=True)
    return rstd * (scaled - first - normed * second)


def log2(n):
    return n.bit_length() - 1


def outer_mask(core, step):
    outer = log2(lax.axis_size("dp")) - 1
    return 2 << (step if core == 0 else outer - 1 - step)


def outer_exchange(value, step):
    pairs = [(i, i ^ outer_mask(i & 1, step)) for i in range(lax.axis_size("dp"))]
    return lax.ppermute(value, "dp", pairs)


def core_exchange(value):
    return lax.ppermute(value, "dp", [(i, i ^ 1) for i in range(lax.axis_size("dp"))])


def line_exchange(value, step):
    n = lax.axis_size("tensor")
    pairs = []
    for i in range(lax.axis_size("dp")):
        mask = 1 << (step if i & 1 == 0 else log2(n) - 1 - step)
        pairs += [(i * n + t, i * n + (t ^ mask)) for t in range(n)]
    return lax.ppermute(value, ("dp", "tensor"), pairs)


def outer_steps():
    return range(log2(lax.axis_size("dp")) - 1)


def line_steps():
    return range(log2(lax.axis_size("tensor")))


def arrival_sources():
    half = lax.axis_size("dp") // 2
    tables = [
        jnp.array([sum(outer_mask(core, i) for i in outer_steps() if j >> i & 1) for j in range(half)], jnp.int32)
        for core in (0, 1)
    ]
    d = lax.axis_index("dp")
    core = d % 2
    mine = jnp.where(core == 0, tables[0], tables[1])
    theirs = jnp.where(core == 0, tables[1], tables[0])
    return jnp.concatenate([d ^ mine, d ^ 1 ^ theirs])


def slot_masks():
    n = lax.axis_size("tensor")
    orders = []
    for flip in (False, True):
        places = [log2(n) - 1 - i if flip else i for i in line_steps()]
        orders.append(jnp.array([sum(1 << places[i] for i in line_steps() if s >> i & 1) for s in range(n)], jnp.int32))
    core = lax.axis_index("dp") % 2
    return jnp.where(core == 0, orders[0], orders[1]), jnp.where(core == 0, orders[1], orders[0])


def other_half_slots():
    n = lax.axis_size("tensor")
    return [sum(1 << (log2(n) - 1 - i) for i in line_steps() if s >> i & 1) for s in range(n)]


def cost(flops, transcendentals, operands, shapes):
    moved = sum(a.size * a.dtype.itemsize for a in list(operands) + list(shapes))
    return pl.CostEstimate(flops=flops, transcendentals=transcendentals, bytes_accessed=moved)


def moved_call(body, table, grid, ins, outs, operands, name, scratch=(), flops=0, transcendentals=0):
    shapes = [shape for _, shape in outs]
    return pl.pallas_call(
        body,
        grid_spec=pltpu.PrefetchScalarGridSpec(
            num_scalar_prefetch=1,
            grid=grid,
            in_specs=[pl.BlockSpec(*spec) for spec in ins],
            out_specs=[pl.BlockSpec(*spec) for spec, _ in outs],
            scratch_shapes=list(scratch),
        ),
        out_shape=shapes,
        cost_estimate=cost(flops, transcendentals, operands, shapes),
        name=name,
    )(table, *operands)


def aligned(rows):
    return rows % 16 == 0


def place_table():
    return jnp.concatenate([arrival_sources(), jnp.array([max(s - 1, 0) for s in other_half_slots()], jnp.int32)])


def pack_table():
    return jnp.concatenate([arrival_sources(), jnp.array(other_half_slots(), jnp.int32)])


def raw_specs(chunks, at=0):
    n, rows, width = chunks.shape
    block = (n // 2, 1, rows, width)
    return [
        ((n, rows, width), lambda s, table: (0, 0, 0)),
        (block, lambda s, table: (0, jnp.maximum(s - 1, 0), at, 0)),
        (block, lambda s, table: (0, table[n + s], at, 0)),
    ]


def settle(table_ref, chunks_ref, own_ref, received_ref, out):
    half = own_ref.shape[0]

    @pl.when(pl.program_id(0) == 0)
    def _():
        out[...] = chunks_ref[...]

    @pl.when(pl.program_id(0) > 0)
    def _():
        for p in range(half):
            out[table_ref[p]] = own_ref[p, 0]
            out[table_ref[half + p]] = received_ref[p, 0]


def packed_outs(slots, n, rows, width):
    shape = jax.ShapeDtypeStruct((n // 2, slots, rows, width), BF16)
    block = (n // 2, 1, rows, width)
    return [
        ((block, lambda s, table: (0, s, 0, 0)), shape),
        ((block, lambda s, table: (0, table[n + s], 0, 0)), shape),
    ]


def place(chunks, own, received):
    others = own.shape[1]
    swap = other_half_slots()
    received = jnp.stack([received[:, swap[s] - 1] for s in range(1, others + 1)], 1)
    moved = jnp.concatenate([own, received])[jnp.argsort(arrival_sources())]
    return jnp.concatenate([chunks[None], moved.transpose(1, 0, 2, 3)])


def pack(total):
    half = total.shape[1] // 2
    moved = total.transpose(1, 0, 2, 3)[arrival_sources()]
    return moved[:half], jnp.stack([moved[half:, s] for s in other_half_slots()], 1)


def finish(own, received, count):
    half, rows, width = own.shape
    rows = rows // count
    source = arrival_sources()
    if not aligned(rows):
        full = jnp.concatenate([own, received])[jnp.argsort(source)].astype(F32)
        return [full[:, i * rows : (i + 1) * rows] for i in range(count)]

    def body(table_ref, own_ref, received_ref, *out_refs):
        for p in range(half):
            for i, out_ref in enumerate(out_refs):
                at = slice(i * rows, (i + 1) * rows)
                out_ref[table_ref[p]] = own_ref[p, at].astype(F32)
                out_ref[table_ref[half + p]] = received_ref[p, at].astype(F32)

    whole = (own.shape, lambda i, table: (0, 0, 0))
    shape = (2 * half, rows, width)
    out = ((shape, lambda i, table: (0, 0, 0)), jax.ShapeDtypeStruct(shape, F32))
    return moved_call(body, source, (1,), [whole, whole], [out] * count, (own, received), "finish")


def finish_kinds(own, received, head_part):
    half, rows, width = own.shape
    n = 2 * half
    if not aligned(rows):
        full = finish(own, received, 1)[0].reshape(4, head_part, width)
        return full[:3], full[3]

    def body(table_ref, own_ref, received_ref, qkv_ref, out_ref, scratch):
        for p in range(half):
            scratch[table_ref[p]] = own_ref[p].astype(F32)
            scratch[table_ref[half + p]] = received_ref[p].astype(F32)
        full = scratch[...].reshape(n * rows, width)
        for i in range(3):
            qkv_ref[i] = full[i * head_part : (i + 1) * head_part]
        out_ref[...] = full[3 * head_part :]

    whole = (own.shape, lambda i, table: (0, 0, 0))
    shapes = [(3, head_part, width), (head_part, width)]
    outs = [
        ((shape, lambda i, table, rank=len(shape): (0,) * rank), jax.ShapeDtypeStruct(shape, F32)) for shape in shapes
    ]
    return moved_call(
        body, arrival_sources(), (1,), [whole, whole], outs, (own, received), "finish_kinds",
        [pltpu.VMEM((n, rows, width), F32)],
    )


def place_kinds(chunks, own, received):
    n, rows, width = chunks.shape
    slots = own.shape[1] + 1
    part = n * rows // 4
    if not (aligned(rows) and aligned(part)):
        full = place(chunks, own, received).reshape(slots, 4, part, width)
        return [full[:, i].reshape(-1, width) for i in range(4)]

    def body(table_ref, chunks_ref, own_ref, received_ref, *refs):
        settle(table_ref, chunks_ref, own_ref, received_ref, refs[-1])
        full = refs[-1][...].reshape(n * rows, width)
        for i in range(4):
            refs[i][...] = full[i * part : (i + 1) * part]

    out = (((part, width), lambda s, table: (s, 0)), jax.ShapeDtypeStruct((slots * part, width), BF16))
    return moved_call(
        body, place_table(), (slots,), raw_specs(chunks), [out] * 4, (chunks, own, received), "place_kinds",
        [pltpu.VMEM((n, rows, width), BF16)],
    )


def gather_outer(rest, steps):
    for step in steps:
        rest = jnp.concatenate([rest, outer_exchange(rest, step)])
    return rest


def plus(a, b):
    return (a.astype(F32) + b.astype(F32)).astype(BF16)


def core_step(packed):
    return plus(packed[0], core_exchange(packed[1]))


def reduce_steps():
    def outer(step):
        def run(total):
            half = total.shape[0] // 2
            return plus(total[:half], outer_exchange(total[half:], step))

        return run

    def line(step):
        def run(total):
            half = total.shape[1] // 2
            return plus(total[:, :half], line_exchange(total[:, half:], step))

        return run

    return [outer(step) for step in reversed(outer_steps())], [line(step) for step in reversed(line_steps())]


def small_steps():
    def run(axis, bit):
        return lambda value: value + lax.ppermute(value, axis, [(i, i ^ bit) for i in range(lax.axis_size(axis))])

    return [run(axis, 1 << i) for axis in ("dp", "tensor") for i in range(log2(lax.axis_size(axis)))]


def chain(steps):
    def run(value):
        for step in steps:
            value = step(value)
        return value

    return run


def lockstep(values, chains):
    for stage in range(max(len(chain) for chain in chains)):
        values = [
            chain[stage](value) if stage < len(chain) and chain[stage] else value
            for value, chain in zip(values, chains)
        ]
        values = lax.optimization_barrier(values)
    return values


def ffn_cost(rows, hidden, width, products):
    return 2 * rows * hidden * width * products


def ffn_slot(low_ref, up, bias_ref, down, act_ref, slope_ref, out_ref):
    @pl.when(pl.program_id(0) == 0)
    def _():
        out_ref[...] = jnp.zeros_like(out_ref)

    step = low_ref.shape[0] // 4
    for i in range(4):
        at = slice(i * step, (i + 1) * step)
        hidden = dot(low_ref[at, :], up, 1, 0) + bias_ref[0]
        cdf = 0.5 * (1.0 + lax.erf(hidden * math.sqrt(0.5)))
        act = (hidden * cdf).astype(BF16)
        act_ref[0, at, :] = act
        pdf = jnp.exp(hidden * hidden * -0.5) * (1.0 / math.sqrt(2.0 * math.pi))
        slope_ref[0, at, :] = (cdf + hidden * pdf).astype(BF16)
        out_ref[at, :] += dot(act, down, 1, 0)


def ffn_specs(rows, width, slots, part):
    whole = ((rows, width), lambda s, table: (0, 0))
    units = ((1, rows, part), lambda s, table: (s, 0, 0))
    shape = jax.ShapeDtypeStruct((slots, rows, part), BF16)
    return whole, units, [(units, shape), (units, shape), (whole, jax.ShapeDtypeStruct((rows, width), F32))]


def ffn_first(low, up_bias, chunks, own, received):
    rows, width = low.shape
    slots, part = up_bias.shape[0], up_bias.shape[2]
    count = chunks[0].shape[1]
    if not aligned(count):
        up, down = (place(c, *(h[:, :, i * count : (i + 1) * count] for h in (own, received))) for i, c in enumerate(chunks))
        up, down = up.reshape(slots, width, part), down.reshape(slots, part, width)
        return (*ffn_forward(low, up, up_bias, down), up, down)

    def body(table_ref, low_ref, bias_ref, *refs):
        up_refs, down_refs, (act_ref, slope_ref, out_ref, up_ref, down_ref) = refs[:3], refs[3:6], refs[6:]
        settle(table_ref, *up_refs, up_ref.at[0])
        settle(table_ref, *down_refs, down_ref.at[0])
        up, down = up_ref[0].reshape(width, part), down_ref[0].reshape(part, width)
        ffn_slot(low_ref, up, bias_ref, down, act_ref, slope_ref, out_ref)

    whole, _, outs = ffn_specs(rows, width, slots, part)
    for c in chunks:
        outs.append((((1,) + c.shape, lambda s, table: (s, 0, 0, 0)), jax.ShapeDtypeStruct((slots,) + c.shape, BF16)))
    act, slope, out, up, down = moved_call(
        body, place_table(), (slots,),
        [whole, ((1, 1, part), lambda s, table: (s, 0, 0))] + raw_specs(chunks[0], 0) + raw_specs(chunks[1], 1),
        outs, (low, up_bias, chunks[0], own, received, chunks[1], own, received), "ffn_first",
        flops=ffn_cost(rows, slots * part, width, 2), transcendentals=rows * slots * part * 2,
    )
    return act, slope, out, up.reshape(slots, width, part), down.reshape(slots, part, width)


def ffn_forward(low, up, up_bias, down):
    rows, width = low.shape
    slots, part = up_bias.shape[0], up_bias.shape[2]

    def body(table_ref, low_ref, up_ref, bias_ref, down_ref, act_ref, slope_ref, out_ref):
        ffn_slot(low_ref, up_ref[0], bias_ref, down_ref[0], act_ref, slope_ref, out_ref)

    whole, _, outs = ffn_specs(rows, width, slots, part)
    slot = lambda s, table: (s, 0, 0)
    return moved_call(
        body, jnp.zeros((1,), jnp.int32), (slots,),
        [whole, ((1, width, part), slot), ((1, 1, part), slot), ((1, part, width), slot)],
        outs, (low, up, up_bias, down), "ffn_forward",
        flops=ffn_cost(rows, slots * part, width, 2), transcendentals=rows * slots * part * 2,
    )


def ffn_backward(g_ffn, low, act, slope, up, down, earlier):
    rows, width = low.shape
    slots, part = up.shape[0], up.shape[2]
    n = lax.axis_size("dp")
    fused = bool(earlier) and aligned(width // n) and aligned(part // n)
    half = n // 2

    def body(table_ref, g_ref, low_ref, act_ref, slope_ref, up_ref, down_ref, *refs):
        olds, refs = refs[: len(earlier)], refs[len(earlier) :]
        mid_ref, bias_ref, outs = refs[0], refs[1], refs[2:]
        g = g_ref[...]
        hid = (dot(g, down_ref[0], 1, 1) * slope_ref[0].astype(F32)).astype(BF16)
        bias_ref[0] = jnp.sum(hid.astype(F32), 0, keepdims=True)
        back = dot(hid, up_ref[0], 1, 1)

        @pl.when(pl.program_id(0) == 0)
        def _():
            mid_ref[...] = back

        @pl.when(pl.program_id(0) > 0)
        def _():
            mid_ref[...] += back

        for i, (left, right) in enumerate(((low_ref[...], hid), (act_ref[0], g))):
            total = dot(left, right, 0, 0)
            if olds:
                total = total + olds[i][0].astype(F32)
            if fused:
                keep_ref, send_ref, scratch = outs[2 * i], outs[2 * i + 1], outs[4 + i]
                scratch[...] = total.astype(BF16).reshape(scratch.shape)
                for p in range(half):
                    keep_ref[p, 0] = scratch[table_ref[p]]
                    send_ref[p, 0] = scratch[table_ref[half + p]]
            else:
                outs[i][0] = total.astype(BF16)

    whole, units, _ = ffn_specs(rows, width, slots, part)
    slot = lambda s, table: (s, 0, 0)
    shapes = [(width, part), (part, width)]
    weights = [((1,) + shape, slot) for shape in shapes]
    outs = [
        (whole, jax.ShapeDtypeStruct((rows, width), F32)),
        (((1, 1, part), slot), jax.ShapeDtypeStruct((slots, 1, part), F32)),
    ]
    scratch = []
    for shape, spec in zip(shapes, weights):
        if fused:
            chunk = (n, shape[0] // n, shape[1])
            outs += packed_outs(slots, *chunk)
            scratch.append(pltpu.VMEM(chunk, BF16))
        else:
            outs.append((spec, jax.ShapeDtypeStruct((slots,) + shape, BF16)))
    got = moved_call(
        body, pack_table(), (slots,),
        [whole, whole, units, units] + weights + (weights if earlier else []),
        outs, (g_ffn, low, act, slope, up, down, *earlier), "ffn_backward", scratch,
        flops=ffn_cost(rows, slots * part, width, 4),
    )
    if fused:
        return got[0], got[1], got[2:4], got[4:6]
    if earlier:
        return got[0], got[1], *(pack(d.reshape(slots, n, -1, d.shape[-1])) for d in got[2:])
    return got


def lane_masks(rows):
    lane = lax.broadcasted_iota(jnp.int32, (rows, LANES), 1)
    return [(lane >= h * HEAD_DIM) & (lane < (h + 1) * HEAD_DIM) for h in range(LANES // HEAD_DIM)]


def only(mask, value):
    return jnp.where(mask, value, jnp.zeros_like(value))


def attention_forward(q, k, v, keys):
    rows, width = q.shape
    padded = k.shape[0]
    scale = 1.0 / math.sqrt(HEAD_DIM)

    def body(q_ref, k_ref, v_ref, out_ref, lse_ref):
        q = q_ref[...] * jnp.asarray(scale, BF16)
        k, v = k_ref[...], v_ref[...]
        live = lax.broadcasted_iota(jnp.int32, (1, padded), 1) < keys
        out = jnp.zeros((rows, LANES), F32)
        lses = jnp.zeros((rows, LANES), F32)
        for mine, theirs in zip(lane_masks(rows), lane_masks(padded)):
            scores = jnp.where(live, dot(only(mine, q), k, 1, 1), -jnp.inf)
            top = jnp.max(scores, -1, keepdims=True)
            weights = jnp.exp(scores - top)
            total = jnp.sum(weights, -1, keepdims=True)
            probs = (weights * (1.0 / total)).astype(BF16)
            out = out + dot(probs, only(theirs, v), 1, 0)
            lses = jnp.where(mine, top + jnp.log(total), lses)
        out_ref[...] = out.astype(BF16)
        lse_ref[...] = lses

    q_spec = pl.BlockSpec((rows, LANES), lambda h: (0, h))
    k_spec = pl.BlockSpec((padded, LANES), lambda h: (0, h))
    return pl.pallas_call(
        body,
        grid=(width // LANES,),
        in_specs=[q_spec, k_spec, k_spec],
        out_specs=[q_spec, q_spec],
        out_shape=[jax.ShapeDtypeStruct((rows, width), BF16), jax.ShapeDtypeStruct((rows, width), F32)],
        cost_estimate=cost(8 * rows * padded * width, rows * padded * width // HEAD_DIM, (q, k, v, q, q), ()),
        name="attention_forward",
    )(q, k, v)


def attention_backward(q, k, v, lse, g_att, keys):
    rows, width = q.shape
    padded = k.shape[0]
    scale = 1.0 / math.sqrt(HEAD_DIM)

    def body(q_ref, k_ref, v_ref, lse_ref, g_ref, gq_ref, gk_ref, gv_ref, sum_q_ref, sum_v_ref):
        q, g = q_ref[...] * jnp.asarray(scale, BF16), g_ref[...]
        k, v = k_ref[...], v_ref[...]
        live = lax.broadcasted_iota(jnp.int32, (1, padded), 1) < keys
        gq = jnp.zeros((rows, LANES), F32)
        gk = jnp.zeros((padded, LANES), F32)
        gv = jnp.zeros((padded, LANES), F32)
        for h, (mine, theirs) in enumerate(zip(lane_masks(rows), lane_masks(padded))):
            q_h, g_h = only(mine, q), only(mine, g)
            scores = dot(q_h, k, 1, 1)
            full = jnp.where(live, jnp.exp(scores - lse_ref[:, h * HEAD_DIM : h * HEAD_DIM + 1]), 0.0)
            g_probs = dot(g_h, v, 1, 1)
            inner = jnp.sum(g_probs * full, -1, keepdims=True)
            g_scores = (full * (g_probs - inner)).astype(BF16)
            gq = gq + dot(g_scores, only(theirs, k), 1, 0)
            gk = gk + dot(g_scores, q_h, 0, 0)
            gv = gv + dot(full.astype(BF16), g_h, 0, 0)
        gq = (gq * scale).astype(BF16)
        gv = gv.astype(BF16)
        gq_ref[...] = gq
        gk_ref[...] = gk.astype(BF16)
        gv_ref[...] = gv
        sum_q_ref[...] = jnp.sum(gq.astype(F32), 0, keepdims=True)
        sum_v_ref[...] = jnp.sum(gv.astype(F32), 0, keepdims=True)

    q_spec = pl.BlockSpec((rows, LANES), lambda h: (0, h))
    k_spec = pl.BlockSpec((padded, LANES), lambda h: (0, h))
    sum_spec = pl.BlockSpec((1, LANES), lambda h: (0, h))
    return pl.pallas_call(
        body,
        grid=(width // LANES,),
        in_specs=[q_spec, k_spec, k_spec, q_spec, q_spec],
        out_specs=[q_spec, k_spec, k_spec, sum_spec, sum_spec],
        out_shape=[
            jax.ShapeDtypeStruct((rows, width), BF16),
            jax.ShapeDtypeStruct((padded, width), BF16),
            jax.ShapeDtypeStruct((padded, width), BF16),
            jax.ShapeDtypeStruct((1, width), F32),
            jax.ShapeDtypeStruct((1, width), F32),
        ],
        cost_estimate=cost(20 * rows * padded * width, rows * padded * width // HEAD_DIM, (q, k, v, lse, g_att, q, k, v), ()),
        name="attention_backward",
    )(q, k, v, lse, g_att)


def attention_weights(segments, slots):
    width = segments[0][0].shape[1]
    part = width // slots
    n = lax.axis_size("dp")
    rows = 4 * part // n
    half = n // 2
    fused = aligned(rows)
    swap = other_half_slots()
    operands = [a for segment in segments for a in segment]

    def body(table_ref, *refs):
        out_refs = refs[len(operands) :]
        full = out_refs[-1]
        groups = [refs[i : i + 6] for i in range(0, len(operands), 6)]
        for kind in range(4):
            total = None
            for refs_of in groups:
                left = refs_of[4] if kind == 3 else refs_of[kind]
                right = refs_of[5][...] if kind == 3 else refs_of[3][: left.shape[0], :]
                one = dot(left[...], right, 0, 0)
                total = one if total is None else total + one
            for s in range(slots):
                full[s, kind * part : (kind + 1) * part, :] = total[s * part : (s + 1) * part].astype(BF16)
        if fused:
            for p in range(half):
                mine = pl.ds(pl.multiple_of(table_ref[p] * rows, 16), rows)
                theirs = pl.ds(pl.multiple_of(table_ref[half + p] * rows, 16), rows)
                for s in range(slots):
                    out_refs[0][p, s] = full[s, mine, :]
                    out_refs[1][p, s] = full[swap[s], theirs, :]

    everything = lambda a: (a.shape, lambda i, table: (0,) * len(a.shape))
    packed = jax.ShapeDtypeStruct((half, slots, rows, width), BF16)
    whole = jax.ShapeDtypeStruct((slots, 4 * part, width), BF16)
    shapes = [packed, packed] if fused else [whole]
    got = moved_call(
        body, arrival_sources(), (1,), [everything(a) for a in operands], [(everything(a), a) for a in shapes], operands,
        "attention_weights", [pltpu.VMEM(whole.shape, BF16)] if fused else [],
        flops=sum(2 * a.size * width for a in operands) * 2 // 3,
    )
    return got if fused else pack(got[0].reshape(slots, n, rows, width))


def local(text_in, start_memory, w_qkv, b_qv, w_o, w_up, b_up, w_down, norm_gains, biases, cot_text, cot_memory):
    text, cot_rows, cot_mem = text_in[0], cot_text[0], cot_memory[0]
    text_total, width = text.shape
    mem = start_memory.shape[0]
    seg = text_total // SEGMENTS
    rows = seg + mem
    keys = rows + mem
    padded = -(-keys // LANES) * LANES
    n_t, n_dp = lax.axis_size("tensor"), lax.axis_size("dp")
    head_part = w_qkv.shape[2]
    part = b_up.shape[0]
    t = lax.axis_index("tensor")

    small = jnp.concatenate([b_qv.reshape(-1), b_up])
    small = jnp.pad(small, (0, 8 * width - small.shape[0])).reshape(1, 8, width)
    d = lax.axis_index("dp")
    own_chunk = lambda chunks: lax.dynamic_index_in_dim(chunks, d, 0)
    kinds = jnp.concatenate([w_qkv.transpose(0, 2, 1).reshape(-1, width), w_o]).reshape(n_dp, -1, width)
    chunks = [w_up.reshape(n_dp, -1, part), w_down.reshape(n_dp, -1, width)]
    lined = jnp.concatenate([own_chunk(kinds), small], 1)
    ffn_own = jnp.concatenate([own_chunk(c) for c in chunks], 1)
    grow = lambda exchange, step: lambda value: jnp.concatenate([value, exchange(value, step)])
    grow_line = [grow(line_exchange, step) for step in line_steps()]
    lined = chain(grow_line)(lined)
    rest, ffn_rest = lockstep(
        [lined[None, 1:, : kinds.shape[1]], ffn_own], [[grow(outer_exchange, step) for step in outer_steps()], grow_line]
    )
    small = lined[:, kinds.shape[1] :].reshape(n_t, -1).astype(F32)
    q_bias = small[:, :head_part].reshape(1, -1)
    v_bias = small[:, head_part : 2 * head_part].reshape(1, -1)
    up_bias = small[:, None, 2 * head_part : 2 * head_part + part]
    received = core_exchange(rest)
    ffn_rest = ffn_rest[None, 1:]
    first, *middle, last = outer_steps()
    (q_w, k_w, v_w, o_w), ffn_received = lax.optimization_barrier(
        (place_kinds(kinds, rest, received), outer_exchange(ffn_rest, first))
    )
    ffn_rest = gather_outer(jnp.concatenate([ffn_rest, ffn_received]), middle)

    read = start_memory
    kept, pieces = [], []
    for s in range(SEGMENTS):
        x = jnp.concatenate([text[s * seg : (s + 1) * seg], start_memory, read, jnp.zeros((padded - keys, width), BF16)])
        q = (dot(x[:rows], q_w, 1, 1) + q_bias).astype(BF16)
        k = dot(x, k_w, 1, 1).astype(BF16)
        v = (dot(x, v_w, 1, 1) + v_bias).astype(BF16)
        att, lse = attention_forward(q, k, v, keys)
        if s == 0:
            att, ffn_received = lax.optimization_barrier((att, outer_exchange(ffn_rest, last)))
            ffn_rest = jnp.concatenate([ffn_rest, ffn_received])
        n1, r1 = norm_stats(x[:rows].astype(F32) + dot(att, o_w, 1, 0) + biases[0])
        middle = n1 * norm_gains[0] + biases[1]
        low = middle.astype(BF16)
        if s == 0:
            act, slope, ffn, up_full, down_full = ffn_first(low, up_bias, chunks, ffn_rest, core_exchange(ffn_rest))
        else:
            act, slope, ffn = ffn_forward(low, up_full, up_bias, down_full)
        n2, r2 = norm_stats(middle + ffn + biases[2])
        result = (n2 * norm_gains[1] + biases[3]).astype(BF16)
        pieces.append(result[:seg])
        read = result[seg:]
        kept.append((x, q, k, v, lse, att, n1, r1, low, act, slope, n2, r2))

    segments, sums, ends = [], [], []
    carry = cot_mem.astype(F32)
    d_text = [None] * SEGMENTS
    outers, lines = reduce_steps()
    earlier = ()
    for s in reversed(range(SEGMENTS)):
        x, q, k, v, lse, att, n1, r1, low, act, slope, n2, r2 = kept[s]
        g_res = jnp.concatenate([cot_rows[s * seg : (s + 1) * seg].astype(F32), carry])
        g_pre2 = norm_backward(g_res, n2, r2, norm_gains[1])
        g_ffn = g_pre2.astype(BF16)
        g_mid, g_bup, *got = ffn_backward(g_ffn, low, act, slope, up_full, down_full, earlier)
        if s == 0:
            d_up, d_down = got
        else:
            earlier = tuple(got)
        g_mid = g_mid + g_pre2
        g_pre1 = norm_backward(g_mid, n1, r1, norm_gains[0])
        g_attn = g_pre1.astype(BF16)
        g_att = dot(g_attn, o_w, 1, 1).astype(BF16)
        if s == 0:
            g_att, total_up = lax.optimization_barrier((g_att, core_step(d_up)))
            total_up, total_down = outers[0](total_up), core_step(d_down)
        g_q, g_k, g_v, sum_q, sum_v = attention_backward(q, k, v, lse, g_att, keys)
        if s == 0:
            (g_q, g_k, g_v), total_up, total_down = lax.optimization_barrier(((g_q, g_k, g_v), total_up, total_down))
            total_up, total_down = chain(outers[1:])(total_up), outers[0](total_down)
        segments.append((g_q, g_k, g_v, x, att, g_attn))
        g_x = dot(g_k, k_w, 1, 0) + dot(g_v, v_w, 1, 0)
        top = g_x[:rows] + dot(g_q, q_w, 1, 0) + g_pre1
        d_text[s] = top[:seg]
        carry = g_x[rows:keys]
        ends += [top[seg:]] if s > 0 else [top[seg:], carry]
        over = lambda value: jnp.sum(value, 0, keepdims=True)
        sums.append(
            [over(g_mid * n1), over(g_res * n2), over(g_pre1), over(g_mid), over(g_pre2), over(g_res)]
            + [sum_q, sum_v, g_bup[:, 0]]
        )

    packed = attention_weights(segments, n_t)
    packed, total_up, total_down = lax.optimization_barrier((packed, total_up, total_down))
    total, total_down = lockstep([packed, total_down], [[core_step], [chain(outers[1:])]])
    total, sums, ends = lax.optimization_barrier((total, sums, ends))
    sums = [a + b for a, b in zip(*sums)]
    pick = (jnp.arange(n_t)[:, None] == t ^ slot_masks()[0]).astype(F32)
    by_slot = jnp.concatenate([sums[6].reshape(n_t, -1), sums[7].reshape(n_t, -1), sums[8]], 1)
    by_index = jnp.dot(pick, by_slot, precision=lax.Precision.HIGHEST)
    d_mem = sum(ends[1:], ends[0])
    vectors = jnp.concatenate(
        sums[:6] + [d_mem]
        + [by_index[:, i * head_part : (i + 1) * head_part].reshape(1, width) for i in (0, 1)]
        + [by_index[:, 2 * head_part :].reshape(-1, width)]
    )
    spread = [grow(outer_exchange, step) for step in outer_steps()]
    smalls = small_steps()
    ffn = jnp.concatenate([total_up, total_down], 2)
    merge = lambda value: value.reshape(1, -1, width)
    main = outers + lines
    inside = len(main) - 1
    total, ffn, vectors = lockstep(
        [total, ffn, vectors],
        [main, lines + [chain([merge] + spread[:1])] + spread[1:], [None] + smalls[:inside]],
    )
    first, *rest = smalls[inside:]
    total, ffn_received, vectors = lax.optimization_barrier(
        (spread[0](merge(total)), core_exchange(ffn), first(vectors))
    )
    g_up, g_down = (a.reshape(-1, width) for a in finish(ffn, ffn_received, 2))
    total, g_up, g_down, vectors = lax.optimization_barrier(
        (chain(spread[1:])(total), g_up, g_down, chain(rest)(vectors))
    )
    g_bqv = lax.dynamic_slice_in_dim(vectors[6 + mem : 8 + mem], t * head_part, head_part, 1)
    g_bup = lax.dynamic_slice_in_dim(vectors[8 + mem :].reshape(n_t, -1), t, 1, 0)[0]
    g_qkv, g_out = finish_kinds(total, core_exchange(total), head_part)
    g_qkv = g_qkv.transpose(0, 2, 1)

    return (
        jnp.concatenate(pieces)[None],
        read[None],
        jnp.concatenate(d_text)[None],
        vectors[6 : 6 + mem],
        g_qkv,
        g_bqv,
        g_out,
        g_up,
        g_bup,
        g_down,
        vectors[:2],
        vectors[2:6],
    )


def solution(mesh):
    own = P(("dp", "tensor"), None, None)
    return jax.shard_map(
        local,
        mesh=mesh,
        in_specs=(
            own, P(), P(None, None, "tensor"), P(None, "tensor"), P("tensor", None), P(None, "tensor"),
            P("tensor"), P("tensor", None), P(), P(), own, own,
        ),
        out_specs=(
            own, own, own, P(), P(None, None, "tensor"), P(None, "tensor"), P("tensor", None),
            P(None, "tensor"), P("tensor"), P("tensor", None), P(), P(),
        ),
        check_vma=False,
    )
```

```python
import math

import jax
import jax.numpy as jnp
from jax import lax
from jax.experimental import pallas as pl
from jax.experimental.pallas import tpu as pltpu
from jax.sharding import PartitionSpec as P

HEAD_DIM = 64
SEGMENTS = 2
EPSILON = 1e-06
LANES = 128
F32 = jnp.float32
BF16 = jnp.bfloat16


def dot(a, b, ca, cb):
    return lax.dot_general(a, b, (((ca,), (cb,)), ((), ())), preferred_element_type=F32)


def norm_stats(value):
    centred = value - jnp.mean(value, -1, keepdims=True)
    rstd = lax.rsqrt(jnp.mean(centred * centred, -1, keepdims=True) + EPSILON)
    return centred * rstd, rstd


def norm_backward(grad_out, normed, rstd, gain):
    scaled = grad_out * gain
    first = jnp.mean(scaled, -1, keepdims=True)
    second = jnp.mean(scaled * normed, -1, keepdims=True)
    return rstd * (scaled - first - normed * second)


def log2(n):
    return n.bit_length() - 1


def outer_mask(core, step):
    outer = log2(lax.axis_size("dp")) - 1
    return 2 << (step if core == 0 else outer - 1 - step)


def outer_exchange(value, step):
    pairs = [(i, i ^ outer_mask(i & 1, step)) for i in range(lax.axis_size("dp"))]
    return lax.ppermute(value, "dp", pairs)


def core_exchange(value):
    return lax.ppermute(value, "dp", [(i, i ^ 1) for i in range(lax.axis_size("dp"))])


def line_exchange(value, step):
    n = lax.axis_size("tensor")
    pairs = []
    for i in range(lax.axis_size("dp")):
        mask = 1 << (step if i & 1 == 0 else log2(n) - 1 - step)
        pairs += [(i * n + t, i * n + (t ^ mask)) for t in range(n)]
    return lax.ppermute(value, ("dp", "tensor"), pairs)


def outer_steps():
    return range(log2(lax.axis_size("dp")) - 1)


def line_steps():
    return range(log2(lax.axis_size("tensor")))


def arrival_sources():
    half = lax.axis_size("dp") // 2
    tables = [
        jnp.array([sum(outer_mask(core, i) for i in outer_steps() if j >> i & 1) for j in range(half)], jnp.int32)
        for core in (0, 1)
    ]
    d = lax.axis_index("dp")
    core = d % 2
    mine = jnp.where(core == 0, tables[0], tables[1])
    theirs = jnp.where(core == 0, tables[1], tables[0])
    return jnp.concatenate([d ^ mine, d ^ 1 ^ theirs])


def slot_masks():
    n = lax.axis_size("tensor")
    orders = []
    for flip in (False, True):
        places = [log2(n) - 1 - i if flip else i for i in line_steps()]
        orders.append(jnp.array([sum(1 << places[i] for i in line_steps() if s >> i & 1) for s in range(n)], jnp.int32))
    core = lax.axis_index("dp") % 2
    return jnp.where(core == 0, orders[0], orders[1]), jnp.where(core == 0, orders[1], orders[0])


def other_half_slots():
    n = lax.axis_size("tensor")
    return [sum(1 << (log2(n) - 1 - i) for i in line_steps() if s >> i & 1) for s in range(n)]


def cost(flops, transcendentals, operands, shapes):
    moved = sum(a.size * a.dtype.itemsize for a in list(operands) + list(shapes))
    return pl.CostEstimate(flops=flops, transcendentals=transcendentals, bytes_accessed=moved)


def moved_call(body, table, grid, ins, outs, operands, name, scratch=(), flops=0, transcendentals=0):
    shapes = [shape for _, shape in outs]
    return pl.pallas_call(
        body,
        grid_spec=pltpu.PrefetchScalarGridSpec(
            num_scalar_prefetch=1,
            grid=grid,
            in_specs=[pl.BlockSpec(*spec) for spec in ins],
            out_specs=[pl.BlockSpec(*spec) for spec, _ in outs],
            scratch_shapes=list(scratch),
        ),
        out_shape=shapes,
        cost_estimate=cost(flops, transcendentals, operands, shapes),
        name=name,
    )(table, *operands)


def aligned(rows):
    return rows % 16 == 0


def place_table():
    return jnp.concatenate([arrival_sources(), jnp.array([max(s - 1, 0) for s in other_half_slots()], jnp.int32)])


def pack_table():
    return jnp.concatenate([arrival_sources(), jnp.array(other_half_slots(), jnp.int32)])


def raw_specs(chunks, at=0):
    n, rows, width = chunks.shape
    block = (n // 2, 1, rows, width)
    return [
        ((n, rows, width), lambda s, table: (0, 0, 0)),
        (block, lambda s, table: (0, jnp.maximum(s - 1, 0), at, 0)),
        (block, lambda s, table: (0, table[n + s], at, 0)),
    ]


def settle(table_ref, chunks_ref, own_ref, received_ref, out):
    half = own_ref.shape[0]

    @pl.when(pl.program_id(0) == 0)
    def _():
        out[...] = chunks_ref[...]

    @pl.when(pl.program_id(0) > 0)
    def _():
        for p in range(half):
            out[table_ref[p]] = own_ref[p, 0]
            out[table_ref[half + p]] = received_ref[p, 0]


def packed_outs(slots, n, rows, width):
    shape = jax.ShapeDtypeStruct((n // 2, slots, rows, width), BF16)
    block = (n // 2, 1, rows, width)
    return [
        ((block, lambda s, table: (0, s, 0, 0)), shape),
        ((block, lambda s, table: (0, table[n + s], 0, 0)), shape),
    ]


def place(chunks, own, received):
    others = own.shape[1]
    swap = other_half_slots()
    received = jnp.stack([received[:, swap[s] - 1] for s in range(1, others + 1)], 1)
    moved = jnp.concatenate([own, received])[jnp.argsort(arrival_sources())]
    return jnp.concatenate([chunks[None], moved.transpose(1, 0, 2, 3)])


def pack(total):
    half = total.shape[1] // 2
    moved = total.transpose(1, 0, 2, 3)[arrival_sources()]
    return moved[:half], jnp.stack([moved[half:, s] for s in other_half_slots()], 1)


def finish(own, received, count):
    half, rows, width = own.shape
    rows = rows // count
    source = arrival_sources()
    if not aligned(rows):
        full = jnp.concatenate([own, received])[jnp.argsort(source)].astype(F32)
        return [full[:, i * rows : (i + 1) * rows] for i in range(count)]

    def body(table_ref, own_ref, received_ref, *out_refs):
        for p in range(half):
            for i, out_ref in enumerate(out_refs):
                at = slice(i * rows, (i + 1) * rows)
                out_ref[table_ref[p]] = own_ref[p, at].astype(F32)
                out_ref[table_ref[half + p]] = received_ref[p, at].astype(F32)

    whole = (own.shape, lambda i, table: (0, 0, 0))
    shape = (2 * half, rows, width)
    out = ((shape, lambda i, table: (0, 0, 0)), jax.ShapeDtypeStruct(shape, F32))
    return moved_call(body, source, (1,), [whole, whole], [out] * count, (own, received), "finish")


def finish_kinds(own, received, head_part):
    half, rows, width = own.shape
    n = 2 * half
    if not aligned(rows):
        full = finish(own, received, 1)[0].reshape(4, head_part, width)
        return full[:3], full[3]

    def body(table_ref, own_ref, received_ref, qkv_ref, out_ref, scratch):
        for p in range(half):
            scratch[table_ref[p]] = own_ref[p].astype(F32)
            scratch[table_ref[half + p]] = received_ref[p].astype(F32)
        full = scratch[...].reshape(n * rows, width)
        for i in range(3):
            qkv_ref[i] = full[i * head_part : (i + 1) * head_part]
        out_ref[...] = full[3 * head_part :]

    whole = (own.shape, lambda i, table: (0, 0, 0))
    shapes = [(3, head_part, width), (head_part, width)]
    outs = [
        ((shape, lambda i, table, rank=len(shape): (0,) * rank), jax.ShapeDtypeStruct(shape, F32)) for shape in shapes
    ]
    return moved_call(
        body, arrival_sources(), (1,), [whole, whole], outs, (own, received), "finish_kinds",
        [pltpu.VMEM((n, rows, width), F32)],
    )


def place_kinds(chunks, own, received):
    n, rows, width = chunks.shape
    slots = own.shape[1] + 1
    part = n * rows // 4
    if not (aligned(rows) and aligned(part)):
        full = place(chunks, own, received).reshape(slots, 4, part, width)
        return [full[:, i].reshape(-1, width) for i in range(4)]

    def body(table_ref, chunks_ref, own_ref, received_ref, *refs):
        settle(table_ref, chunks_ref, own_ref, received_ref, refs[-1])
        full = refs[-1][...].reshape(n * rows, width)
        for i in range(4):
            refs[i][...] = full[i * part : (i + 1) * part]

    out = (((part, width), lambda s, table: (s, 0)), jax.ShapeDtypeStruct((slots * part, width), BF16))
    return moved_call(
        body, place_table(), (slots,), raw_specs(chunks), [out] * 4, (chunks, own, received), "place_kinds",
        [pltpu.VMEM((n, rows, width), BF16)],
    )


def gather_outer(rest, steps):
    for step in steps:
        rest = jnp.concatenate([rest, outer_exchange(rest, step)])
    return rest


def plus(a, b):
    return (a.astype(F32) + b.astype(F32)).astype(BF16)


def core_step(packed):
    return plus(packed[0], core_exchange(packed[1]))


def reduce_steps():
    def outer(step):
        def run(total):
            half = total.shape[0] // 2
            return plus(total[:half], outer_exchange(total[half:], step))

        return run

    def line(step):
        def run(total):
            half = total.shape[1] // 2
            return plus(total[:, :half], line_exchange(total[:, half:], step))

        return run

    return [outer(step) for step in reversed(outer_steps())], [line(step) for step in reversed(line_steps())]


def small_steps():
    def run(axis, bit):
        return lambda value: value + lax.ppermute(value, axis, [(i, i ^ bit) for i in range(lax.axis_size(axis))])

    return [run(axis, 1 << i) for axis in ("dp", "tensor") for i in range(log2(lax.axis_size(axis)))]


def chain(steps):
    def run(value):
        for step in steps:
            value = step(value)
        return value

    return run


def lockstep(values, chains):
    for stage in range(max(len(chain) for chain in chains)):
        values = [
            chain[stage](value) if stage < len(chain) and chain[stage] else value
            for value, chain in zip(values, chains)
        ]
        values = lax.optimization_barrier(values)
    return values


def ffn_cost(rows, hidden, width, products):
    return 2 * rows * hidden * width * products


def ffn_slot(low_ref, up, bias_ref, down, act_ref, slope_ref, out_ref):
    @pl.when(pl.program_id(0) == 0)
    def _():
        out_ref[...] = jnp.zeros_like(out_ref)

    step = low_ref.shape[0] // 4
    for i in range(4):
        at = slice(i * step, (i + 1) * step)
        hidden = dot(low_ref[at, :], up, 1, 0) + bias_ref[0]
        cdf = 0.5 * (1.0 + lax.erf(hidden * math.sqrt(0.5)))
        act = (hidden * cdf).astype(BF16)
        act_ref[0, at, :] = act
        pdf = jnp.exp(hidden * hidden * -0.5) * (1.0 / math.sqrt(2.0 * math.pi))
        slope_ref[0, at, :] = (cdf + hidden * pdf).astype(BF16)
        out_ref[at, :] += dot(act, down, 1, 0)


def ffn_specs(rows, width, slots, part):
    whole = ((rows, width), lambda s, table: (0, 0))
    units = ((1, rows, part), lambda s, table: (s, 0, 0))
    shape = jax.ShapeDtypeStruct((slots, rows, part), BF16)
    return whole, units, [(units, shape), (units, shape), (whole, jax.ShapeDtypeStruct((rows, width), F32))]


def ffn_first(low, up_bias, chunks, own, received):
    rows, width = low.shape
    slots, part = up_bias.shape[0], up_bias.shape[2]
    count = chunks[0].shape[1]
    if not aligned(count):
        up, down = (place(c, *(h[:, :, i * count : (i + 1) * count] for h in (own, received))) for i, c in enumerate(chunks))
        up, down = up.reshape(slots, width, part), down.reshape(slots, part, width)
        return (*ffn_forward(low, up, up_bias, down), up, down)

    def body(table_ref, low_ref, bias_ref, *refs):
        up_refs, down_refs, (act_ref, slope_ref, out_ref, up_ref, down_ref) = refs[:3], refs[3:6], refs[6:]
        settle(table_ref, *up_refs, up_ref.at[0])
        settle(table_ref, *down_refs, down_ref.at[0])
        up, down = up_ref[0].reshape(width, part), down_ref[0].reshape(part, width)
        ffn_slot(low_ref, up, bias_ref, down, act_ref, slope_ref, out_ref)

    whole, _, outs = ffn_specs(rows, width, slots, part)
    for c in chunks:
        outs.append((((1,) + c.shape, lambda s, table: (s, 0, 0, 0)), jax.ShapeDtypeStruct((slots,) + c.shape, BF16)))
    act, slope, out, up, down = moved_call(
        body, place_table(), (slots,),
        [whole, ((1, 1, part), lambda s, table: (s, 0, 0))] + raw_specs(chunks[0], 0) + raw_specs(chunks[1], 1),
        outs, (low, up_bias, chunks[0], own, received, chunks[1], own, received), "ffn_first",
        flops=ffn_cost(rows, slots * part, width, 2), transcendentals=rows * slots * part * 2,
    )
    return act, slope, out, up.reshape(slots, width, part), down.reshape(slots, part, width)


def ffn_forward(low, up, up_bias, down):
    rows, width = low.shape
    slots, part = up_bias.shape[0], up_bias.shape[2]

    def body(table_ref, low_ref, up_ref, bias_ref, down_ref, act_ref, slope_ref, out_ref):
        ffn_slot(low_ref, up_ref[0], bias_ref, down_ref[0], act_ref, slope_ref, out_ref)

    whole, _, outs = ffn_specs(rows, width, slots, part)
    slot = lambda s, table: (s, 0, 0)
    return moved_call(
        body, jnp.zeros((1,), jnp.int32), (slots,),
        [whole, ((1, width, part), slot), ((1, 1, part), slot), ((1, part, width), slot)],
        outs, (low, up, up_bias, down), "ffn_forward",
        flops=ffn_cost(rows, slots * part, width, 2), transcendentals=rows * slots * part * 2,
    )


def ffn_backward(g_ffn, low, act, slope, up, down, earlier):
    rows, width = low.shape
    slots, part = up.shape[0], up.shape[2]
    n = lax.axis_size("dp")
    fused = bool(earlier) and aligned(width // n) and aligned(part // n)
    half = n // 2

    def body(table_ref, g_ref, low_ref, act_ref, slope_ref, up_ref, down_ref, *refs):
        olds, refs = refs[: len(earlier)], refs[len(earlier) :]
        mid_ref, bias_ref, outs = refs[0], refs[1], refs[2:]
        g = g_ref[...]
        hid = (dot(g, down_ref[0], 1, 1) * slope_ref[0].astype(F32)).astype(BF16)
        bias_ref[0] = jnp.sum(hid.astype(F32), 0, keepdims=True)
        back = dot(hid, up_ref[0], 1, 1)

        @pl.when(pl.program_id(0) == 0)
        def _():
            mid_ref[...] = back

        @pl.when(pl.program_id(0) > 0)
        def _():
            mid_ref[...] += back

        for i, (left, right) in enumerate(((low_ref[...], hid), (act_ref[0], g))):
            total = dot(left, right, 0, 0)
            if olds:
                total = total + olds[i][0].astype(F32)
            if fused:
                keep_ref, send_ref, scratch = outs[2 * i], outs[2 * i + 1], outs[4 + i]
                scratch[...] = total.astype(BF16).reshape(scratch.shape)
                for p in range(half):
                    keep_ref[p, 0] = scratch[table_ref[p]]
                    send_ref[p, 0] = scratch[table_ref[half + p]]
            else:
                outs[i][0] = total.astype(BF16)

    whole, units, _ = ffn_specs(rows, width, slots, part)
    slot = lambda s, table: (s, 0, 0)
    shapes = [(width, part), (part, width)]
    weights = [((1,) + shape, slot) for shape in shapes]
    outs = [
        (whole, jax.ShapeDtypeStruct((rows, width), F32)),
        (((1, 1, part), slot), jax.ShapeDtypeStruct((slots, 1, part), F32)),
    ]
    scratch = []
    for shape, spec in zip(shapes, weights):
        if fused:
            chunk = (n, shape[0] // n, shape[1])
            outs += packed_outs(slots, *chunk)
            scratch.append(pltpu.VMEM(chunk, BF16))
        else:
            outs.append((spec, jax.ShapeDtypeStruct((slots,) + shape, BF16)))
    got = moved_call(
        body, pack_table(), (slots,),
        [whole, whole, units, units] + weights + (weights if earlier else []),
        outs, (g_ffn, low, act, slope, up, down, *earlier), "ffn_backward", scratch,
        flops=ffn_cost(rows, slots * part, width, 4),
    )
    if fused:
        return got[0], got[1], got[2:4], got[4:6]
    if earlier:
        return got[0], got[1], *(pack(d.reshape(slots, n, -1, d.shape[-1])) for d in got[2:])
    return got


def lane_masks(rows):
    lane = lax.broadcasted_iota(jnp.int32, (rows, LANES), 1)
    return [(lane >= h * HEAD_DIM) & (lane < (h + 1) * HEAD_DIM) for h in range(LANES // HEAD_DIM)]


def only(mask, value):
    return jnp.where(mask, value, jnp.zeros_like(value))


def attention_forward(q, k, v, keys):
    rows, width = q.shape
    padded = k.shape[0]
    scale = 1.0 / math.sqrt(HEAD_DIM)

    def body(q_ref, k_ref, v_ref, out_ref, lse_ref):
        q = q_ref[...] * jnp.asarray(scale, BF16)
        k, v = k_ref[...], v_ref[...]
        live = lax.broadcasted_iota(jnp.int32, (1, padded), 1) < keys
        out = jnp.zeros((rows, LANES), F32)
        lses = jnp.zeros((rows, LANES), F32)
        for mine, theirs in zip(lane_masks(rows), lane_masks(padded)):
            scores = jnp.where(live, dot(only(mine, q), k, 1, 1), -jnp.inf)
            top = jnp.max(scores, -1, keepdims=True)
            weights = jnp.exp(scores - top)
            total = jnp.sum(weights, -1, keepdims=True)
            probs = (weights * (1.0 / total)).astype(BF16)
            out = out + dot(probs, only(theirs, v), 1, 0)
            lses = jnp.where(mine, top + jnp.log(total), lses)
        out_ref[...] = out.astype(BF16)
        lse_ref[...] = lses

    q_spec = pl.BlockSpec((rows, LANES), lambda h: (0, h))
    k_spec = pl.BlockSpec((padded, LANES), lambda h: (0, h))
    return pl.pallas_call(
        body,
        grid=(width // LANES,),
        in_specs=[q_spec, k_spec, k_spec],
        out_specs=[q_spec, q_spec],
        out_shape=[jax.ShapeDtypeStruct((rows, width), BF16), jax.ShapeDtypeStruct((rows, width), F32)],
        cost_estimate=cost(8 * rows * padded * width, rows * padded * width // HEAD_DIM, (q, k, v, q, q), ()),
        name="attention_forward",
    )(q, k, v)


def attention_backward(q, k, v, lse, g_att, keys):
    rows, width = q.shape
    padded = k.shape[0]
    scale = 1.0 / math.sqrt(HEAD_DIM)

    def body(q_ref, k_ref, v_ref, lse_ref, g_ref, gq_ref, gk_ref, gv_ref, sum_q_ref, sum_v_ref):
        q, g = q_ref[...] * jnp.asarray(scale, BF16), g_ref[...]
        k, v = k_ref[...], v_ref[...]
        live = lax.broadcasted_iota(jnp.int32, (1, padded), 1) < keys
        gq = jnp.zeros((rows, LANES), F32)
        gk = jnp.zeros((padded, LANES), F32)
        gv = jnp.zeros((padded, LANES), F32)
        for h, (mine, theirs) in enumerate(zip(lane_masks(rows), lane_masks(padded))):
            q_h, g_h = only(mine, q), only(mine, g)
            scores = dot(q_h, k, 1, 1)
            full = jnp.where(live, jnp.exp(scores - lse_ref[:, h * HEAD_DIM : h * HEAD_DIM + 1]), 0.0)
            g_probs = dot(g_h, v, 1, 1)
            inner = jnp.sum(g_probs * full, -1, keepdims=True)
            g_scores = (full * (g_probs - inner)).astype(BF16)
            gq = gq + dot(g_scores, only(theirs, k), 1, 0)
            gk = gk + dot(g_scores, q_h, 0, 0)
            gv = gv + dot(full.astype(BF16), g_h, 0, 0)
        gq = (gq * scale).astype(BF16)
        gv = gv.astype(BF16)
        gq_ref[...] = gq
        gk_ref[...] = gk.astype(BF16)
        gv_ref[...] = gv
        sum_q_ref[...] = jnp.sum(gq.astype(F32), 0, keepdims=True)
        sum_v_ref[...] = jnp.sum(gv.astype(F32), 0, keepdims=True)

    q_spec = pl.BlockSpec((rows, LANES), lambda h: (0, h))
    k_spec = pl.BlockSpec((padded, LANES), lambda h: (0, h))
    sum_spec = pl.BlockSpec((1, LANES), lambda h: (0, h))
    return pl.pallas_call(
        body,
        grid=(width // LANES,),
        in_specs=[q_spec, k_spec, k_spec, q_spec, q_spec],
        out_specs=[q_spec, k_spec, k_spec, sum_spec, sum_spec],
        out_shape=[
            jax.ShapeDtypeStruct((rows, width), BF16),
            jax.ShapeDtypeStruct((padded, width), BF16),
            jax.ShapeDtypeStruct((padded, width), BF16),
            jax.ShapeDtypeStruct((1, width), F32),
            jax.ShapeDtypeStruct((1, width), F32),
        ],
        cost_estimate=cost(20 * rows * padded * width, rows * padded * width // HEAD_DIM, (q, k, v, lse, g_att, q, k, v), ()),
        name="attention_backward",
    )(q, k, v, lse, g_att)


def attention_weights(segments, slots):
    width = segments[0][0].shape[1]
    part = width // slots
    n = lax.axis_size("dp")
    rows = 4 * part // n
    half = n // 2
    fused = aligned(rows)
    swap = other_half_slots()
    operands = [a for segment in segments for a in segment]

    def body(table_ref, *refs):
        out_refs = refs[len(operands) :]
        full = out_refs[-1]
        groups = [refs[i : i + 6] for i in range(0, len(operands), 6)]
        for kind in range(4):
            total = None
            for refs_of in groups:
                left = refs_of[4] if kind == 3 else refs_of[kind]
                right = refs_of[5][...] if kind == 3 else refs_of[3][: left.shape[0], :]
                one = dot(left[...], right, 0, 0)
                total = one if total is None else total + one
            for s in range(slots):
                full[s, kind * part : (kind + 1) * part, :] = total[s * part : (s + 1) * part].astype(BF16)
        if fused:
            for p in range(half):
                mine = pl.ds(pl.multiple_of(table_ref[p] * rows, 16), rows)
                theirs = pl.ds(pl.multiple_of(table_ref[half + p] * rows, 16), rows)
                for s in range(slots):
                    out_refs[0][p, s] = full[s, mine, :]
                    out_refs[1][p, s] = full[swap[s], theirs, :]

    everything = lambda a: (a.shape, lambda i, table: (0,) * len(a.shape))
    packed = jax.ShapeDtypeStruct((half, slots, rows, width), BF16)
    whole = jax.ShapeDtypeStruct((slots, 4 * part, width), BF16)
    shapes = [packed, packed] if fused else [whole]
    got = moved_call(
        body, arrival_sources(), (1,), [everything(a) for a in operands], [(everything(a), a) for a in shapes], operands,
        "attention_weights", [pltpu.VMEM(whole.shape, BF16)] if fused else [],
        flops=sum(2 * a.size * width for a in operands) * 2 // 3,
    )
    return got if fused else pack(got[0].reshape(slots, n, rows, width))


def join_rows(tops, seg):
    width = tops[0].shape[1]

    def body(table_ref, *refs):
        for i, top_ref in enumerate(refs[:-1]):
            refs[-1][i * seg : (i + 1) * seg] = top_ref[:seg, :].reshape(seg, 1, width)

    shape = jax.ShapeDtypeStruct((len(tops) * seg, 1, width), F32)
    whole = lambda a: (a.shape, lambda i, table: (0,) * len(a.shape))
    return moved_call(
        body, jnp.zeros((1,), jnp.int32), (1,), [whole(a) for a in tops], [(whole(shape), shape)], tops, "join_rows"
    )[0]


def local(text_in, start_memory, w_qkv, b_qv, w_o, w_up, b_up, w_down, norm_gains, biases, cot_text, cot_memory):
    text, cot_rows, cot_mem = text_in[0], cot_text[0], cot_memory[0]
    text_total, width = text.shape
    mem = start_memory.shape[0]
    seg = text_total // SEGMENTS
    rows = seg + mem
    keys = rows + mem
    padded = -(-keys // LANES) * LANES
    n_t, n_dp = lax.axis_size("tensor"), lax.axis_size("dp")
    head_part = w_qkv.shape[2]
    part = b_up.shape[0]
    t = lax.axis_index("tensor")

    small = jnp.concatenate([b_qv.reshape(-1), b_up])
    small = jnp.pad(small, (0, 8 * width - small.shape[0])).reshape(1, 8, width)
    d = lax.axis_index("dp")
    own_chunk = lambda chunks: lax.dynamic_index_in_dim(chunks, d, 0)
    kinds = jnp.concatenate([w_qkv.transpose(0, 2, 1).reshape(-1, width), w_o]).reshape(n_dp, -1, width)
    chunks = [w_up.reshape(n_dp, -1, part), w_down.reshape(n_dp, -1, width)]
    lined = jnp.concatenate([own_chunk(kinds), small], 1)
    ffn_own = jnp.concatenate([own_chunk(c) for c in chunks], 1)
    grow = lambda exchange, step: lambda value: jnp.concatenate([value, exchange(value, step)])
    grow_line = [grow(line_exchange, step) for step in line_steps()]
    lined = chain(grow_line)(lined)
    rest, ffn_rest = lockstep(
        [lined[None, 1:, : kinds.shape[1]], ffn_own], [[grow(outer_exchange, step) for step in outer_steps()], grow_line]
    )
    small = lined[:, kinds.shape[1] :].reshape(n_t, -1).astype(F32)
    q_bias = small[:, :head_part].reshape(1, -1)
    v_bias = small[:, head_part : 2 * head_part].reshape(1, -1)
    up_bias = small[:, None, 2 * head_part : 2 * head_part + part]
    received = core_exchange(rest)
    ffn_rest = ffn_rest[None, 1:]
    first, *middle, last = outer_steps()
    (q_w, k_w, v_w, o_w), ffn_received = lax.optimization_barrier(
        (place_kinds(kinds, rest, received), outer_exchange(ffn_rest, first))
    )
    ffn_rest = gather_outer(jnp.concatenate([ffn_rest, ffn_received]), middle)

    read = start_memory
    kept, pieces = [], []
    for s in range(SEGMENTS):
        x = jnp.concatenate([text[s * seg : (s + 1) * seg], start_memory, read, jnp.zeros((padded - keys, width), BF16)])
        q = (dot(x[:rows], q_w, 1, 1) + q_bias).astype(BF16)
        k = dot(x, k_w, 1, 1).astype(BF16)
        v = (dot(x, v_w, 1, 1) + v_bias).astype(BF16)
        att, lse = attention_forward(q, k, v, keys)
        if s == 0:
            att, ffn_received = lax.optimization_barrier((att, outer_exchange(ffn_rest, last)))
            ffn_rest = jnp.concatenate([ffn_rest, ffn_received])
        n1, r1 = norm_stats(x[:rows].astype(F32) + dot(att, o_w, 1, 0) + biases[0])
        middle = n1 * norm_gains[0] + biases[1]
        low = middle.astype(BF16)
        if s == 0:
            act, slope, ffn, up_full, down_full = ffn_first(low, up_bias, chunks, ffn_rest, core_exchange(ffn_rest))
        else:
            act, slope, ffn = ffn_forward(low, up_full, up_bias, down_full)
        n2, r2 = norm_stats(middle + ffn + biases[2])
        result = (n2 * norm_gains[1] + biases[3]).astype(BF16)
        pieces.append(result[:seg])
        read = result[seg:]
        kept.append((x, q, k, v, lse, att, n1, r1, low, act, slope, n2, r2))

    segments, sums, ends = [], [], []
    carry = cot_mem.astype(F32)
    d_text = [None] * SEGMENTS
    outers, lines = reduce_steps()
    earlier = ()
    for s in reversed(range(SEGMENTS)):
        x, q, k, v, lse, att, n1, r1, low, act, slope, n2, r2 = kept[s]
        g_res = jnp.concatenate([cot_rows[s * seg : (s + 1) * seg].astype(F32), carry])
        g_pre2 = norm_backward(g_res, n2, r2, norm_gains[1])
        g_ffn = g_pre2.astype(BF16)
        g_mid, g_bup, *got = ffn_backward(g_ffn, low, act, slope, up_full, down_full, earlier)
        if s == 0:
            d_up, d_down = got
        else:
            earlier = tuple(got)
        g_mid = g_mid + g_pre2
        g_pre1 = norm_backward(g_mid, n1, r1, norm_gains[0])
        g_attn = g_pre1.astype(BF16)
        g_att = dot(g_attn, o_w, 1, 1).astype(BF16)
        if s == 0:
            g_att, total_up = lax.optimization_barrier((g_att, core_step(d_up)))
            total_up, total_down = outers[0](total_up), core_step(d_down)
        g_q, g_k, g_v, sum_q, sum_v = attention_backward(q, k, v, lse, g_att, keys)
        if s == 0:
            (g_q, g_k, g_v), total_up, total_down = lax.optimization_barrier(((g_q, g_k, g_v), total_up, total_down))
            total_up, total_down = chain(outers[1:])(total_up), outers[0](total_down)
        segments.append((g_q, g_k, g_v, x, att, g_attn))
        g_x = dot(g_k, k_w, 1, 0) + dot(g_v, v_w, 1, 0)
        top = g_x[:rows] + dot(g_q, q_w, 1, 0) + g_pre1
        d_text[s] = top
        carry = g_x[rows:keys]
        ends += [top[seg:]] if s > 0 else [top[seg:], carry]
        over = lambda value: jnp.sum(value, 0, keepdims=True)
        sums.append(
            [over(g_mid * n1), over(g_res * n2), over(g_pre1), over(g_mid), over(g_pre2), over(g_res)]
            + [sum_q, sum_v, g_bup[:, 0]]
        )

    packed = attention_weights(segments, n_t)
    packed, total_up, total_down = lax.optimization_barrier((packed, total_up, total_down))
    total, total_down = lockstep([packed, total_down], [[core_step], [chain(outers[1:])]])
    total, sums, ends = lax.optimization_barrier((total, sums, ends))
    sums = [a + b for a, b in zip(*sums)]
    pick = (jnp.arange(n_t)[:, None] == t ^ slot_masks()[0]).astype(F32)
    by_slot = jnp.concatenate([sums[6].reshape(n_t, -1), sums[7].reshape(n_t, -1), sums[8]], 1)
    by_index = jnp.dot(pick, by_slot, precision=lax.Precision.HIGHEST)
    d_mem = sum(ends[1:], ends[0])
    vectors = jnp.concatenate(
        sums[:6] + [d_mem]
        + [by_index[:, i * head_part : (i + 1) * head_part].reshape(1, width) for i in (0, 1)]
        + [by_index[:, 2 * head_part :].reshape(-1, width)]
    )
    spread = [grow(outer_exchange, step) for step in outer_steps()]
    smalls = small_steps()
    ffn = jnp.concatenate([total_up, total_down], 2)
    merge = lambda value: value.reshape(1, -1, width)
    main = outers + lines
    inside = len(main) - 1
    total, ffn, vectors, text_grad = lockstep(
        [total, ffn, vectors, d_text],
        [main, lines + [chain([merge] + spread[:1])] + spread[1:], [None] + smalls[:inside], [None, None, lambda tops: join_rows(tops, seg)]],
    )
    first, *rest = smalls[inside:]
    total, ffn_received, vectors = lax.optimization_barrier(
        (spread[0](merge(total)), core_exchange(ffn), first(vectors))
    )
    g_up, g_down = (a.reshape(-1, width) for a in finish(ffn, ffn_received, 2))
    total, g_up, g_down, vectors = lax.optimization_barrier(
        (chain(spread[1:])(total), g_up, g_down, chain(rest)(vectors))
    )
    g_bqv = lax.dynamic_slice_in_dim(vectors[6 + mem : 8 + mem], t * head_part, head_part, 1)
    g_bup = lax.dynamic_slice_in_dim(vectors[8 + mem :].reshape(n_t, -1), t, 1, 0)[0]
    g_qkv, g_out = finish_kinds(total, core_exchange(total), head_part)
    g_qkv = g_qkv.transpose(0, 2, 1)

    return (
        jnp.concatenate(pieces)[None],
        read[None],
        text_grad.transpose(1, 0, 2),
        vectors[6 : 6 + mem],
        g_qkv,
        g_bqv,
        g_out,
        g_up,
        g_bup,
        g_down,
        vectors[:2],
        vectors[2:6],
    )


def solution(mesh):
    own = P(("dp", "tensor"), None, None)
    return jax.shard_map(
        local,
        mesh=mesh,
        in_specs=(
            own, P(), P(None, None, "tensor"), P(None, "tensor"), P("tensor", None), P(None, "tensor"),
            P("tensor"), P("tensor", None), P(), P(), own, own,
        ),
        out_specs=(
            own, own, own, P(), P(None, None, "tensor"), P(None, "tensor"), P("tensor", None),
            P(None, "tensor"), P("tensor"), P("tensor", None), P(), P(),
        ),
        check_vma=False,
    )
```
